32 devices in a mesh: grp: 2 (over x), lon: 16 (over z, y, core).
Axes of the slice: x: 2, y: 2, z: 4, core: 2. Of those that a mesh axis runs over, the one named last changes fastest.
Arguments:
- tracer_pert: float32 [4, 50, 32, 1024], P('grp', None, 'lon'), parts along dimension 0, may hold values from -60 to 60
- surface_pert: float32 [4, 32, 1024], P('grp', 'lon'), parts along dimension 0, may hold values from -60 to 60
- zonal_flow: float32 [50, 32, 1024], P(None, 'lon'), may hold values from -3.2 to 3.2
- merid_flow: float32 [50, 32, 1024], P(None, 'lon'), may hold values from -3.2 to 3.2
- bottom_level: int32 [32, 1024], P('lon'), may hold values from 0 to 50
Outputs:
- tracer_vec: float32 [4, 50, 32, 1024], P('grp', None, 'lon'), parts along dimension 0
- surface_vec: float32 [4, 32, 1024], P('grp', 'lon'), parts along dimension 0
- growth: float32 [6], P('grp'), parts along dimension 0
The draws below stay inside these ranges and needn't reach their ends.
There are 2 independent parts, one for each index of `grp`. The reference program is written for one: setup_inputs(seed, part) draws one part's arguments, and reference() takes and returns one part's arrays. A program takes and returns all parts, laid end to end along the dimension named above; an argument that names none is the same for every part. Nothing has to cross between parts.
Inputs may be any that keep to these rules, and one draw needn't show every extreme that they name: `bottom_level`: 0 marks a land column, 50 a column wet to the bottom level.
All inputs are finite; a program needn't handle non-finite values.
Results may differ from the reference program's by a relative error of at most 0.0001.
Values sent between devices are 32-bit elements; how exact they have to be, the bound alone decides.
A program may use at most 64 MiB of HBM per device.

```python
import jax
import jax.numpy as jnp
from jax import lax

NV = 2
NZ = 50
NY = 1024
NSUB = 2
ITERS = 3
NX = 32


def shaped_field(key, shape):
    key_base, key_rough, key_rows = jax.random.split(key, 3)
    base = jnp.clip(jax.random.normal(key_base, shape, jnp.float32), -4.0, 4.0)
    mixed = jnp.concatenate([base[:1], 0.6 * base[:1] + 0.8 * base[1:]], axis=0)
    envelope = 0.5 + 1.5 * jnp.arange(NX, dtype=jnp.float32) / NX
    rough = jnp.exp(jax.random.uniform(key_rough, shape, jnp.float32, -0.5, 0.5))
    row_scale = jnp.exp(jax.random.uniform(key_rows, (NY,), jnp.float32, -1.15, 1.15))
    return mixed * envelope[:, None] * rough * row_scale


def draw_tracer_pert(key, part):
    return shaped_field(jax.random.fold_in(key, 11), (NV, NZ, NX, NY))


def draw_surface_pert(key, part):
    return shaped_field(jax.random.fold_in(key, 23), (NV, NX, NY))


def touch_ends(drawn, key, least, largest):
    longest = drawn.shape.index(max(drawn.shape))
    spots = []
    for shift in (0, 1):
        where = [jax.random.randint(jax.random.fold_in(key, axis), (), 0, length) for axis, length in enumerate(drawn.shape)]
        where[longest] = (where[longest] + shift) % drawn.shape[longest]
        spots.append(tuple(where))
    return drawn.at[spots[0]].set(least).at[spots[1]].set(largest)


def level_of(rng, dims, shards, low, high):
    factor_of = 1.0
    for position, shards_of in shards:
        steps = jax.random.uniform(jax.random.fold_in(jax.random.fold_in(rng, 6), position), (shards_of,), jnp.float32, low / len(shards), high / len(shards))
        factor_of = factor_of * jnp.repeat(jnp.exp(steps), dims[position] // shards_of).reshape((-1,) + (1,) * (len(dims) - 1 - position))
    return factor_of


def scatter_about(own_key, shape, deviation, bound, cuts=(), held_as=jnp.bfloat16):
    array = deviation * jax.random.normal(own_key, shape, jnp.float32)
    if cuts:
        array = array * level_of(own_key, shape, cuts, -0.22, 0.18)
    return jnp.clip(array, -bound, bound).astype(held_as)


def setup_inputs(seed: int = 0, part: int = 0) -> dict:
    seeds = jax.random.split(jax.random.key(seed), 6)
    part_splits = jax.random.split(jax.random.fold_in(seeds[5], part), 6)
    return {
        "tracer_pert": draw_tracer_pert(jax.random.fold_in(jax.random.fold_in(seeds[5], part), 71), part),
        "surface_pert": draw_surface_pert(jax.random.fold_in(jax.random.fold_in(seeds[5], part), 71), part),
        "zonal_flow": scatter_about(seeds[2], (NZ, NX, NY), 0.8, 3.2, ((1, 16),), jnp.float32),
        "merid_flow": scatter_about(seeds[3], (NZ, NX, NY), 0.8, 3.2, ((1, 16),), jnp.float32),
        "bottom_level": touch_ends(jax.random.randint(seeds[4], (NX, NY), 0, NZ + 1), jax.random.fold_in(seeds[4], 1), 0, NZ).astype(jnp.int32),
    }


DIFFUSIVITY = 0.5
TIME_STEP = 0.2
SURFACE_COUPLING = 0.5
STERIC_GAIN = 2.0
EPSILON = 1e-06

def tracer_update(tracer, zonal_flow, merid_flow, wet_cells):
    east_vals = jnp.roll(tracer, -1, axis=2)
    face_x = wet_cells * jnp.roll(wet_cells, -1, axis=1)
    flow_x = 0.5 * (zonal_flow + jnp.roll(zonal_flow, -1, axis=1))
    flux_x = face_x * (0.5 * flow_x * (tracer + east_vals) - DIFFUSIVITY * (east_vals - tracer))
    div_x = flux_x - jnp.roll(flux_x, 1, axis=2)
    face_y = wet_cells[..., :-1] * wet_cells[..., 1:]
    flow_y = 0.5 * (merid_flow[..., :-1] + merid_flow[..., 1:])
    flux_y = face_y * (0.5 * flow_y * (tracer[..., :-1] + tracer[..., 1:]) - DIFFUSIVITY * (tracer[..., 1:] - tracer[..., :-1]))
    padded = jnp.pad(flux_y, ((0, 0), (0, 0), (0, 0), (1, 1)))
    div_y = padded[..., 1:] - padded[..., :-1]
    return tracer - TIME_STEP * (div_x + div_y)

def surface_operator(surface, face_x, face_y):
    grad_x = face_x * (jnp.roll(surface, -1, axis=1) - surface)
    lap_x = grad_x - jnp.roll(grad_x, 1, axis=1)
    grad_y = face_y * (surface[..., 1:] - surface[..., :-1])
    padded = jnp.pad(grad_y, ((0, 0), (0, 0), (1, 1)))
    lap_y = padded[..., 1:] - padded[..., :-1]
    return surface - SURFACE_COUPLING * (lap_x + lap_y)

def reference(tracer_pert, surface_pert, zonal_flow, merid_flow, bottom_level):
    levels = jnp.arange(NZ, dtype=jnp.int32)[:, None, None]
    wet_cells = (levels < bottom_level[None]).astype(jnp.float32)
    depths = bottom_level.astype(jnp.float32)
    tracer = wet_cells[None] * tracer_pert
    for substep in range(NSUB):
        tracer = tracer_update(tracer, zonal_flow, merid_flow, wet_cells)
    height = surface_pert * (depths > 0).astype(jnp.float32)[None]
    forcing = height + STERIC_GAIN * lax.optimization_barrier(jnp.sum(tracer, axis=1)) / NZ
    face_x = jnp.minimum(depths, jnp.roll(depths, -1, axis=0))
    face_y = jnp.minimum(depths[:, :-1], depths[:, 1:])
    solution = height
    residual = forcing - surface_operator(height, face_x, face_y)
    direction = residual
    norm_now = lax.optimization_barrier(jnp.sum(residual * residual, axis=(1, 2)))
    for iteration in range(ITERS):
        image_vec = surface_operator(direction, face_x, face_y)
        step_size = norm_now / lax.optimization_barrier(jnp.sum(direction * image_vec, axis=(1, 2)))
        solution = solution + step_size[:, None, None] * direction
        residual = residual - step_size[:, None, None] * image_vec
        if iteration + 1 < ITERS:
            norm_next = lax.optimization_barrier(jnp.sum(residual * residual, axis=(1, 2)))
            direction = residual + (norm_next / norm_now)[:, None, None] * direction
            norm_now = norm_next
    cell_count = (NZ + 1) * NX * NY

    def inner_product(tracer_a, surface_a, tracer_b, surface_b):
        return (jnp.sum(tracer_a * tracer_b) + jnp.sum(surface_a * surface_b)) / cell_count
    first_tracer, second_tracer = (tracer[0], tracer[1])
    first_surface, second_surface = (solution[0], solution[1])
    scale_one = jnp.sqrt(inner_product(first_tracer, first_surface, first_tracer, first_surface) + EPSILON)
    unit_tracer = first_tracer / scale_one
    unit_surface = first_surface / scale_one
    cross = inner_product(second_tracer, second_surface, unit_tracer, unit_surface)
    rest_tracer = second_tracer - cross * unit_tracer
    rest_surface = second_surface - cross * unit_surface
    scale_two = jnp.sqrt(inner_product(rest_tracer, rest_surface, rest_tracer, rest_surface) + EPSILON)
    tracer_vec = jnp.stack([unit_tracer, rest_tracer / scale_two])
    surface_vec = jnp.stack([unit_surface, rest_surface / scale_two])
    growth = jnp.stack([scale_one, cross, scale_two])
    return (tracer_vec, surface_vec, growth)
```

```python
import functools

import jax
import jax.numpy as jnp
from jax import lax
from jax.experimental import pallas as pl
from jax.experimental.pallas import tpu as pltpu
from jax.sharding import PartitionSpec as P

DIFFUSIVITY = 0.5
TIME_STEP = 0.2
SURFACE_COUPLING = 0.5
STERIC_GAIN = 2.0
EPSILON = 1e-06
MESH = pl.DeviceIdType.MESH
CHUNKS = 5
UNROLL = 5
SHIFTS = (1, -1, 2, -2)
SLOTS = 5
OWN = 2
CENTRES = (0.0, 0.04, 0.16, 0.64)
TILE = (8, 128)


def chunk_bounds(levels):
    count = min(CHUNKS, levels)
    edges = [levels * i // count for i in range(count + 1)]
    return list(zip(edges[:-1], edges[1:]))


def spread_rounds(n):
    reach, rounds = 2, []
    while 2 * reach < n:
        rounds.append(reach)
        reach *= 2
    return rounds


def shares_zonal(groups, levels):
    return groups == 2 and all((b - a) % 2 == 0 for a, b in chunk_bounds(levels))


def peers_loop(n, body):
    if n <= 16:
        for i in range(1, n):
            body(i)
    else:

        def step(i, carry):
            body(i)
            return carry

        lax.fori_loop(1, n, step, 0)


def kernel(
    n, share, trc_h, surf_h, zon_h, mer_h, bot_h, out, sout, gout,
    trc, surf, zon, mer, bot, s_t, r_t, s_z, r_z, s_b, r_b, coef, st, rx, red,
    in_sem, t_send, t_recv, z_send, z_recv, b_send, b_recv,
    st_send, st_recv, rx_send, rx_recv, rd_send, rd_recv, met,
):
    me = lax.axis_index("lon")
    grp = lax.axis_index("grp")
    levels = zon.shape[0]
    chunks = chunk_bounds(levels)
    side_dev = (lax.rem(me + n - 1, n), lax.rem(me + 1, n))
    outer = lax.rem(me, 2)
    inner = 1 - outer
    lane = lax.broadcasted_iota(jnp.int32, TILE, 1)
    row = lax.broadcasted_iota(jnp.int32, TILE, 0)
    last_lane, first_lane = lane == 127, lane == 0

    def north(x):
        rolled = pltpu.roll(x, 127, 1)
        return jnp.where(last_lane, pltpu.roll(rolled, 7, 0), rolled)

    def south(x):
        rolled = pltpu.roll(x, 1, 1)
        return jnp.where(first_lane, pltpu.roll(rolled, 1, 0), rolled)

    def col(c):
        return pl.ds(c, 8, stride=2)

    def lon_peer(s):
        return {"lon": lax.rem(me + s + n, n)}

    barrier = pltpu.get_barrier_semaphore()
    for s in SHIFTS:
        pl.semaphore_signal(barrier, inc=1, device_id=lon_peer(s), device_id_type=MESH)
    if share:
        pl.semaphore_signal(barrier, inc=1, device_id={"grp": 1 - grp}, device_id_type=MESH)

    def load(which, g):
        k0, k1 = chunks[g]
        ks = pl.ds(k0, k1 - k0)
        src, dst = (
            (zon_h.at[ks], zon.at[ks]),
            (trc_h.at[:, ks], trc.at[:, ks]),
            (mer_h.at[ks], mer.at[ks]),
        )[which]
        return pltpu.make_async_copy(src, dst, in_sem.at[which, g])

    count = len(chunks)
    load_bot = pltpu.make_async_copy(bot_h, bot, in_sem.at[3, 0])
    load_surf = pltpu.make_async_copy(surf_h, surf, in_sem.at[4, 0])
    load_bot.start()
    load_surf.start()
    for g in range(count):
        load(0, g).start()
        load(1, g).start()
    for g in range(count):
        load(2, g).start()
    load_bot.wait()
    load_surf.wait()
    for c in range(2):
        d = bot[col(c), :].astype(jnp.float32)
        st[OWN, 2 + c] = d
        for v in range(2):
            st[OWN, (4, 0)[c] + v] = jnp.where(d > 0, surf[v, col(c), :], 0.0)

    def gather_chunk(g):
        load(0, g).wait()
        load(1, g).wait()

        def step(k, carry):
            for c in range(2):
                s_t[c, k, 0] = trc[0, k, col(c), :]
                s_t[c, k, 1] = trc[1, k, col(c), :]
                s_z[c, k] = zon[k, col(c), :]
            return carry

        lax.fori_loop(*chunks[g], step, 0, unroll=UNROLL)

    def side_copy(src, dst, send, recv, g, side):
        k0, k1 = chunks[g]
        return pltpu.make_async_remote_copy(
            src_ref=src.at[side, pl.ds(k0, k1 - k0)],
            dst_ref=dst.at[1 - side, pl.ds(k0, k1 - k0)],
            send_sem=send.at[side, g],
            recv_sem=recv.at[1 - side, g],
            device_id={"lon": side_dev[side]},
            device_id_type=MESH,
        )

    def t_copy(g, side):
        return side_copy(s_t, r_t, t_send, t_recv, g, side)

    def b_copy(g, side):
        return side_copy(s_b, r_b, b_send, b_recv, g, side)

    def z_copies(g):
        if not share:
            return [side_copy(s_z, r_z, z_send, z_recv, g, side) for side in range(2)]
        k0, k1 = chunks[g]
        half = (k1 - k0) // 2
        mine = pl.ds(k0 + grp * half, half)
        across = pltpu.make_async_remote_copy(
            src_ref=s_z.at[outer, mine],
            dst_ref=r_z.at[1 - outer, mine],
            send_sem=z_send.at[0, g],
            recv_sem=z_recv.at[0, g],
            device_id=lon_peer(2 * outer - 1),
            device_id_type=MESH,
        )
        within = pltpu.make_async_remote_copy(
            src_ref=s_z.at[inner, pl.ds(k0, k1 - k0)],
            dst_ref=r_z.at[1 - inner, pl.ds(k0, k1 - k0)],
            send_sem=z_send.at[1, g],
            recv_sem=z_recv.at[1, g],
            device_id=lon_peer(2 * inner - 1),
            device_id_type=MESH,
        )
        onward = pltpu.make_async_remote_copy(
            src_ref=r_z.at[outer, mine],
            dst_ref=r_z.at[outer, mine],
            send_sem=z_send.at[2, g],
            recv_sem=z_recv.at[2, g],
            device_id={"grp": 1 - grp},
            device_id_type=MESH,
        )
        return [across, within, onward]

    def send_chunk(g):
        for copy in z_copies(g)[:2]:
            copy.start()
        for side in range(2):
            t_copy(g, side).start()

    def shift_copy(buf, send, recv, s, part):
        return pltpu.make_async_remote_copy(
            src_ref=buf.at[OWN, part],
            dst_ref=buf.at[OWN - s, part],
            send_sem=send.at[OWN - s],
            recv_sem=recv.at[OWN - s],
            device_id=lon_peer(s),
            device_id_type=MESH,
        )

    def st_copy(s):
        part = {1: pl.ds(0, 4), -1: pl.ds(2, 4), 2: pl.ds(3, 1), -2: pl.ds(2, 1)}[s]
        return shift_copy(st, st_send, st_recv, s, part)

    def rx_copy(s):
        part = {1: pl.ds(0, 4), -1: pl.ds(0, 4), 2: pl.ds(2, 2), -2: pl.ds(0, 2)}[s]
        return shift_copy(rx, rx_send, rx_recv, s, part)

    gather_chunk(0)
    pl.semaphore_wait(barrier, len(SHIFTS) + (1 if share else 0))
    for s in SHIFTS:
        st_copy(s).start()
    send_chunk(0)
    rounds = spread_rounds(n)

    def spread(i):
        if i < len(rounds):
            for s in (rounds[i], -rounds[i]):
                pl.semaphore_signal(
                    met.at[i], inc=1, device_id=lon_peer(s), device_id_type=MESH
                )

    def spread_wait(i):
        if i < len(rounds):
            pl.semaphore_wait(met.at[i], 2)

    spread(0)
    for g in range(1, count):
        gather_chunk(g)
        send_chunk(g)

    for s in SHIFTS:
        st_copy(s).wait_recv()

    depths = {-3: st[0, 3], -2: st[1, 2], -1: st[1, 3], 0: st[2, 2], 1: st[2, 3]}
    depths.update({2: st[3, 2], 3: st[3, 3], 4: st[4, 2]})

    def y_face(i):
        wall = jnp.logical_and(last_lane, row == 7)
        return jnp.where(wall, 0.0, jnp.minimum(depths[i], north(depths[i])))

    def x_face(i):
        return jnp.minimum(depths[i], depths[i + 1])

    half = TIME_STEP * 0.25
    diff = TIME_STEP * DIFFUSIVITY
    faces_x = [x_face(f - 1) for f in range(3)]
    faces_y = [y_face(c) for c in range(2)]
    own_depth = [depths[c] for c in range(2)]

    for g, (k0, k1) in enumerate(chunks):
        arrivals = z_copies(g)
        for copy in arrivals[:2]:
            copy.wait_recv()
        if share:
            arrivals[2].start()
        load(2, g).wait()
        for side in range(2):
            t_copy(g, side).wait_recv()
        if share:
            arrivals[2].wait_recv()

        def first(k, carry):
            kf = k.astype(jnp.float32)
            z = (r_z[0, k], s_z[0, k], s_z[1, k], r_z[1, k])
            cx = []
            for f in range(3):
                open_f = kf < faces_x[f]
                u = half * (z[f] + z[f + 1])
                cx.append((jnp.where(open_f, u + diff, 0.0), jnp.where(open_f, u - diff, 0.0)))
            cy = []
            for c in range(2):
                open_f = kf < faces_y[c]
                m = mer[k, col(c), :]
                u = half * (m + north(m))
                cy.append((jnp.where(open_f, u + diff, 0.0), jnp.where(open_f, u - diff, 0.0)))
            for q, (lo, hi) in enumerate(cx + cy):
                coef[k, 2 * q] = lo
                coef[k, 2 * q + 1] = hi
            wet = [kf < own_depth[c] for c in range(2)]
            for v in range(2):
                t = (
                    r_t[0, k, v],
                    jnp.where(wet[0], s_t[0, k, v], 0.0),
                    jnp.where(wet[1], s_t[1, k, v], 0.0),
                    r_t[1, k, v],
                )
                fx = [cx[f][0] * t[f] + cx[f][1] * t[f + 1] for f in range(3)]
                for c in range(2):
                    fy = cy[c][0] * t[c + 1] + cy[c][1] * north(t[c + 1])
                    s_b[c, k, v] = t[c + 1] - ((fx[c + 1] - fx[c]) + (fy - south(fy)))
            return carry

        lax.fori_loop(k0, k1, first, 0, unroll=UNROLL)
        for side in range(2):
            b_copy(g, side).start()
        spread_wait(g)
        spread(g + 1)
    for i in range(count, len(rounds)):
        spread_wait(i)
        spread(i + 1)

    face_x = {i: SURFACE_COUPLING * x_face(i) for i in range(-3, 4)}
    face_y = {i: SURFACE_COUPLING * y_face(i) for i in range(-2, 4)}

    def lap(s, cols):
        gx = {i: face_x[i] * (s[i + 1] - s[i]) for i in range(cols[0] - 1, cols[-1] + 1)}
        res = {}
        for i in cols:
            gy = face_y[i] * (north(s[i]) - s[i])
            res[i] = -((gx[i] - gx[i - 1]) + (gy - south(gy)))
        return res

    own = (0, 1)
    height = [{-1: st[1, v], 0: st[2, 4 + v], 1: st[2, v], 2: st[3, 4 + v]} for v in range(2)]
    lap_h = [lap(height[v], own) for v in range(2)]

    zero = jnp.zeros(TILE, jnp.float32)
    totals = (zero,) * 7
    for g, (k0, k1) in enumerate(chunks):
        for side in range(2):
            b_copy(g, side).wait_recv()

        def second(k, carry):
            sums, grams = list(carry[:4]), list(carry[4:])
            cx = [(coef[k, 2 * f], coef[k, 2 * f + 1]) for f in range(3)]
            cy = [(coef[k, 6 + 2 * c], coef[k, 7 + 2 * c]) for c in range(2)]
            new = []
            for v in range(2):
                t = (r_b[0, k, v], s_b[0, k, v], s_b[1, k, v], r_b[1, k, v])
                fx = [cx[f][0] * t[f] + cx[f][1] * t[f + 1] for f in range(3)]
                for c in range(2):
                    fy = cy[c][0] * t[c + 1] + cy[c][1] * north(t[c + 1])
                    val = t[c + 1] - ((fx[c + 1] - fx[c]) + (fy - south(fy)))
                    out[v, k, col(c), :] = val
                    sums[2 * v + c] = sums[2 * v + c] + val
                    new.append(val)
            grams[0] = grams[0] + (new[0] * new[0] + new[1] * new[1])
            grams[1] = grams[1] + (new[0] * new[2] + new[1] * new[3])
            grams[2] = grams[2] + (new[2] * new[2] + new[3] * new[3])
            return tuple(sums + grams)

        totals = lax.fori_loop(k0, k1, second, totals, unroll=UNROLL)

    gain = STERIC_GAIN / levels
    for v in range(2):
        for c in range(2):
            rx[OWN, 2 * c + v] = gain * totals[2 * v + c] - lap_h[v][c]
    for s in SHIFTS:
        rx_copy(s).start()

    def dot(a, b):
        return a[0] * b[0] + a[1] * b[1]

    parts = {}
    for q in range(3):
        parts["gram", q] = totals[4 + q]
    parts["hh", 0] = dot(height[0], height[0])
    parts["hh", 1] = dot(height[1], height[1])
    parts["hh", 2] = dot(height[0], height[1])
    for s in SHIFTS:
        rx_copy(s).wait_recv()

    span = 4.0 * levels
    powers = []
    for v in range(2):
        r = {-3: rx[0, 2 + v], 4: rx[4, v]}
        for c in range(2):
            r.update({c - 2: rx[1, 2 * c + v], c: rx[2, 2 * c + v], c + 2: rx[3, 2 * c + v]})
        l1 = lap(r, range(-2, 4))
        l2 = lap(l1, range(-1, 3))
        l3 = lap(l2, own)
        powers.append((r, l1, l2, l3))
    for v in range(2):
        for i, centre in enumerate(CENTRES):
            b = [{c: p[c] for c in own} for p in powers[v]]
            base = [b[0]]
            for j in range(3):
                if centre:
                    b = [
                        {c: b[q + 1][c] - (centre * span) * b[q][c] for c in own}
                        for q in range(3 - j)
                    ]
                else:
                    b = b[1:]
                base.append(b[0])
            for k in range(1 if i else 0, 6):
                parts["m", v, i, k] = dot(base[k // 2], base[(k + 1) // 2])
        for j in range(3):
            parts["h", v, v, j] = dot(height[v], powers[v][j])
            parts["h", v, 1 - v, j] = dot(height[v], powers[1 - v][j])
    for k in range(5):
        parts["c", k] = dot(powers[0][k // 2], powers[1][(k + 1) // 2])

    names = list(parts)
    level, shift = [parts[name] for name in names], 1
    while shift < 128:
        if len(level) == 1:
            level = [level[0] + pltpu.roll(level[0], shift, 1)]
        else:
            even = jnp.bitwise_and(lane, shift) == 0
            merged = []
            for i in range(0, len(level), 2):
                a, b = level[i], level[min(i + 1, len(level) - 1)]
                merged.append(jnp.where(even, a, b) + pltpu.roll(jnp.where(even, b, a), shift, 1))
            level = merged
        shift *= 2
    mine = level[0]
    for shift in (4, 2, 1):
        mine = mine + pltpu.roll(mine, shift, 0)
    red[me] = mine[0:1]

    def red_copy(i):
        return pltpu.make_async_remote_copy(
            src_ref=red.at[me],
            dst_ref=red.at[me],
            send_sem=rd_send,
            recv_sem=rd_recv,
            device_id=lon_peer(i),
            device_id_type=MESH,
        )

    def every(sem):
        return pltpu.make_async_copy(red.at[pl.ds(0, n - 1)], red.at[pl.ds(0, n - 1)], sem)

    peers_loop(n, lambda i: red_copy(i).start())
    every(rd_recv).wait()
    terms = [red[i] for i in range(n)]
    while len(terms) > 1:
        terms = [
            terms[i] + terms[i + 1] if i + 1 < len(terms) else terms[i]
            for i in range(0, len(terms), 2)
        ]
    total = {
        name: jnp.broadcast_to(terms[0][:, q : q + 1], TILE) for q, name in enumerate(names)
    }

    coefs = []
    for v in range(2):
        m0 = total["m", v, 0, 0]
        m = [m0] + [total["m", v, 0, k] for k in range(1, 6)]
        first_moment = m[1]
        centre = zero
        for i in range(1, len(CENTRES)):
            limit = 0.5 * (CENTRES[i] + CENTRES[i - 1]) * span
            above = first_moment > limit * m0
            centre = jnp.where(above, CENTRES[i] * span, centre)
            m = [m0] + [jnp.where(above, total["m", v, i, k], m[k]) for k in range(1, 6)]
        unit = 1.0 + centre
        a = [unit * m[k] + m[k + 1] for k in range(5)]
        ratio = m[1] / m0
        step0 = m0 / a[0]
        rr1 = step0 * step0 * (m[2] - ratio * m[1])
        beta0 = rr1 / m0
        along = step0 * ratio + beta0
        p1ap1 = along * along * a[0] - 2.0 * along * step0 * a[1] + step0 * step0 * a[2]
        step1 = rr1 / p1ap1
        x0 = step0 * ratio - step1 * along * unit
        x1 = step1 * step0 * unit - (step0 + step1 * along)
        x2 = step1 * step0

        def form(y0, y1, y2, f):
            return (
                y0 * (y0 * f[0] + 2.0 * (y1 * f[1] + y2 * f[2]))
                + y1 * (y1 * f[2] + 2.0 * (y2 * f[3]))
                + y2 * (y2 * f[4])
            )

        rr2 = form(x0, x1, x2, m)
        beta1 = rr2 / rr1
        y0, y1, y2 = x0 + beta1 * along, x1 - beta1 * step0, x2
        step2 = rr2 / form(y0, y1, y2, a)
        e0 = step0 + step1 * along + step2 * y0
        e1 = step2 * y1 - step1 * step0
        e2 = step2 * y2
        coefs.append((e0 - centre * (e1 - centre * e2), e1 - 2.0 * centre * e2, e2))
        for c in own:
            w = coefs[v]
            s = powers[v][0][c] * w[0] + (powers[v][1][c] * w[1] + powers[v][2][c] * w[2])
            sout[v, col(c), :] = height[v][c] + s

    def plain(v, k):
        return total["m", v, 0, k]

    gram = []
    for v in range(2):
        w = coefs[v]
        s = total["hh", v] + 2.0 * sum(w[j] * total["h", v, v, j] for j in range(3))
        for i in range(3):
            for j in range(3):
                s = s + w[i] * w[j] * plain(v, i + j)
        gram.append(total["gram", 2 * v] + s)
    mix = total["gram", 1] + total["hh", 2]
    for j in range(3):
        mix = mix + (coefs[1][j] * total["h", 0, 1, j] + coefs[0][j] * total["h", 1, 0, j])
    for i in range(3):
        for j in range(3):
            mix = mix + coefs[0][i] * coefs[1][j] * total["c", i + j]
    cells = float((levels + 1) * 2 * 8 * 128 * n)
    gram_one, gram_two, gram_mix = gram[0] / cells, gram[1] / cells, mix / cells
    scale_one = jnp.sqrt(gram_one + EPSILON)
    cross = gram_mix / scale_one
    rest = gram_two - 2.0 * cross * cross + cross * cross * gram_one / (gram_one + EPSILON)
    scale_two = jnp.sqrt(rest + EPSILON)
    gout[0] = 1.0 / scale_one
    gout[1] = cross
    gout[2] = 1.0 / scale_two
    gout[3] = jnp.where(lane == 0, scale_one, jnp.where(lane == 1, cross, scale_two))

    for g in range(count):
        for side in range(2):
            t_copy(g, side).wait_send()
            b_copy(g, side).wait_send()
        for copy in z_copies(g):
            copy.wait_send()
    for s in SHIFTS:
        st_copy(s).wait_send()
        rx_copy(s).wait_send()
    every(rd_send).wait()


def scale_kernel(trc, surf, tail, out_h, sout_h, gout, out, sout, sem):
    levels = trc.shape[1]
    chunks = chunk_bounds(levels)
    one, cross, two = tail[0], tail[1], tail[2]

    def store(g):
        k0, k1 = chunks[g]
        return pltpu.make_async_copy(
            out.at[:, pl.ds(k0, k1 - k0)], out_h.at[:, pl.ds(k0, k1 - k0)], sem.at[g]
        )

    for g, (k0, k1) in enumerate(chunks):

        def step(k, carry):
            for h in range(2):
                rows = pl.ds(8 * h, 8)
                unit = trc[0, k, rows, :] * one
                out[0, k, rows, :] = unit
                out[1, k, rows, :] = (trc[1, k, rows, :] - cross * unit) * two
            return carry

        lax.fori_loop(k0, k1, step, 0, unroll=UNROLL)
        store(g).start()
    for h in range(2):
        rows = pl.ds(8 * h, 8)
        unit = surf[0, rows, :] * one
        sout[0, rows, :] = unit
        sout[1, rows, :] = (surf[1, rows, :] - cross * unit) * two
    last = pltpu.make_async_copy(sout, sout_h, sem.at[len(chunks)])
    last.start()
    gout[...] = tail[3]
    for g in range(len(chunks)):
        store(g).wait()
    last.wait()


def packed(x):
    lead, (cols, rows) = x.shape[:-2], x.shape[-2:]
    x = x.reshape(lead + (cols, rows // 128, 128))
    x = jnp.swapaxes(x, -3, -2)
    return x.reshape(lead + (cols * (rows // 128), 128))


def unpacked(x, cols):
    lead, (rows, lanes) = x.shape[:-2], x.shape[-2:]
    x = x.reshape(lead + (rows // cols, cols, lanes))
    x = jnp.swapaxes(x, -3, -2)
    return x.reshape(lead + (cols, rows // cols * lanes))


def on_device(n, groups, tracer_pert, surface_pert, zonal_flow, merid_flow, bottom_level):
    vectors, levels, columns, rows = tracer_pert.shape
    count = len(chunk_bounds(levels))
    share = shares_zonal(groups, levels)
    f32 = jnp.float32
    vmem = pl.BlockSpec(memory_space=pltpu.VMEM)
    hbm = pl.BlockSpec(memory_space=pltpu.HBM)
    dma = pltpu.SemaphoreType.DMA
    zonal_sems = 3 if share else 2
    tracer, surface, tail = pl.pallas_call(
        functools.partial(kernel, n, share),
        out_shape=(
            jax.ShapeDtypeStruct((vectors, levels, 16, 128), f32),
            jax.ShapeDtypeStruct((vectors, 16, 128), f32),
            jax.ShapeDtypeStruct((4, 8, 128), f32),
        ),
        in_specs=[hbm] * 5,
        out_specs=(vmem,) * 3,
        scratch_shapes=[
            pltpu.VMEM((vectors, levels, 16, 128), f32),
            pltpu.VMEM((vectors, 16, 128), f32),
            pltpu.VMEM((levels, 16, 128), f32),
            pltpu.VMEM((levels, 16, 128), f32),
            pltpu.VMEM((16, 128), jnp.int32),
            pltpu.VMEM((2, levels, 2, 8, 128), f32),
            pltpu.VMEM((2, levels, 2, 8, 128), f32),
            pltpu.VMEM((2, levels, 8, 128), f32),
            pltpu.VMEM((2, levels, 8, 128), f32),
            pltpu.VMEM((2, levels, 2, 8, 128), f32),
            pltpu.VMEM((2, levels, 2, 8, 128), f32),
            pltpu.VMEM((levels, 10, 8, 128), f32),
            pltpu.VMEM((SLOTS, 6, 8, 128), f32),
            pltpu.VMEM((SLOTS, 4, 8, 128), f32),
            pltpu.VMEM((n, 1, 128), f32),
            dma((5, count)),
            dma((2, count)),
            dma((2, count)),
            dma((zonal_sems, count)),
            dma((zonal_sems, count)),
            dma((2, count)),
            dma((2, count)),
            dma((SLOTS,)),
            dma((SLOTS,)),
            dma((SLOTS,)),
            dma((SLOTS,)),
            dma(()),
            dma(()),
            pltpu.SemaphoreType.REGULAR((max(1, len(spread_rounds(n))),)),
        ],
        compiler_params=pltpu.CompilerParams(
            collective_id=0, has_side_effects=True, vmem_limit_bytes=40 * 1024 * 1024
        ),
    )(
        *(
            pltpu.with_memory_space_constraint(packed(x), pltpu.HBM)
            for x in (tracer_pert, surface_pert, zonal_flow, merid_flow, bottom_level)
        )
    )
    tracer, surface, growth = pl.pallas_call(
        scale_kernel,
        out_shape=(
            jax.ShapeDtypeStruct((vectors, levels, 16, 128), f32),
            jax.ShapeDtypeStruct((vectors, 16, 128), f32),
            jax.ShapeDtypeStruct((8, 128), f32),
        ),
        in_specs=[vmem] * 3,
        out_specs=(hbm, hbm, vmem),
        scratch_shapes=[
            pltpu.VMEM((vectors, levels, 16, 128), f32),
            pltpu.VMEM((vectors, 16, 128), f32),
            dma((count + 1,)),
        ],
        compiler_params=pltpu.CompilerParams(vmem_limit_bytes=16 * 1024 * 1024),
    )(tracer, surface, tail)
    return unpacked(tracer, columns), unpacked(surface, columns), growth[0, :3]


def solution(mesh):
    placed = (
        P("grp", None, "lon", None),
        P("grp", "lon", None),
        P(None, "lon", None),
        P(None, "lon", None),
        P("lon", None),
    )
    return jax.shard_map(
        functools.partial(on_device, mesh.shape["lon"], mesh.shape["grp"]),
        mesh=mesh,
        in_specs=placed,
        out_specs=(P("grp", None, "lon", None), P("grp", "lon", None), P("grp")),
        check_vma=False,
    )
```

```python
import functools

import jax
import jax.numpy as jnp
from jax import lax
from jax.experimental import pallas as pl
from jax.experimental.pallas import tpu as pltpu
from jax.sharding import PartitionSpec as P

DIFFUSIVITY = 0.5
TIME_STEP = 0.2
SURFACE_COUPLING = 0.5
STERIC_GAIN = 2.0
EPSILON = 1e-06
MESH = pl.DeviceIdType.MESH
CHUNKS = 5
UNROLL = 5
NEAR = (1, -1)
SHIFTS = (1, -1, 2, -2)
SLOTS = 5
OWN = 2
CENTRES = (0.0, 0.04, 0.16, 0.64)
TILE = (8, 128)


def chunk_bounds(levels):
    count = min(CHUNKS, levels)
    edges = [levels * i // count for i in range(count + 1)]
    return list(zip(edges[:-1], edges[1:]))


def spread_rounds(n):
    reach, rounds = 1, []
    while 2 * reach < n:
        rounds.append(reach)
        reach *= 2
    return rounds


def shares_zonal(groups, levels):
    return groups == 2 and levels % 2 == 0


def peers_loop(n, body):
    if n <= 16:
        for i in range(1, n):
            body(i)
    else:

        def step(i, carry):
            body(i)
            return carry

        lax.fori_loop(1, n, step, 0)


def kernel(
    n, share, trc_h, surf_h, zon_h, mer_h, bot_h, out, sout, gout,
    trc, surf, zon, mer, bot, s_t, r_t, s_z, r_z, s_b, r_b, coef, st, rx, red,
    in_sem, t_send, t_recv, z_send, z_recv, b_send, b_recv,
    st_send, st_recv, rx_send, rx_recv, rd_send, rd_recv, met,
):
    me = lax.axis_index("lon")
    grp = lax.axis_index("grp")
    levels = zon.shape[0]
    chunks = chunk_bounds(levels)
    side_dev = (lax.rem(me + n - 1, n), lax.rem(me + 1, n))
    outer = lax.rem(me, 2)
    inner = 1 - outer
    lane = lax.broadcasted_iota(jnp.int32, TILE, 1)
    row = lax.broadcasted_iota(jnp.int32, TILE, 0)
    last_lane, first_lane = lane == 127, lane == 0

    def north(x):
        rolled = pltpu.roll(x, 127, 1)
        return jnp.where(last_lane, pltpu.roll(rolled, 7, 0), rolled)

    def south(x):
        rolled = pltpu.roll(x, 1, 1)
        return jnp.where(first_lane, pltpu.roll(rolled, 1, 0), rolled)

    def col(c):
        return pl.ds(c, 8, stride=2)

    def lon_peer(s):
        return {"lon": lax.rem(me + s + n, n)}

    barrier = pltpu.get_barrier_semaphore()
    for s in NEAR:
        pl.semaphore_signal(barrier, inc=1, device_id=lon_peer(s), device_id_type=MESH)
    if share:
        pl.semaphore_signal(barrier, inc=1, device_id={"grp": 1 - grp}, device_id_type=MESH)

    half = levels // 2
    mine = pl.ds(grp * half if share else 0, half)
    theirs = pl.ds((1 - grp) * half, half) if share else pl.ds(half, levels - half)

    def load(which, g):
        k0, k1 = chunks[g]
        ks = pl.ds(k0, k1 - k0)
        src, dst = ((trc_h.at[:, ks], trc.at[:, ks]), (mer_h.at[ks], mer.at[ks]))[which]
        return pltpu.make_async_copy(src, dst, in_sem.at[which, g])

    count = len(chunks)
    load_zon = [
        pltpu.make_async_copy(zon_h.at[ks], zon.at[ks], in_sem.at[2, i])
        for i, ks in enumerate((mine, theirs))
    ]
    load_bot = pltpu.make_async_copy(bot_h, bot, in_sem.at[3, 0])
    load_surf = pltpu.make_async_copy(surf_h, surf, in_sem.at[3, 1])
    load_zon[0].start()
    load_bot.start()
    load_surf.start()
    load(0, 0).start()
    load_zon[1].start()
    for g in range(1, count):
        load(0, g).start()
    for g in range(count):
        load(1, g).start()
    def gather_chunk(g):
        load(0, g).wait()

        def step(k, carry):
            for c in range(2):
                s_t[c, k, 0] = trc[0, k, col(c), :]
                s_t[c, k, 1] = trc[1, k, col(c), :]
            return carry

        lax.fori_loop(*chunks[g], step, 0, unroll=UNROLL)

    def side_copy(src, dst, send, recv, g, side):
        k0, k1 = chunks[g]
        return pltpu.make_async_remote_copy(
            src_ref=src.at[side, pl.ds(k0, k1 - k0)],
            dst_ref=dst.at[1 - side, pl.ds(k0, k1 - k0)],
            send_sem=send.at[side, g],
            recv_sem=recv.at[1 - side, g],
            device_id={"lon": side_dev[side]},
            device_id_type=MESH,
        )

    def t_copy(g, side):
        return side_copy(s_t, r_t, t_send, t_recv, g, side)

    def b_copy(g, side):
        return side_copy(s_b, r_b, b_send, b_recv, g, side)

    def gather_zonal(i):
        load_zon[i].wait()
        ks = (mine, theirs)[i]

        def step(k, carry):
            for c in range(2):
                s_z[c, ks.start + k] = zon[ks.start + k, col(c), :]
            return carry

        lax.fori_loop(0, ks.size, step, 0, unroll=UNROLL)

    def z_copy(which):
        if not share:
            return pltpu.make_async_remote_copy(
                src_ref=s_z.at[which],
                dst_ref=r_z.at[1 - which],
                send_sem=z_send.at[which],
                recv_sem=z_recv.at[which],
                device_id={"lon": side_dev[which]},
                device_id_type=MESH,
            )
        src, dst, dev = (
            (s_z.at[outer, mine], r_z.at[1 - outer, mine], lon_peer(2 * outer - 1)),
            (s_z.at[inner], r_z.at[1 - inner], lon_peer(2 * inner - 1)),
            (r_z.at[outer, mine], r_z.at[outer, mine], {"grp": 1 - grp}),
        )[which]
        return pltpu.make_async_remote_copy(
            src_ref=src,
            dst_ref=dst,
            send_sem=z_send.at[which],
            recv_sem=z_recv.at[which],
            device_id=dev,
            device_id_type=MESH,
        )

    def send_chunk(g):
        for side in range(2):
            t_copy(g, side).start()

    def shift_copy(buf, send, recv, s, part):
        return pltpu.make_async_remote_copy(
            src_ref=buf.at[OWN, part],
            dst_ref=buf.at[OWN - s, part],
            send_sem=send.at[OWN - s],
            recv_sem=recv.at[OWN - s],
            device_id=lon_peer(s),
            device_id_type=MESH,
        )

    def st_copy(s):
        part = {1: pl.ds(0, 4), -1: pl.ds(2, 4), 2: pl.ds(3, 1), -2: pl.ds(2, 1)}[s]
        return shift_copy(st, st_send, st_recv, s, part)

    def rx_copy(s):
        part = {1: pl.ds(0, 4), -1: pl.ds(0, 4), 2: pl.ds(2, 2), -2: pl.ds(0, 2)}[s]
        return shift_copy(rx, rx_send, rx_recv, s, part)

    gather_zonal(0)
    pl.semaphore_wait(barrier, len(NEAR) + (1 if share else 0))
    if share:
        z_copy(0).start()
    load_bot.wait()
    load_surf.wait()
    for c in range(2):
        d = bot[col(c), :].astype(jnp.float32)
        st[OWN, 2 + c] = d
        for v in range(2):
            st[OWN, (4, 0)[c] + v] = jnp.where(d > 0, surf[v, col(c), :], 0.0)
    for s in NEAR:
        st_copy(s).start()
    gather_chunk(0)
    send_chunk(0)
    gather_zonal(1)
    for which in range(1 if share else 0, 2):
        z_copy(which).start()
    rounds = spread_rounds(n)

    def spread(i):
        if i < len(rounds):
            for s in (rounds[i], -rounds[i]):
                pl.semaphore_signal(
                    met.at[i], inc=1, device_id=lon_peer(s), device_id_type=MESH
                )

    def spread_wait(i):
        if i < len(rounds):
            pl.semaphore_wait(met.at[i], 2)

    spread(0)
    for g in range(1, count):
        gather_chunk(g)
        send_chunk(g)

    spread_wait(0)
    for s in SHIFTS[2:]:
        st_copy(s).start()
    spread(1)
    for s in NEAR:
        st_copy(s).wait_recv()

    depths = {-2: st[1, 2], -1: st[1, 3], 0: st[2, 2], 1: st[2, 3], 2: st[3, 2], 3: st[3, 3]}

    def y_face(i):
        wall = jnp.logical_and(last_lane, row == 7)
        return jnp.where(wall, 0.0, jnp.minimum(depths[i], north(depths[i])))

    def x_face(i):
        return jnp.minimum(depths[i], depths[i + 1])

    for which in range(2):
        z_copy(which).wait_recv()
    if share:
        z_copy(2).start()
        z_copy(2).wait_recv()
    quarter = TIME_STEP * 0.25
    diff = TIME_STEP * DIFFUSIVITY
    faces_x = [x_face(f - 1) for f in range(3)]
    faces_y = [y_face(c) for c in range(2)]
    own_depth = [depths[c] for c in range(2)]

    for g, (k0, k1) in enumerate(chunks):
        load(1, g).wait()
        for side in range(2):
            t_copy(g, side).wait_recv()

        def first(k, carry):
            kf = k.astype(jnp.float32)
            z = (r_z[0, k], s_z[0, k], s_z[1, k], r_z[1, k])
            cx = []
            for f in range(3):
                open_f = kf < faces_x[f]
                u = quarter * (z[f] + z[f + 1])
                cx.append((jnp.where(open_f, u + diff, 0.0), jnp.where(open_f, u - diff, 0.0)))
            cy = []
            for c in range(2):
                open_f = kf < faces_y[c]
                m = mer[k, col(c), :]
                u = quarter * (m + north(m))
                cy.append((jnp.where(open_f, u + diff, 0.0), jnp.where(open_f, u - diff, 0.0)))
            for q, (lo, hi) in enumerate(cx + cy):
                coef[k, 2 * q] = lo
                coef[k, 2 * q + 1] = hi
            wet = [kf < own_depth[c] for c in range(2)]
            for v in range(2):
                t = (
                    r_t[0, k, v],
                    jnp.where(wet[0], s_t[0, k, v], 0.0),
                    jnp.where(wet[1], s_t[1, k, v], 0.0),
                    r_t[1, k, v],
                )
                fx = [cx[f][0] * t[f] + cx[f][1] * t[f + 1] for f in range(3)]
                for c in range(2):
                    fy = cy[c][0] * t[c + 1] + cy[c][1] * north(t[c + 1])
                    s_b[c, k, v] = t[c + 1] - ((fx[c + 1] - fx[c]) + (fy - south(fy)))
            return carry

        lax.fori_loop(k0, k1, first, 0, unroll=UNROLL)
        for side in range(2):
            b_copy(g, side).start()
        spread_wait(g + 1)
        spread(g + 2)
    for i in range(count + 1, len(rounds)):
        spread_wait(i)
        spread(i + 1)
    for s in SHIFTS[2:]:
        st_copy(s).wait_recv()
    depths.update({-3: st[0, 3], 4: st[4, 2]})

    face_x = {i: SURFACE_COUPLING * x_face(i) for i in range(-3, 4)}
    face_y = {i: SURFACE_COUPLING * y_face(i) for i in range(-2, 4)}

    def lap(s, cols):
        gx = {i: face_x[i] * (s[i + 1] - s[i]) for i in range(cols[0] - 1, cols[-1] + 1)}
        res = {}
        for i in cols:
            gy = face_y[i] * (north(s[i]) - s[i])
            res[i] = -((gx[i] - gx[i - 1]) + (gy - south(gy)))
        return res

    own = (0, 1)
    height = [{-1: st[1, v], 0: st[2, 4 + v], 1: st[2, v], 2: st[3, 4 + v]} for v in range(2)]
    lap_h = [lap(height[v], own) for v in range(2)]

    zero = jnp.zeros(TILE, jnp.float32)
    totals = (zero,) * 7
    for g, (k0, k1) in enumerate(chunks):
        for side in range(2):
            b_copy(g, side).wait_recv()

        def second(k, carry):
            sums, grams = list(carry[:4]), list(carry[4:])
            cx = [(coef[k, 2 * f], coef[k, 2 * f + 1]) for f in range(3)]
            cy = [(coef[k, 6 + 2 * c], coef[k, 7 + 2 * c]) for c in range(2)]
            new = []
            for v in range(2):
                t = (r_b[0, k, v], s_b[0, k, v], s_b[1, k, v], r_b[1, k, v])
                fx = [cx[f][0] * t[f] + cx[f][1] * t[f + 1] for f in range(3)]
                for c in range(2):
                    fy = cy[c][0] * t[c + 1] + cy[c][1] * north(t[c + 1])
                    val = t[c + 1] - ((fx[c + 1] - fx[c]) + (fy - south(fy)))
                    out[v, k, col(c), :] = val
                    sums[2 * v + c] = sums[2 * v + c] + val
                    new.append(val)
            grams[0] = grams[0] + (new[0] * new[0] + new[1] * new[1])
            grams[1] = grams[1] + (new[0] * new[2] + new[1] * new[3])
            grams[2] = grams[2] + (new[2] * new[2] + new[3] * new[3])
            return tuple(sums + grams)

        totals = lax.fori_loop(k0, k1, second, totals, unroll=UNROLL)

    gain = STERIC_GAIN / levels
    for v in range(2):
        for c in range(2):
            rx[OWN, 2 * c + v] = gain * totals[2 * v + c] - lap_h[v][c]
    for s in SHIFTS:
        rx_copy(s).start()

    def dot(a, b):
        return a[0] * b[0] + a[1] * b[1]

    parts = {}
    for q in range(3):
        parts["gram", q] = totals[4 + q]
    parts["hh", 0] = dot(height[0], height[0])
    parts["hh", 1] = dot(height[1], height[1])
    parts["hh", 2] = dot(height[0], height[1])
    for s in SHIFTS:
        rx_copy(s).wait_recv()

    span = 4.0 * levels
    powers = []
    for v in range(2):
        r = {-3: rx[0, 2 + v], 4: rx[4, v]}
        for c in range(2):
            r.update({c - 2: rx[1, 2 * c + v], c: rx[2, 2 * c + v], c + 2: rx[3, 2 * c + v]})
        l1 = lap(r, range(-2, 4))
        l2 = lap(l1, range(-1, 3))
        l3 = lap(l2, own)
        powers.append((r, l1, l2, l3))
    for v in range(2):
        for i, centre in enumerate(CENTRES):
            b = [{c: p[c] for c in own} for p in powers[v]]
            base = [b[0]]
            for j in range(3):
                if centre:
                    b = [
                        {c: b[q + 1][c] - (centre * span) * b[q][c] for c in own}
                        for q in range(3 - j)
                    ]
                else:
                    b = b[1:]
                base.append(b[0])
            for k in range(1 if i else 0, 6):
                parts["m", v, i, k] = dot(base[k // 2], base[(k + 1) // 2])
        for j in range(3):
            parts["h", v, v, j] = dot(height[v], powers[v][j])
            parts["h", v, 1 - v, j] = dot(height[v], powers[1 - v][j])
    for k in range(5):
        parts["c", k] = dot(powers[0][k // 2], powers[1][(k + 1) // 2])

    names = list(parts)
    level, shift = [parts[name] for name in names], 1
    while shift < 128:
        if len(level) == 1:
            level = [level[0] + pltpu.roll(level[0], shift, 1)]
        else:
            even = jnp.bitwise_and(lane, shift) == 0
            merged = []
            for i in range(0, len(level), 2):
                a, b = level[i], level[min(i + 1, len(level) - 1)]
                merged.append(jnp.where(even, a, b) + pltpu.roll(jnp.where(even, b, a), shift, 1))
            level = merged
        shift *= 2
    local = level[0]
    for shift in (4, 2, 1):
        local = local + pltpu.roll(local, shift, 0)
    red[me] = local[0:1]

    def red_copy(i):
        return pltpu.make_async_remote_copy(
            src_ref=red.at[me],
            dst_ref=red.at[me],
            send_sem=rd_send,
            recv_sem=rd_recv,
            device_id=lon_peer(i),
            device_id_type=MESH,
        )

    def every(sem):
        return pltpu.make_async_copy(red.at[pl.ds(0, n - 1)], red.at[pl.ds(0, n - 1)], sem)

    peers_loop(n, lambda i: red_copy(i).start())
    every(rd_recv).wait()
    terms = [red[i] for i in range(n)]
    while len(terms) > 1:
        terms = [
            terms[i] + terms[i + 1] if i + 1 < len(terms) else terms[i]
            for i in range(0, len(terms), 2)
        ]
    total = {
        name: jnp.broadcast_to(terms[0][:, q : q + 1], TILE) for q, name in enumerate(names)
    }

    coefs = []
    for v in range(2):
        m0 = total["m", v, 0, 0]
        m = [m0] + [total["m", v, 0, k] for k in range(1, 6)]
        first_moment = m[1]
        centre = zero
        for i in range(1, len(CENTRES)):
            limit = 0.5 * (CENTRES[i] + CENTRES[i - 1]) * span
            above = first_moment > limit * m0
            centre = jnp.where(above, CENTRES[i] * span, centre)
            m = [m0] + [jnp.where(above, total["m", v, i, k], m[k]) for k in range(1, 6)]
        unit = 1.0 + centre
        a = [unit * m[k] + m[k + 1] for k in range(5)]
        ratio = m[1] / m0
        step0 = m0 / a[0]
        rr1 = step0 * step0 * (m[2] - ratio * m[1])
        beta0 = rr1 / m0
        along = step0 * ratio + beta0
        p1ap1 = along * along * a[0] - 2.0 * along * step0 * a[1] + step0 * step0 * a[2]
        step1 = rr1 / p1ap1
        x0 = step0 * ratio - step1 * along * unit
        x1 = step1 * step0 * unit - (step0 + step1 * along)
        x2 = step1 * step0

        def form(y0, y1, y2, f):
            return (
                y0 * (y0 * f[0] + 2.0 * (y1 * f[1] + y2 * f[2]))
                + y1 * (y1 * f[2] + 2.0 * (y2 * f[3]))
                + y2 * (y2 * f[4])
            )

        rr2 = form(x0, x1, x2, m)
        beta1 = rr2 / rr1
        y0, y1, y2 = x0 + beta1 * along, x1 - beta1 * step0, x2
        step2 = rr2 / form(y0, y1, y2, a)
        e0 = step0 + step1 * along + step2 * y0
        e1 = step2 * y1 - step1 * step0
        e2 = step2 * y2
        coefs.append((e0 - centre * (e1 - centre * e2), e1 - 2.0 * centre * e2, e2))
        for c in own:
            w = coefs[v]
            s = powers[v][0][c] * w[0] + (powers[v][1][c] * w[1] + powers[v][2][c] * w[2])
            sout[v, col(c), :] = height[v][c] + s

    def plain(v, k):
        return total["m", v, 0, k]

    gram = []
    for v in range(2):
        w = coefs[v]
        s = total["hh", v] + 2.0 * sum(w[j] * total["h", v, v, j] for j in range(3))
        for i in range(3):
            for j in range(3):
                s = s + w[i] * w[j] * plain(v, i + j)
        gram.append(total["gram", 2 * v] + s)
    mix = total["gram", 1] + total["hh", 2]
    for j in range(3):
        mix = mix + (coefs[1][j] * total["h", 0, 1, j] + coefs[0][j] * total["h", 1, 0, j])
    for i in range(3):
        for j in range(3):
            mix = mix + coefs[0][i] * coefs[1][j] * total["c", i + j]
    cells = float((levels + 1) * 2 * 8 * 128 * n)
    gram_one, gram_two, gram_mix = gram[0] / cells, gram[1] / cells, mix / cells
    scale_one = jnp.sqrt(gram_one + EPSILON)
    cross = gram_mix / scale_one
    rest = gram_two - 2.0 * cross * cross + cross * cross * gram_one / (gram_one + EPSILON)
    scale_two = jnp.sqrt(rest + EPSILON)
    gout[0] = 1.0 / scale_one
    gout[1] = cross
    gout[2] = 1.0 / scale_two
    gout[3] = jnp.where(lane == 0, scale_one, jnp.where(lane == 1, cross, scale_two))

    for g in range(count):
        for side in range(2):
            t_copy(g, side).wait_send()
            b_copy(g, side).wait_send()
    for which in range(3 if share else 2):
        z_copy(which).wait_send()
    for s in SHIFTS:
        st_copy(s).wait_send()
        rx_copy(s).wait_send()
    every(rd_send).wait()


def scale_kernel(trc, surf, tail, out_h, sout_h, gout, out, sout, sem):
    levels = trc.shape[1]
    chunks = chunk_bounds(levels)
    one, cross, two = tail[0], tail[1], tail[2]

    def store(g):
        k0, k1 = chunks[g]
        return pltpu.make_async_copy(
            out.at[:, pl.ds(k0, k1 - k0)], out_h.at[:, pl.ds(k0, k1 - k0)], sem.at[g]
        )

    for g, (k0, k1) in enumerate(chunks):

        def step(k, carry):
            for h in range(2):
                rows = pl.ds(8 * h, 8)
                unit = trc[0, k, rows, :] * one
                out[0, k, rows, :] = unit
                out[1, k, rows, :] = (trc[1, k, rows, :] - cross * unit) * two
            return carry

        lax.fori_loop(k0, k1, step, 0, unroll=UNROLL)
        store(g).start()
    for h in range(2):
        rows = pl.ds(8 * h, 8)
        unit = surf[0, rows, :] * one
        sout[0, rows, :] = unit
        sout[1, rows, :] = (surf[1, rows, :] - cross * unit) * two
    last = pltpu.make_async_copy(sout, sout_h, sem.at[len(chunks)])
    last.start()
    gout[...] = tail[3]
    for g in range(len(chunks)):
        store(g).wait()
    last.wait()


def packed(x):
    lead, (cols, rows) = x.shape[:-2], x.shape[-2:]
    x = x.reshape(lead + (cols, rows // 128, 128))
    x = jnp.swapaxes(x, -3, -2)
    return x.reshape(lead + (cols * (rows // 128), 128))


def unpacked(x, cols):
    lead, (rows, lanes) = x.shape[:-2], x.shape[-2:]
    x = x.reshape(lead + (rows // cols, cols, lanes))
    x = jnp.swapaxes(x, -3, -2)
    return x.reshape(lead + (cols, rows // cols * lanes))


def on_device(n, groups, tracer_pert, surface_pert, zonal_flow, merid_flow, bottom_level):
    vectors, levels, columns, rows = tracer_pert.shape
    count = len(chunk_bounds(levels))
    share = shares_zonal(groups, levels)
    f32 = jnp.float32
    vmem = pl.BlockSpec(memory_space=pltpu.VMEM)
    hbm = pl.BlockSpec(memory_space=pltpu.HBM)
    dma = pltpu.SemaphoreType.DMA
    zonal_sems = 3 if share else 2
    tracer, surface, tail = pl.pallas_call(
        functools.partial(kernel, n, share),
        out_shape=(
            jax.ShapeDtypeStruct((vectors, levels, 16, 128), f32),
            jax.ShapeDtypeStruct((vectors, 16, 128), f32),
            jax.ShapeDtypeStruct((4, 8, 128), f32),
        ),
        in_specs=[hbm] * 5,
        out_specs=(vmem,) * 3,
        scratch_shapes=[
            pltpu.VMEM((vectors, levels, 16, 128), f32),
            pltpu.VMEM((vectors, 16, 128), f32),
            pltpu.VMEM((levels, 16, 128), f32),
            pltpu.VMEM((levels, 16, 128), f32),
            pltpu.VMEM((16, 128), jnp.int32),
            pltpu.VMEM((2, levels, 2, 8, 128), f32),
            pltpu.VMEM((2, levels, 2, 8, 128), f32),
            pltpu.VMEM((2, levels, 8, 128), f32),
            pltpu.VMEM((2, levels, 8, 128), f32),
            pltpu.VMEM((2, levels, 2, 8, 128), f32),
            pltpu.VMEM((2, levels, 2, 8, 128), f32),
            pltpu.VMEM((levels, 10, 8, 128), f32),
            pltpu.VMEM((SLOTS, 6, 8, 128), f32),
            pltpu.VMEM((SLOTS, 4, 8, 128), f32),
            pltpu.VMEM((n, 1, 128), f32),
            dma((4, max(2, count))),
            dma((2, count)),
            dma((2, count)),
            dma((zonal_sems,)),
            dma((zonal_sems,)),
            dma((2, count)),
            dma((2, count)),
            dma((SLOTS,)),
            dma((SLOTS,)),
            dma((SLOTS,)),
            dma((SLOTS,)),
            dma(()),
            dma(()),
            pltpu.SemaphoreType.REGULAR((max(1, len(spread_rounds(n))),)),
        ],
        compiler_params=pltpu.CompilerParams(
            collective_id=0, has_side_effects=True, vmem_limit_bytes=40 * 1024 * 1024
        ),
    )(
        *(
            pltpu.with_memory_space_constraint(packed(x), pltpu.HBM)
            for x in (tracer_pert, surface_pert, zonal_flow, merid_flow, bottom_level)
        )
    )
    tracer, surface, growth = pl.pallas_call(
        scale_kernel,
        out_shape=(
            jax.ShapeDtypeStruct((vectors, levels, 16, 128), f32),
            jax.ShapeDtypeStruct((vectors, 16, 128), f32),
            jax.ShapeDtypeStruct((8, 128), f32),
        ),
        in_specs=[vmem] * 3,
        out_specs=(hbm, hbm, vmem),
        scratch_shapes=[
            pltpu.VMEM((vectors, levels, 16, 128), f32),
            pltpu.VMEM((vectors, 16, 128), f32),
            dma((count + 1,)),
        ],
        compiler_params=pltpu.CompilerParams(vmem_limit_bytes=16 * 1024 * 1024),
    )(tracer, surface, tail)
    return unpacked(tracer, columns), unpacked(surface, columns), growth[0, :3]


def solution(mesh):
    placed = (
        P("grp", None, "lon", None),
        P("grp", "lon", None),
        P(None, "lon", None),
        P(None, "lon", None),
        P("lon", None),
    )
    return jax.shard_map(
        functools.partial(on_device, mesh.shape["lon"], mesh.shape["grp"]),
        mesh=mesh,
        in_specs=placed,
        out_specs=(P("grp", None, "lon", None), P("grp", "lon", None), P("grp")),
        check_vma=False,
    )
```

```python
import functools

import jax
import jax.numpy as jnp
from jax import lax
from jax.experimental import pallas as pl
from jax.experimental.pallas import tpu as pltpu
from jax.sharding import PartitionSpec as P

DIFFUSIVITY = 0.5
TIME_STEP = 0.2
SURFACE_COUPLING = 0.5
STERIC_GAIN = 2.0
EPSILON = 1e-06
MESH = pl.DeviceIdType.MESH
CHUNKS = 5
UNROLL = 5
NEAR = (1, -1)
SLOT = {0: 0, 1: 1, 2: 2, 3: 3, -1: 4}
WINDOW = (-2, -1, 0, 1)
CENTRES = (0.0, 0.04, 0.16, 0.64)
TILE = (8, 128)


def chunk_bounds(levels):
    count = min(CHUNKS, levels)
    edges = [levels * i // count for i in range(count + 1)]
    return list(zip(edges[:-1], edges[1:]))


def spread_rounds(n):
    reach, rounds = 1, []
    while 2 * reach < n:
        rounds.append(reach)
        reach *= 2
    return rounds


def shares_zonal(groups, levels):
    return groups == 2 and levels % 2 == 0


def peers_loop(n, body):
    if n <= 16:
        for i in range(1, n):
            body(i)
    else:

        def step(i, carry):
            body(i)
            return carry

        lax.fori_loop(1, n, step, 0)


def kernel(
    n, share, trc_h, surf_h, zon_h, mer_h, bot_h, out, sout, gout,
    trc, surf, zon, mer, bot, s_t, r_t, s_z, r_z, s_b, r_b, coef, st, rx, red,
    in_sem, t_send, t_recv, z_send, z_recv, b_send, b_recv,
    st_send, st_recv, rx_send, rx_recv, rd_send, rd_recv, met,
):
    me = lax.axis_index("lon")
    grp = lax.axis_index("grp")
    levels = zon.shape[0]
    chunks = chunk_bounds(levels)
    side_dev = (lax.rem(me + n - 1, n), lax.rem(me + 1, n))
    outer = lax.rem(me, 2)
    inner = 1 - outer
    lane = lax.broadcasted_iota(jnp.int32, TILE, 1)
    row = lax.broadcasted_iota(jnp.int32, TILE, 0)
    last_lane, first_lane = lane == 127, lane == 0

    def north(x):
        rolled = pltpu.roll(x, 127, 1)
        return jnp.where(last_lane, pltpu.roll(rolled, 7, 0), rolled)

    def south(x):
        rolled = pltpu.roll(x, 1, 1)
        return jnp.where(first_lane, pltpu.roll(rolled, 1, 0), rolled)

    def col(c):
        return pl.ds(c, 8, stride=2)

    def lon_peer(s):
        return {"lon": lax.rem(me + s + n, n)}

    barrier = pltpu.get_barrier_semaphore()
    for s in NEAR:
        pl.semaphore_signal(barrier, inc=1, device_id=lon_peer(s), device_id_type=MESH)
    if share:
        pl.semaphore_signal(barrier, inc=1, device_id={"grp": 1 - grp}, device_id_type=MESH)

    half = levels // 2
    mine = pl.ds(grp * half if share else 0, half)
    theirs = pl.ds((1 - grp) * half, half) if share else pl.ds(half, levels - half)

    def load(which, g):
        k0, k1 = chunks[g]
        ks = pl.ds(k0, k1 - k0)
        src, dst = ((trc_h.at[:, ks], trc.at[:, ks]), (mer_h.at[ks], mer.at[ks]))[which]
        return pltpu.make_async_copy(src, dst, in_sem.at[which, g])

    count = len(chunks)
    load_zon = [
        pltpu.make_async_copy(zon_h.at[ks], zon.at[ks], in_sem.at[2, i])
        for i, ks in enumerate((mine, theirs))
    ]
    load_bot = pltpu.make_async_copy(bot_h, bot, in_sem.at[3, 0])
    load_surf = pltpu.make_async_copy(surf_h, surf, in_sem.at[3, 1])
    load_zon[0].start()
    load_bot.start()
    load_surf.start()
    load(0, 0).start()
    load_zon[1].start()
    for g in range(1, count):
        load(0, g).start()
    for g in range(count):
        load(1, g).start()
    def gather_chunk(g):
        load(0, g).wait()

        def step(k, carry):
            for c in range(2):
                s_t[c, k, 0] = trc[0, k, col(c), :]
                s_t[c, k, 1] = trc[1, k, col(c), :]
            return carry

        lax.fori_loop(*chunks[g], step, 0, unroll=UNROLL)

    def side_copy(src, dst, send, recv, g, side):
        k0, k1 = chunks[g]
        return pltpu.make_async_remote_copy(
            src_ref=src.at[side, pl.ds(k0, k1 - k0)],
            dst_ref=dst.at[1 - side, pl.ds(k0, k1 - k0)],
            send_sem=send.at[side, g],
            recv_sem=recv.at[1 - side, g],
            device_id={"lon": side_dev[side]},
            device_id_type=MESH,
        )

    def t_copy(g, side):
        return side_copy(s_t, r_t, t_send, t_recv, g, side)

    def b_copy(g, side):
        return side_copy(s_b, r_b, b_send, b_recv, g, side)

    def gather_zonal(i):
        load_zon[i].wait()
        ks = (mine, theirs)[i]

        def step(k, carry):
            for c in range(2):
                s_z[c, ks.start + k] = zon[ks.start + k, col(c), :]
            return carry

        lax.fori_loop(0, ks.size, step, 0, unroll=UNROLL)

    def z_copy(which):
        if not share:
            return pltpu.make_async_remote_copy(
                src_ref=s_z.at[which],
                dst_ref=r_z.at[1 - which],
                send_sem=z_send.at[which],
                recv_sem=z_recv.at[which],
                device_id={"lon": side_dev[which]},
                device_id_type=MESH,
            )
        src, dst, dev = (
            (s_z.at[outer, mine], r_z.at[1 - outer, mine], lon_peer(2 * outer - 1)),
            (s_z.at[inner], r_z.at[1 - inner], lon_peer(2 * inner - 1)),
            (r_z.at[outer, mine], r_z.at[outer, mine], {"grp": 1 - grp}),
        )[which]
        return pltpu.make_async_remote_copy(
            src_ref=src,
            dst_ref=dst,
            send_sem=z_send.at[which],
            recv_sem=z_recv.at[which],
            device_id=dev,
            device_id_type=MESH,
        )

    def send_chunk(g):
        for side in range(2):
            t_copy(g, side).start()

    def shift_copy(buf, send, recv, s, part):
        return pltpu.make_async_remote_copy(
            src_ref=buf.at[0, part],
            dst_ref=buf.at[SLOT[s], part],
            send_sem=send.at[SLOT[s]],
            recv_sem=recv.at[SLOT[s]],
            device_id=lon_peer(s),
            device_id_type=MESH,
        )

    def shift_copies(buf, send, recv, cases, act):
        for s, usual, closing in cases:
            closes = me == (0 if act == "wait_recv" else n - s)
            if usual == closing:
                getattr(shift_copy(buf, send, recv, s, usual), act)()
                continue
            if usual is not None:

                @pl.when(jnp.logical_not(closes))
                def _():
                    getattr(shift_copy(buf, send, recv, s, usual), act)()

            @pl.when(closes)
            def _():
                getattr(shift_copy(buf, send, recv, s, closing), act)()

    st_near = ((1, pl.ds(0, 4), pl.ds(0, 6)), (-1, pl.ds(2, 4), pl.ds(2, 4)))
    st_far = ((2, pl.ds(3, 1), pl.ds(2, 2)), (3, None, pl.ds(3, 1)))
    rx_all = (
        (2, pl.ds(2, 2), pl.ds(0, 4)),
        (3, None, pl.ds(2, 2)),
        (1, pl.ds(0, 4), pl.ds(0, 4)),
        (-1, pl.ds(0, 4), pl.ds(0, 4)),
    )

    def st_act(cases, act):
        shift_copies(st, st_send, st_recv, cases, act)

    def rx_act(act):
        shift_copies(rx, rx_send, rx_recv, rx_all, act)

    gather_zonal(0)
    pl.semaphore_wait(barrier, len(NEAR) + (1 if share else 0))
    if share:
        z_copy(0).start()
    load_bot.wait()
    load_surf.wait()
    for c in range(2):
        d = bot[col(c), :].astype(jnp.float32)
        st[0, 2 + c] = d
        for v in range(2):
            st[0, (4, 0)[c] + v] = jnp.where(d > 0, surf[v, col(c), :], 0.0)
    st_act(st_near, "start")
    gather_chunk(0)
    send_chunk(0)
    gather_zonal(1)
    for which in range(1 if share else 0, 2):
        z_copy(which).start()
    rounds = spread_rounds(n)

    def spread(i):
        if i < len(rounds):
            for s in (rounds[i], -rounds[i]):
                pl.semaphore_signal(
                    met.at[i], inc=1, device_id=lon_peer(s), device_id_type=MESH
                )

    def spread_wait(i):
        if i < len(rounds):
            pl.semaphore_wait(met.at[i], 2)

    spread(0)
    for g in range(1, count):
        gather_chunk(g)
        send_chunk(g)

    spread_wait(0)
    spread(1)
    st_act(st_near, "wait_recv")

    depths = {-2: st[1, 2], -1: st[1, 3], 0: st[0, 2], 1: st[0, 3], 2: st[4, 2], 3: st[4, 3]}

    def y_face(i):
        wall = jnp.logical_and(last_lane, row == 7)
        return jnp.where(wall, 0.0, jnp.minimum(depths[i], north(depths[i])))

    def x_face(i):
        return jnp.minimum(depths[i], depths[i + 1])

    for which in range(2):
        z_copy(which).wait_recv()
    if share:
        z_copy(2).start()
        z_copy(2).wait_recv()
    quarter = TIME_STEP * 0.25
    diff = TIME_STEP * DIFFUSIVITY
    faces_x = [x_face(f - 1) for f in range(3)]
    faces_y = [y_face(c) for c in range(2)]
    own_depth = [depths[c] for c in range(2)]

    for g, (k0, k1) in enumerate(chunks):
        load(1, g).wait()
        for side in range(2):
            t_copy(g, side).wait_recv()

        def first(k, carry):
            kf = k.astype(jnp.float32)
            z = (r_z[0, k], s_z[0, k], s_z[1, k], r_z[1, k])
            cx = []
            for f in range(3):
                open_f = kf < faces_x[f]
                u = quarter * (z[f] + z[f + 1])
                cx.append((jnp.where(open_f, u + diff, 0.0), jnp.where(open_f, u - diff, 0.0)))
            cy = []
            for c in range(2):
                open_f = kf < faces_y[c]
                m = mer[k, col(c), :]
                u = quarter * (m + north(m))
                cy.append((jnp.where(open_f, u + diff, 0.0), jnp.where(open_f, u - diff, 0.0)))
            for q, (lo, hi) in enumerate(cx + cy):
                coef[k, 2 * q] = lo
                coef[k, 2 * q + 1] = hi
            wet = [kf < own_depth[c] for c in range(2)]
            for v in range(2):
                t = (
                    r_t[0, k, v],
                    jnp.where(wet[0], s_t[0, k, v], 0.0),
                    jnp.where(wet[1], s_t[1, k, v], 0.0),
                    r_t[1, k, v],
                )
                fx = [cx[f][0] * t[f] + cx[f][1] * t[f + 1] for f in range(3)]
                for c in range(2):
                    fy = cy[c][0] * t[c + 1] + cy[c][1] * north(t[c + 1])
                    s_b[c, k, v] = t[c + 1] - ((fx[c + 1] - fx[c]) + (fy - south(fy)))
            return carry

        lax.fori_loop(k0, k1, first, 0, unroll=UNROLL)
        for side in range(2):
            b_copy(g, side).start()
    spread_wait(1)
    st_act(st_far, "start")
    spread(2)

    face_x = {i: SURFACE_COUPLING * x_face(i) for i in range(-2, 3)}
    face_y = {i: SURFACE_COUPLING * y_face(i) for i in range(-2, 3)}

    def lap(s, cols):
        gx = {i: face_x[i] * (s[i + 1] - s[i]) for i in range(cols[0] - 1, cols[-1] + 1)}
        res, rise = {}, {}
        for i in cols:
            rise[i] = north(s[i]) - s[i]
            gy = face_y[i] * rise[i]
            res[i] = -((gx[i] - gx[i - 1]) + (gy - south(gy)))
        return res, rise

    own = (0, 1)
    height = [
        {-2: st[1, 4 + v], -1: st[1, v], 0: st[0, 4 + v], 1: st[0, v], 2: st[4, 4 + v]}
        for v in range(2)
    ]
    lap_h = [lap(height[v], own)[0] for v in range(2)]

    zero = jnp.zeros(TILE, jnp.float32)
    totals = (zero,) * 7
    for g, (k0, k1) in enumerate(chunks):
        for side in range(2):
            b_copy(g, side).wait_recv()

        def second(k, carry):
            sums, grams = list(carry[:4]), list(carry[4:])
            cx = [(coef[k, 2 * f], coef[k, 2 * f + 1]) for f in range(3)]
            cy = [(coef[k, 6 + 2 * c], coef[k, 7 + 2 * c]) for c in range(2)]
            new = []
            for v in range(2):
                t = (r_b[0, k, v], s_b[0, k, v], s_b[1, k, v], r_b[1, k, v])
                fx = [cx[f][0] * t[f] + cx[f][1] * t[f + 1] for f in range(3)]
                for c in range(2):
                    fy = cy[c][0] * t[c + 1] + cy[c][1] * north(t[c + 1])
                    val = t[c + 1] - ((fx[c + 1] - fx[c]) + (fy - south(fy)))
                    out[v, k, col(c), :] = val
                    sums[2 * v + c] = sums[2 * v + c] + val
                    new.append(val)
            grams[0] = grams[0] + (new[0] * new[0] + new[1] * new[1])
            grams[1] = grams[1] + (new[0] * new[2] + new[1] * new[3])
            grams[2] = grams[2] + (new[2] * new[2] + new[3] * new[3])
            return tuple(sums + grams)

        totals = lax.fori_loop(k0, k1, second, totals, unroll=UNROLL)
        if g == (count - 1) // 2:
            for i in range(2, len(rounds)):
                spread_wait(i)
                spread(i + 1)

    gain = STERIC_GAIN / levels
    for v in range(2):
        for c in range(2):
            rx[0, 2 * c + v] = gain * totals[2 * v + c] - lap_h[v][c]
    rx_act("start")
    st_act(st_far, "wait_recv")
    depths.update({-5: st[3, 3], -4: st[2, 2], -3: st[2, 3]})
    for i in (-5, -4, -3):
        face_x[i] = SURFACE_COUPLING * x_face(i)
    for i in (-4, -3):
        face_y[i] = SURFACE_COUPLING * y_face(i)

    is_first, is_last = me == 0, me == n - 1

    def gathered(term):
        left = term(-2) + term(-1)
        return jnp.where(is_first, left, 0.0) + jnp.where(is_last, 0.0, term(0) + term(1))

    def dot(a, b):
        return gathered(lambda i: a[i] * b[i])

    parts = {}
    for q in range(3):
        parts["gram", q] = totals[4 + q]
    parts["hh", 0] = dot(height[0], height[0])
    parts["hh", 1] = dot(height[1], height[1])
    parts["hh", 2] = dot(height[0], height[1])
    rx_act("wait_recv")

    span = 4.0 * levels
    powers = []
    for v in range(2):
        r = {-5: rx[3, 2 + v]}
        for c in range(2):
            r.update({c - 4: rx[2, 2 * c + v], c - 2: rx[1, 2 * c + v]})
            r.update({c: rx[0, 2 * c + v], c + 2: rx[4, 2 * c + v]})
        l1, rise0 = lap(r, range(-4, 3))
        l2, rise1 = lap(l1, range(-3, 2))
        powers.append((r, l1, l2))
        rise2 = {i: north(l2[i]) - l2[i] for i in WINDOW}
        for i, centre in enumerate(CENTRES):
            shift = centre * span
            if i:
                b1 = {c: l1[c] - shift * r[c] for c in WINDOW}
                b2 = {c: (l2[c] - 2.0 * shift * l1[c]) + shift * shift * r[c] for c in range(-3, 2)}
                up = {
                    c: (rise2[c] - 2.0 * shift * rise1[c]) + shift * shift * rise0[c]
                    for c in WINDOW
                }
            else:
                b1, b2, up = l1, l2, rise2
                parts["m", v, i, 0] = dot(r, r)
            parts["m", v, i, 1] = dot(r, b1)
            parts["m", v, i, 2] = dot(b1, b1)
            parts["m", v, i, 3] = dot(b1, b2)
            parts["m", v, i, 4] = dot(b2, b2)

            def energy(c):
                across = b2[c] - b2[c - 1]
                return face_x[c - 1] * across * across + face_y[c] * up[c] * up[c]

            parts["m", v, i, 5] = gathered(energy)
    for v in range(2):
        for j in range(3):
            parts["h", v, v, j] = dot(height[v], powers[v][j])
            parts["h", v, 1 - v, j] = dot(height[v], powers[1 - v][j])
    for k in range(5):
        parts["c", k] = dot(powers[0][k // 2], powers[1][(k + 1) // 2])

    names = list(parts)
    level, shift = [parts[name] for name in names], 1
    while shift < 128:
        if len(level) == 1:
            level = [level[0] + pltpu.roll(level[0], shift, 1)]
        else:
            even = jnp.bitwise_and(lane, shift) == 0
            merged = []
            for i in range(0, len(level), 2):
                a, b = level[i], level[min(i + 1, len(level) - 1)]
                merged.append(jnp.where(even, a, b) + pltpu.roll(jnp.where(even, b, a), shift, 1))
            level = merged
        shift *= 2
    local = level[0]
    for shift in (4, 2, 1):
        local = local + pltpu.roll(local, shift, 0)
    red[me] = local[0:1]

    def red_copy(i):
        return pltpu.make_async_remote_copy(
            src_ref=red.at[me],
            dst_ref=red.at[me],
            send_sem=rd_send,
            recv_sem=rd_recv,
            device_id=lon_peer(i),
            device_id_type=MESH,
        )

    def every(sem):
        return pltpu.make_async_copy(red.at[pl.ds(0, n - 1)], red.at[pl.ds(0, n - 1)], sem)

    peers_loop(n, lambda i: red_copy(i).start())
    every(rd_recv).wait()
    terms = [red[i] for i in range(n)]
    while len(terms) > 1:
        terms = [
            terms[i] + terms[i + 1] if i + 1 < len(terms) else terms[i]
            for i in range(0, len(terms), 2)
        ]
    total = {
        name: jnp.broadcast_to(terms[0][:, q : q + 1], TILE) for q, name in enumerate(names)
    }

    coefs = []
    for v in range(2):
        m0 = total["m", v, 0, 0]
        m = [m0] + [total["m", v, 0, k] for k in range(1, 6)]
        first_moment = m[1]
        centre = zero
        for i in range(1, len(CENTRES)):
            limit = 0.5 * (CENTRES[i] + CENTRES[i - 1]) * span
            above = first_moment > limit * m0
            centre = jnp.where(above, CENTRES[i] * span, centre)
            m = [m0] + [jnp.where(above, total["m", v, i, k], m[k]) for k in range(1, 6)]
        unit = 1.0 + centre
        a = [unit * m[k] + m[k + 1] for k in range(4)] + [m[4] + m[5]]
        ratio = m[1] / m0
        step0 = m0 / a[0]
        rr1 = step0 * step0 * (m[2] - ratio * m[1])
        beta0 = rr1 / m0
        along = step0 * ratio + beta0
        p1ap1 = along * along * a[0] - 2.0 * along * step0 * a[1] + step0 * step0 * a[2]
        step1 = rr1 / p1ap1
        x0 = step0 * ratio - step1 * along * unit
        x1 = step1 * step0 * unit - (step0 + step1 * along)
        x2 = step1 * step0

        def form(y0, y1, y2, f):
            return (
                y0 * (y0 * f[0] + 2.0 * (y1 * f[1] + y2 * f[2]))
                + y1 * (y1 * f[2] + 2.0 * (y2 * f[3]))
                + y2 * (y2 * f[4])
            )

        rr2 = form(x0, x1, x2, m)
        beta1 = rr2 / rr1
        y0, y1, y2 = x0 + beta1 * along, x1 - beta1 * step0, x2
        step2 = rr2 / form(y0, y1, y2, a)
        e0 = step0 + step1 * along + step2 * y0
        e1 = step2 * y1 - step1 * step0
        e2 = step2 * y2
        coefs.append((e0 - centre * (e1 - centre * e2), e1 - 2.0 * centre * e2, e2))
        for c in own:
            w = coefs[v]
            s = powers[v][0][c] * w[0] + (powers[v][1][c] * w[1] + powers[v][2][c] * w[2])
            sout[v, col(c), :] = height[v][c] + s

    def plain(v, k):
        return total["m", v, 0, k]

    gram = []
    for v in range(2):
        w = coefs[v]
        s = total["hh", v] + 2.0 * sum(w[j] * total["h", v, v, j] for j in range(3))
        for i in range(3):
            for j in range(3):
                s = s + w[i] * w[j] * plain(v, i + j)
        gram.append(total["gram", 2 * v] + s)
    mix = total["gram", 1] + total["hh", 2]
    for j in range(3):
        mix = mix + (coefs[1][j] * total["h", 0, 1, j] + coefs[0][j] * total["h", 1, 0, j])
    for i in range(3):
        for j in range(3):
            mix = mix + coefs[0][i] * coefs[1][j] * total["c", i + j]
    cells = float((levels + 1) * 2 * 8 * 128 * n)
    gram_one, gram_two, gram_mix = gram[0] / cells, gram[1] / cells, mix / cells
    scale_one = jnp.sqrt(gram_one + EPSILON)
    cross = gram_mix / scale_one
    rest = gram_two - 2.0 * cross * cross + cross * cross * gram_one / (gram_one + EPSILON)
    scale_two = jnp.sqrt(rest + EPSILON)
    gout[0] = 1.0 / scale_one
    gout[1] = cross
    gout[2] = 1.0 / scale_two
    gout[3] = jnp.where(lane == 0, scale_one, jnp.where(lane == 1, cross, scale_two))

    for g in range(count):
        for side in range(2):
            t_copy(g, side).wait_send()
            b_copy(g, side).wait_send()
    for which in range(3 if share else 2):
        z_copy(which).wait_send()
    st_act(st_near + st_far, "wait_send")
    rx_act("wait_send")
    every(rd_send).wait()


def scale_kernel(trc, surf, tail, out_h, sout_h, gout_h, out, sout, gvec, sem):
    levels = trc.shape[1]
    chunks = chunk_bounds(levels)
    one, cross, two = tail[0], tail[1], tail[2]
    gvec[...] = tail[3, 0, :3]
    grow = pltpu.make_async_copy(gvec, gout_h, sem.at[len(chunks) + 1])
    grow.start()

    def store(g):
        k0, k1 = chunks[g]
        return pltpu.make_async_copy(
            out.at[:, pl.ds(k0, k1 - k0)], out_h.at[:, pl.ds(k0, k1 - k0)], sem.at[g]
        )

    for g, (k0, k1) in enumerate(chunks):

        def step(k, carry):
            for h in range(2):
                rows = pl.ds(8 * h, 8)
                unit = trc[0, k, rows, :] * one
                out[0, k, rows, :] = unit
                out[1, k, rows, :] = (trc[1, k, rows, :] - cross * unit) * two
            return carry

        lax.fori_loop(k0, k1, step, 0, unroll=UNROLL)
        store(g).start()
    for h in range(2):
        rows = pl.ds(8 * h, 8)
        unit = surf[0, rows, :] * one
        sout[0, rows, :] = unit
        sout[1, rows, :] = (surf[1, rows, :] - cross * unit) * two
    last = pltpu.make_async_copy(sout, sout_h, sem.at[len(chunks)])
    last.start()
    for g in range(len(chunks)):
        store(g).wait()
    last.wait()
    grow.wait()


def packed(x):
    lead, (cols, rows) = x.shape[:-2], x.shape[-2:]
    x = x.reshape(lead + (cols, rows // 128, 128))
    x = jnp.swapaxes(x, -3, -2)
    return x.reshape(lead + (cols * (rows // 128), 128))


def unpacked(x, cols):
    lead, (rows, lanes) = x.shape[:-2], x.shape[-2:]
    x = x.reshape(lead + (rows // cols, cols, lanes))
    x = jnp.swapaxes(x, -3, -2)
    return x.reshape(lead + (cols, rows // cols * lanes))


def on_device(n, groups, tracer_pert, surface_pert, zonal_flow, merid_flow, bottom_level):
    vectors, levels, columns, rows = tracer_pert.shape
    count = len(chunk_bounds(levels))
    share = shares_zonal(groups, levels)
    f32 = jnp.float32
    vmem = pl.BlockSpec(memory_space=pltpu.VMEM)
    hbm = pl.BlockSpec(memory_space=pltpu.HBM)
    dma = pltpu.SemaphoreType.DMA
    zonal_sems = 3 if share else 2
    tracer, surface, tail = pl.pallas_call(
        functools.partial(kernel, n, share),
        out_shape=(
            jax.ShapeDtypeStruct((vectors, levels, 16, 128), f32),
            jax.ShapeDtypeStruct((vectors, 16, 128), f32),
            jax.ShapeDtypeStruct((4, 8, 128), f32),
        ),
        in_specs=[hbm] * 5,
        out_specs=(vmem,) * 3,
        scratch_shapes=[
            pltpu.VMEM((vectors, levels, 16, 128), f32),
            pltpu.VMEM((vectors, 16, 128), f32),
            pltpu.VMEM((levels, 16, 128), f32),
            pltpu.VMEM((levels, 16, 128), f32),
            pltpu.VMEM((16, 128), jnp.int32),
            pltpu.VMEM((2, levels, 2, 8, 128), f32),
            pltpu.VMEM((2, levels, 2, 8, 128), f32),
            pltpu.VMEM((2, levels, 8, 128), f32),
            pltpu.VMEM((2, levels, 8, 128), f32),
            pltpu.VMEM((2, levels, 2, 8, 128), f32),
            pltpu.VMEM((2, levels, 2, 8, 128), f32),
            pltpu.VMEM((levels, 10, 8, 128), f32),
            pltpu.VMEM((len(SLOT), 6, 8, 128), f32),
            pltpu.VMEM((len(SLOT), 4, 8, 128), f32),
            pltpu.VMEM((n, 1, 128), f32),
            dma((4, max(2, count))),
            dma((2, count)),
            dma((2, count)),
            dma((zonal_sems,)),
            dma((zonal_sems,)),
            dma((2, count)),
            dma((2, count)),
            dma((len(SLOT),)),
            dma((len(SLOT),)),
            dma((len(SLOT),)),
            dma((len(SLOT),)),
            dma(()),
            dma(()),
            pltpu.SemaphoreType.REGULAR((max(1, len(spread_rounds(n))),)),
        ],
        compiler_params=pltpu.CompilerParams(
            collective_id=0, has_side_effects=True, vmem_limit_bytes=40 * 1024 * 1024
        ),
    )(
        *(
            pltpu.with_memory_space_constraint(packed(x), pltpu.HBM)
            for x in (tracer_pert, surface_pert, zonal_flow, merid_flow, bottom_level)
        )
    )
    tracer, surface, growth = pl.pallas_call(
        scale_kernel,
        out_shape=(
            jax.ShapeDtypeStruct((vectors, levels, 16, 128), f32),
            jax.ShapeDtypeStruct((vectors, 16, 128), f32),
            jax.ShapeDtypeStruct((3,), f32),
        ),
        in_specs=[vmem] * 3,
        out_specs=(hbm,) * 3,
        scratch_shapes=[
            pltpu.VMEM((vectors, levels, 16, 128), f32),
            pltpu.VMEM((vectors, 16, 128), f32),
            pltpu.VMEM((3,), f32),
            dma((count + 2,)),
        ],
        compiler_params=pltpu.CompilerParams(vmem_limit_bytes=16 * 1024 * 1024),
    )(tracer, surface, tail)
    return unpacked(tracer, columns), unpacked(surface, columns), growth


def solution(mesh):
    placed = (
        P("grp", None, "lon", None),
        P("grp", "lon", None),
        P(None, "lon", None),
        P(None, "lon", None),
        P("lon", None),
    )
    return jax.shard_map(
        functools.partial(on_device, mesh.shape["lon"], mesh.shape["grp"]),
        mesh=mesh,
        in_specs=placed,
        out_specs=(P("grp", None, "lon", None), P("grp", "lon", None), P("grp")),
        check_vma=False,
    )
```

```python
import functools

import jax
import jax.numpy as jnp
from jax import lax
from jax.experimental import pallas as pl
from jax.experimental.pallas import tpu as pltpu
from jax.sharding import PartitionSpec as P

DIFFUSIVITY = 0.5
TIME_STEP = 0.2
SURFACE_COUPLING = 0.5
STERIC_GAIN = 2.0
EPSILON = 1e-06
MESH = pl.DeviceIdType.MESH
CHUNKS = 5
UNROLL = 5
NEAR = (1, -1)
SLOT = {0: 0, 1: 1, 2: 2, 3: 3, -1: 4}
WINDOW = (-2, -1, 0, 1)
CENTRES = (0.0, 0.04, 0.16, 0.64)
TILE = (8, 128)


def chunk_bounds(levels):
    count = min(CHUNKS, levels)
    edges = [levels * i // count for i in range(count + 1)]
    return list(zip(edges[:-1], edges[1:]))


def spread_rounds(n):
    reach, rounds = 1, []
    while 2 * reach < n:
        rounds.append(reach)
        reach *= 2
    return rounds


def shares_zonal(groups, levels):
    return groups == 2 and levels % 2 == 0


def peers_loop(n, body):
    if n <= 16:
        for i in range(1, n):
            body(i)
    else:

        def step(i, carry):
            body(i)
            return carry

        lax.fori_loop(1, n, step, 0)


def kernel(
    n, share, trc_h, surf_h, zon_h, mer_h, bot_h, out, sout, gout,
    trc, surf, zon, mer, bot, s_t, r_t, s_z, r_z, s_b, r_b, coef, st, rx, red, flat,
    in_sem, t_send, t_recv, z_send, z_recv, b_send, b_recv,
    st_send, st_recv, rx_send, rx_recv, rd_send, rd_recv, met,
):
    me = lax.axis_index("lon")
    grp = lax.axis_index("grp")
    levels = zon.shape[0]
    chunks = chunk_bounds(levels)
    side_dev = (lax.rem(me + n - 1, n), lax.rem(me + 1, n))
    outer = lax.rem(me, 2)
    inner = 1 - outer
    lane = lax.broadcasted_iota(jnp.int32, TILE, 1)
    row = lax.broadcasted_iota(jnp.int32, TILE, 0)
    last_lane, first_lane = lane == 127, lane == 0

    def north(x):
        rolled = pltpu.roll(x, 127, 1)
        return jnp.where(last_lane, pltpu.roll(rolled, 7, 0), rolled)

    def south(x):
        rolled = pltpu.roll(x, 1, 1)
        return jnp.where(first_lane, pltpu.roll(rolled, 1, 0), rolled)

    def col(c):
        return pl.ds(c, 8, stride=2)

    def lon_peer(s):
        return {"lon": lax.rem(me + s + n, n)}

    barrier = pltpu.get_barrier_semaphore()
    for s in NEAR:
        pl.semaphore_signal(barrier, inc=1, device_id=lon_peer(s), device_id_type=MESH)
    if share:
        pl.semaphore_signal(barrier, inc=1, device_id={"grp": 1 - grp}, device_id_type=MESH)

    half = levels // 2
    mine = pl.ds(grp * half if share else 0, half)
    theirs = pl.ds((1 - grp) * half, half) if share else pl.ds(half, levels - half)

    def load(which, g):
        k0, k1 = chunks[g]
        ks = pl.ds(k0, k1 - k0)
        src, dst = ((trc_h.at[:, ks], trc.at[:, ks]), (mer_h.at[ks], mer.at[ks]))[which]
        return pltpu.make_async_copy(src, dst, in_sem.at[which, g])

    count = len(chunks)
    load_zon = [
        pltpu.make_async_copy(zon_h.at[ks], zon.at[ks], in_sem.at[2, i])
        for i, ks in enumerate((mine, theirs))
    ]
    load_bot = pltpu.make_async_copy(bot_h, bot, in_sem.at[3, 0])
    load_surf = pltpu.make_async_copy(surf_h, surf, in_sem.at[3, 1])
    load_zon[0].start()
    load_bot.start()
    load_surf.start()
    load(0, 0).start()
    load_zon[1].start()
    for g in range(1, count):
        load(0, g).start()
    for g in range(count):
        load(1, g).start()
    def gather_chunk(g):
        load(0, g).wait()

        def step(k, carry):
            for c in range(2):
                s_t[c, k, 0] = trc[0, k, col(c), :]
                s_t[c, k, 1] = trc[1, k, col(c), :]
            return carry

        lax.fori_loop(*chunks[g], step, 0, unroll=UNROLL)

    def side_copy(src, dst, send, recv, g, side):
        k0, k1 = chunks[g]
        return pltpu.make_async_remote_copy(
            src_ref=src.at[side, pl.ds(k0, k1 - k0)],
            dst_ref=dst.at[1 - side, pl.ds(k0, k1 - k0)],
            send_sem=send.at[side, g],
            recv_sem=recv.at[1 - side, g],
            device_id={"lon": side_dev[side]},
            device_id_type=MESH,
        )

    def t_copy(g, side):
        return side_copy(s_t, r_t, t_send, t_recv, g, side)

    def b_copy(g, side):
        return side_copy(s_b, r_b, b_send, b_recv, g, side)

    def gather_zonal(i):
        load_zon[i].wait()
        ks = (mine, theirs)[i]

        def step(k, carry):
            for c in range(2):
                s_z[c, ks.start + k] = zon[ks.start + k, col(c), :]
            return carry

        lax.fori_loop(0, ks.size, step, 0, unroll=UNROLL)

    def z_copy(which):
        if not share:
            return pltpu.make_async_remote_copy(
                src_ref=s_z.at[which],
                dst_ref=r_z.at[1 - which],
                send_sem=z_send.at[which],
                recv_sem=z_recv.at[which],
                device_id={"lon": side_dev[which]},
                device_id_type=MESH,
            )
        src, dst, dev = (
            (s_z.at[outer, mine], r_z.at[1 - outer, mine], lon_peer(2 * outer - 1)),
            (s_z.at[inner], r_z.at[1 - inner], lon_peer(2 * inner - 1)),
            (r_z.at[outer, mine], r_z.at[outer, mine], {"grp": 1 - grp}),
        )[which]
        return pltpu.make_async_remote_copy(
            src_ref=src,
            dst_ref=dst,
            send_sem=z_send.at[which],
            recv_sem=z_recv.at[which],
            device_id=dev,
            device_id_type=MESH,
        )

    def send_chunk(g):
        for side in range(2):
            t_copy(g, side).start()

    def shift_copy(buf, send, recv, s, part):
        return pltpu.make_async_remote_copy(
            src_ref=buf.at[0, part],
            dst_ref=buf.at[SLOT[s], part],
            send_sem=send.at[SLOT[s]],
            recv_sem=recv.at[SLOT[s]],
            device_id=lon_peer(s),
            device_id_type=MESH,
        )

    def shift_copies(buf, send, recv, cases, act):
        for s, usual, closing in cases:
            closes = me == (0 if act == "wait_recv" else n - s)
            if usual == closing:
                getattr(shift_copy(buf, send, recv, s, usual), act)()
                continue
            if usual is not None:

                @pl.when(jnp.logical_not(closes))
                def _():
                    getattr(shift_copy(buf, send, recv, s, usual), act)()

            @pl.when(closes)
            def _():
                getattr(shift_copy(buf, send, recv, s, closing), act)()

    st_near = ((1, pl.ds(0, 4), pl.ds(0, 6)), (-1, pl.ds(2, 4), pl.ds(2, 4)))
    st_far = ((2, pl.ds(3, 1), pl.ds(2, 2)), (3, None, pl.ds(3, 1)))
    rx_all = (
        (2, pl.ds(2, 2), pl.ds(0, 4)),
        (3, None, pl.ds(2, 2)),
        (1, pl.ds(0, 4), pl.ds(0, 4)),
        (-1, pl.ds(0, 4), pl.ds(0, 4)),
    )

    def st_act(cases, act):
        shift_copies(st, st_send, st_recv, cases, act)

    def rx_act(act):
        shift_copies(rx, rx_send, rx_recv, rx_all, act)

    gather_zonal(0)
    pl.semaphore_wait(barrier, len(NEAR) + (1 if share else 0))
    if share:
        z_copy(0).start()
    load_bot.wait()
    load_surf.wait()
    for c in range(2):
        d = bot[col(c), :].astype(jnp.float32)
        st[0, 2 + c] = d
        for v in range(2):
            st[0, (4, 0)[c] + v] = jnp.where(d > 0, surf[v, col(c), :], 0.0)
    st_act(st_near, "start")
    gather_chunk(0)
    send_chunk(0)
    gather_zonal(1)
    for which in range(1 if share else 0, 2):
        z_copy(which).start()
    rounds = spread_rounds(n)

    def spread(i):
        if i < len(rounds):
            for s in (rounds[i], -rounds[i]):
                pl.semaphore_signal(
                    met.at[i], inc=1, device_id=lon_peer(s), device_id_type=MESH
                )

    def spread_wait(i):
        if i < len(rounds):
            pl.semaphore_wait(met.at[i], 2)

    spread(0)
    for g in range(1, count):
        gather_chunk(g)
        send_chunk(g)

    spread_wait(0)
    spread(1)
    st_act(st_near, "wait_recv")

    depths = {-2: st[1, 2], -1: st[1, 3], 0: st[0, 2], 1: st[0, 3], 2: st[4, 2], 3: st[4, 3]}

    def y_face(i):
        wall = jnp.logical_and(last_lane, row == 7)
        return jnp.where(wall, 0.0, jnp.minimum(depths[i], north(depths[i])))

    def x_face(i):
        return jnp.minimum(depths[i], depths[i + 1])

    for which in range(2):
        z_copy(which).wait_recv()
    if share:
        z_copy(2).start()
        z_copy(2).wait_recv()
    quarter = TIME_STEP * 0.25
    diff = TIME_STEP * DIFFUSIVITY
    faces_x = [x_face(f - 1) for f in range(3)]
    faces_y = [y_face(c) for c in range(2)]
    own_depth = [depths[c] for c in range(2)]

    for g, (k0, k1) in enumerate(chunks):
        load(1, g).wait()
        for side in range(2):
            t_copy(g, side).wait_recv()

        def first(k, carry):
            kf = k.astype(jnp.float32)
            z = (r_z[0, k], s_z[0, k], s_z[1, k], r_z[1, k])
            cx = []
            for f in range(3):
                open_f = kf < faces_x[f]
                u = quarter * (z[f] + z[f + 1])
                cx.append((jnp.where(open_f, u + diff, 0.0), jnp.where(open_f, u - diff, 0.0)))
            cy = []
            for c in range(2):
                open_f = kf < faces_y[c]
                m = mer[k, col(c), :]
                u = quarter * (m + north(m))
                cy.append((jnp.where(open_f, u + diff, 0.0), jnp.where(open_f, u - diff, 0.0)))
            for q, (lo, hi) in enumerate(cx + cy):
                coef[k, 2 * q] = lo
                coef[k, 2 * q + 1] = hi
            wet = [kf < own_depth[c] for c in range(2)]
            for v in range(2):
                t = (
                    r_t[0, k, v],
                    jnp.where(wet[0], s_t[0, k, v], 0.0),
                    jnp.where(wet[1], s_t[1, k, v], 0.0),
                    r_t[1, k, v],
                )
                fx = [cx[f][0] * t[f] + cx[f][1] * t[f + 1] for f in range(3)]
                for c in range(2):
                    fy = cy[c][0] * t[c + 1] + cy[c][1] * north(t[c + 1])
                    s_b[c, k, v] = t[c + 1] - ((fx[c + 1] - fx[c]) + (fy - south(fy)))
            return carry

        lax.fori_loop(k0, k1, first, 0, unroll=UNROLL)
        for side in range(2):
            b_copy(g, side).start()
    spread_wait(1)
    st_act(st_far, "start")
    spread(2)

    face_x = {i: SURFACE_COUPLING * x_face(i) for i in range(-2, 3)}
    face_y = {i: SURFACE_COUPLING * y_face(i) for i in range(-2, 3)}
    face_s = {i: south(face_y[i]) for i in face_y}

    def lap(s, cols):
        gx = {i: face_x[i] * (s[i + 1] - s[i]) for i in range(cols[0] - 1, cols[-1] + 1)}
        res, rise = {}, {}
        for i in cols:
            rise[i] = north(s[i]) - s[i]
            fall = s[i] - south(s[i])
            res[i] = (gx[i - 1] - gx[i]) + (face_s[i] * fall - face_y[i] * rise[i])
        return res, rise

    own = (0, 1)
    height = [
        {-2: st[1, 4 + v], -1: st[1, v], 0: st[0, 4 + v], 1: st[0, v], 2: st[4, 4 + v]}
        for v in range(2)
    ]
    lap_h = [lap(height[v], own)[0] for v in range(2)]

    zero = jnp.zeros(TILE, jnp.float32)
    totals = (zero,) * 7
    for g, (k0, k1) in enumerate(chunks):
        for side in range(2):
            b_copy(g, side).wait_recv()

        def second(k, carry):
            sums, grams = list(carry[:4]), list(carry[4:])
            cx = [(coef[k, 2 * f], coef[k, 2 * f + 1]) for f in range(3)]
            cy = [(coef[k, 6 + 2 * c], coef[k, 7 + 2 * c]) for c in range(2)]
            new = []
            for v in range(2):
                t = (r_b[0, k, v], s_b[0, k, v], s_b[1, k, v], r_b[1, k, v])
                fx = [cx[f][0] * t[f] + cx[f][1] * t[f + 1] for f in range(3)]
                for c in range(2):
                    fy = cy[c][0] * t[c + 1] + cy[c][1] * north(t[c + 1])
                    val = t[c + 1] - ((fx[c + 1] - fx[c]) + (fy - south(fy)))
                    out[v, k, col(c), :] = val
                    sums[2 * v + c] = sums[2 * v + c] + val
                    new.append(val)
            grams[0] = grams[0] + (new[0] * new[0] + new[1] * new[1])
            grams[1] = grams[1] + (new[0] * new[2] + new[1] * new[3])
            grams[2] = grams[2] + (new[2] * new[2] + new[3] * new[3])
            return tuple(sums + grams)

        totals = lax.fori_loop(k0, k1, second, totals, unroll=UNROLL)
        if g == (count - 1) // 2:
            for i in range(2, len(rounds)):
                spread_wait(i)
                spread(i + 1)

    gain = STERIC_GAIN / levels
    for v in range(2):
        for c in range(2):
            rx[0, 2 * c + v] = gain * totals[2 * v + c] - lap_h[v][c]
    rx_act("start")
    st_act(st_far, "wait_recv")
    depths.update({-5: st[3, 3], -4: st[2, 2], -3: st[2, 3]})
    for i in (-5, -4, -3):
        face_x[i] = SURFACE_COUPLING * x_face(i)
    for i in (-4, -3):
        face_y[i] = SURFACE_COUPLING * y_face(i)
        face_s[i] = south(face_y[i])

    is_first, is_last = me == 0, me == n - 1

    def gathered(term):
        left = term(-2) + term(-1)
        return jnp.where(is_first, left, 0.0) + jnp.where(is_last, 0.0, term(0) + term(1))

    def dot(a, b):
        return gathered(lambda i: a[i] * b[i])

    parts = {}
    for q in range(3):
        parts["gram", q] = totals[4 + q]
    parts["hh", 0] = dot(height[0], height[0])
    parts["hh", 1] = dot(height[1], height[1])
    parts["hh", 2] = dot(height[0], height[1])
    rx_act("wait_recv")

    span = 4.0 * levels
    powers = []
    for v in range(2):
        r = {-5: rx[3, 2 + v]}
        for c in range(2):
            r.update({c - 4: rx[2, 2 * c + v], c - 2: rx[1, 2 * c + v]})
            r.update({c: rx[0, 2 * c + v], c + 2: rx[4, 2 * c + v]})
        l1, rise0 = lap(r, range(-4, 3))
        l2, rise1 = lap(l1, range(-3, 2))
        powers.append((r, l1, l2))
        rise2 = {i: north(l2[i]) - l2[i] for i in WINDOW}
        for i, centre in enumerate(CENTRES):
            shift = centre * span
            if i:
                b1 = {c: l1[c] - shift * r[c] for c in WINDOW}
                b2 = {c: (l2[c] - 2.0 * shift * l1[c]) + shift * shift * r[c] for c in range(-3, 2)}
                up = {
                    c: (rise2[c] - 2.0 * shift * rise1[c]) + shift * shift * rise0[c]
                    for c in WINDOW
                }
            else:
                b1, b2, up = l1, l2, rise2
                parts["m", v, i, 0] = dot(r, r)
            parts["m", v, i, 1] = dot(r, b1)
            parts["m", v, i, 2] = dot(b1, b1)
            parts["m", v, i, 3] = dot(b1, b2)
            parts["m", v, i, 4] = dot(b2, b2)

            def energy(c):
                across = b2[c] - b2[c - 1]
                return face_x[c - 1] * across * across + face_y[c] * up[c] * up[c]

            parts["m", v, i, 5] = gathered(energy)
    for v in range(2):
        for j in range(3):
            parts["h", v, v, j] = dot(height[v], powers[v][j])
            parts["h", v, 1 - v, j] = dot(height[v], powers[1 - v][j])
    for k in range(5):
        parts["c", k] = dot(powers[0][k // 2], powers[1][(k + 1) // 2])

    names = list(parts)
    place = lane - 16 * row
    local = zero
    for q in range(0, len(names), 8):
        level = [parts[name] for name in names[q : q + 8]]
        for shift in (1, 2, 4):
            even = jnp.bitwise_and(row, shift) == 0
            merged = []
            for i in range(0, len(level), 2):
                a, b = level[i], level[min(i + 1, len(level) - 1)]
                merged.append(jnp.where(even, a, b) + pltpu.roll(jnp.where(even, b, a), shift, 0))
            level = merged
        local = jnp.where(place == q // 8, jnp.sum(level[0], axis=1, keepdims=True), local)
    for shift in (4, 2, 1):
        local = local + pltpu.roll(local, shift, 0)
    red[me] = local[0:1]

    def red_copy(i):
        return pltpu.make_async_remote_copy(
            src_ref=red.at[me],
            dst_ref=red.at[me],
            send_sem=rd_send,
            recv_sem=rd_recv,
            device_id=lon_peer(i),
            device_id_type=MESH,
        )

    def every(sem):
        return pltpu.make_async_copy(red.at[pl.ds(0, n - 1)], red.at[pl.ds(0, n - 1)], sem)

    peers_loop(n, lambda i: red_copy(i).start())
    every(rd_recv).wait()
    terms = [red[i] for i in range(n)]
    while len(terms) > 1:
        terms = [
            terms[i] + terms[i + 1] if i + 1 < len(terms) else terms[i]
            for i in range(0, len(terms), 2)
        ]
    every_row = jnp.broadcast_to(terms[0], TILE)
    for q in range(-(-len(names) // 8)):
        picked = jnp.where(place == q, every_row, 0.0)
        flat[q] = jnp.broadcast_to(jnp.sum(picked, axis=1, keepdims=True), TILE)
    total = {
        name: jnp.broadcast_to(flat[q // 8, q % 8 : q % 8 + 1], TILE)
        for q, name in enumerate(names)
    }

    coefs = []
    for v in range(2):
        m0 = total["m", v, 0, 0]
        m = [m0] + [total["m", v, 0, k] for k in range(1, 6)]
        first_moment = m[1]
        centre = zero
        for i in range(1, len(CENTRES)):
            limit = 0.5 * (CENTRES[i] + CENTRES[i - 1]) * span
            above = first_moment > limit * m0
            centre = jnp.where(above, CENTRES[i] * span, centre)
            m = [m0] + [jnp.where(above, total["m", v, i, k], m[k]) for k in range(1, 6)]
        unit = 1.0 + centre
        a = [unit * m[k] + m[k + 1] for k in range(4)] + [m[4] + m[5]]
        ratio = m[1] / m0
        step0 = m0 / a[0]
        rr1 = step0 * step0 * (m[2] - ratio * m[1])
        beta0 = rr1 / m0
        along = step0 * ratio + beta0
        p1ap1 = along * along * a[0] - 2.0 * along * step0 * a[1] + step0 * step0 * a[2]
        step1 = rr1 / p1ap1
        x0 = step0 * ratio - step1 * along * unit
        x1 = step1 * step0 * unit - (step0 + step1 * along)
        x2 = step1 * step0

        def form(y0, y1, y2, f):
            return (
                y0 * (y0 * f[0] + 2.0 * (y1 * f[1] + y2 * f[2]))
                + y1 * (y1 * f[2] + 2.0 * (y2 * f[3]))
                + y2 * (y2 * f[4])
            )

        rr2 = form(x0, x1, x2, m)
        beta1 = rr2 / rr1
        y0, y1, y2 = x0 + beta1 * along, x1 - beta1 * step0, x2
        step2 = rr2 / form(y0, y1, y2, a)
        e0 = step0 + step1 * along + step2 * y0
        e1 = step2 * y1 - step1 * step0
        e2 = step2 * y2
        coefs.append((e0 - centre * (e1 - centre * e2), e1 - 2.0 * centre * e2, e2))
        for c in own:
            w = coefs[v]
            s = powers[v][0][c] * w[0] + (powers[v][1][c] * w[1] + powers[v][2][c] * w[2])
            sout[v, col(c), :] = height[v][c] + s

    def plain(v, k):
        return total["m", v, 0, k]

    gram = []
    for v in range(2):
        w = coefs[v]
        s = total["hh", v] + 2.0 * sum(w[j] * total["h", v, v, j] for j in range(3))
        for i in range(3):
            for j in range(3):
                s = s + w[i] * w[j] * plain(v, i + j)
        gram.append(total["gram", 2 * v] + s)
    mix = total["gram", 1] + total["hh", 2]
    for j in range(3):
        mix = mix + (coefs[1][j] * total["h", 0, 1, j] + coefs[0][j] * total["h", 1, 0, j])
    for i in range(3):
        for j in range(3):
            mix = mix + coefs[0][i] * coefs[1][j] * total["c", i + j]
    cells = float((levels + 1) * 2 * 8 * 128 * n)
    gram_one, gram_two, gram_mix = gram[0] / cells, gram[1] / cells, mix / cells
    scale_one = jnp.sqrt(gram_one + EPSILON)
    cross = gram_mix / scale_one
    rest = gram_two - 2.0 * cross * cross + cross * cross * gram_one / (gram_one + EPSILON)
    scale_two = jnp.sqrt(rest + EPSILON)
    gout[0] = 1.0 / scale_one
    gout[1] = cross
    gout[2] = 1.0 / scale_two
    gout[3] = jnp.where(lane == 0, scale_one, jnp.where(lane == 1, cross, scale_two))

    for g in range(count):
        for side in range(2):
            t_copy(g, side).wait_send()
            b_copy(g, side).wait_send()
    for which in range(3 if share else 2):
        z_copy(which).wait_send()
    st_act(st_near + st_far, "wait_send")
    rx_act("wait_send")
    every(rd_send).wait()


def scale_kernel(trc, surf, tail, out_h, sout_h, gout_h, out, sout, gvec, sem):
    levels = trc.shape[1]
    chunks = chunk_bounds(levels)
    one, cross, two = tail[0], tail[1], tail[2]
    gvec[...] = tail[3, 0, :3]
    grow = pltpu.make_async_copy(gvec, gout_h, sem.at[len(chunks) + 1])
    grow.start()

    def store(g):
        k0, k1 = chunks[g]
        return pltpu.make_async_copy(
            out.at[:, pl.ds(k0, k1 - k0)], out_h.at[:, pl.ds(k0, k1 - k0)], sem.at[g]
        )

    for g, (k0, k1) in enumerate(chunks):

        def step(k, carry):
            for h in range(2):
                rows = pl.ds(8 * h, 8)
                unit = trc[0, k, rows, :] * one
                out[0, k, rows, :] = unit
                out[1, k, rows, :] = (trc[1, k, rows, :] - cross * unit) * two
            return carry

        lax.fori_loop(k0, k1, step, 0, unroll=UNROLL)
        store(g).start()
    for h in range(2):
        rows = pl.ds(8 * h, 8)
        unit = surf[0, rows, :] * one
        sout[0, rows, :] = unit
        sout[1, rows, :] = (surf[1, rows, :] - cross * unit) * two
    last = pltpu.make_async_copy(sout, sout_h, sem.at[len(chunks)])
    last.start()
    for g in range(len(chunks)):
        store(g).wait()
    last.wait()
    grow.wait()


def packed(x):
    lead, (cols, rows) = x.shape[:-2], x.shape[-2:]
    x = x.reshape(lead + (cols, rows // 128, 128))
    x = jnp.swapaxes(x, -3, -2)
    return x.reshape(lead + (cols * (rows // 128), 128))


def unpacked(x, cols):
    lead, (rows, lanes) = x.shape[:-2], x.shape[-2:]
    x = x.reshape(lead + (rows // cols, cols, lanes))
    x = jnp.swapaxes(x, -3, -2)
    return x.reshape(lead + (cols, rows // cols * lanes))


def on_device(n, groups, tracer_pert, surface_pert, zonal_flow, merid_flow, bottom_level):
    vectors, levels, columns, rows = tracer_pert.shape
    count = len(chunk_bounds(levels))
    share = shares_zonal(groups, levels)
    f32 = jnp.float32
    vmem = pl.BlockSpec(memory_space=pltpu.VMEM)
    hbm = pl.BlockSpec(memory_space=pltpu.HBM)
    dma = pltpu.SemaphoreType.DMA
    zonal_sems = 3 if share else 2
    tracer, surface, tail = pl.pallas_call(
        functools.partial(kernel, n, share),
        out_shape=(
            jax.ShapeDtypeStruct((vectors, levels, 16, 128), f32),
            jax.ShapeDtypeStruct((vectors, 16, 128), f32),
            jax.ShapeDtypeStruct((4, 8, 128), f32),
        ),
        in_specs=[hbm] * 5,
        out_specs=(vmem,) * 3,
        scratch_shapes=[
            pltpu.VMEM((vectors, levels, 16, 128), f32),
            pltpu.VMEM((vectors, 16, 128), f32),
            pltpu.VMEM((levels, 16, 128), f32),
            pltpu.VMEM((levels, 16, 128), f32),
            pltpu.VMEM((16, 128), jnp.int32),
            pltpu.VMEM((2, levels, 2, 8, 128), f32),
            pltpu.VMEM((2, levels, 2, 8, 128), f32),
            pltpu.VMEM((2, levels, 8, 128), f32),
            pltpu.VMEM((2, levels, 8, 128), f32),
            pltpu.VMEM((2, levels, 2, 8, 128), f32),
            pltpu.VMEM((2, levels, 2, 8, 128), f32),
            pltpu.VMEM((levels, 10, 8, 128), f32),
            pltpu.VMEM((len(SLOT), 6, 8, 128), f32),
            pltpu.VMEM((len(SLOT), 4, 8, 128), f32),
            pltpu.VMEM((n, 1, 128), f32),
            pltpu.VMEM((16, 8, 128), f32),
            dma((4, max(2, count))),
            dma((2, count)),
            dma((2, count)),
            dma((zonal_sems,)),
            dma((zonal_sems,)),
            dma((2, count)),
            dma((2, count)),
            dma((len(SLOT),)),
            dma((len(SLOT),)),
            dma((len(SLOT),)),
            dma((len(SLOT),)),
            dma(()),
            dma(()),
            pltpu.SemaphoreType.REGULAR((max(1, len(spread_rounds(n))),)),
        ],
        compiler_params=pltpu.CompilerParams(
            collective_id=0, has_side_effects=True, vmem_limit_bytes=40 * 1024 * 1024
        ),
    )(
        *(
            pltpu.with_memory_space_constraint(packed(x), pltpu.HBM)
            for x in (tracer_pert, surface_pert, zonal_flow, merid_flow, bottom_level)
        )
    )
    tracer, surface, growth = pl.pallas_call(
        scale_kernel,
        out_shape=(
            jax.ShapeDtypeStruct((vectors, levels, 16, 128), f32),
            jax.ShapeDtypeStruct((vectors, 16, 128), f32),
            jax.ShapeDtypeStruct((3,), f32),
        ),
        in_specs=[vmem] * 3,
        out_specs=(hbm,) * 3,
        scratch_shapes=[
            pltpu.VMEM((vectors, levels, 16, 128), f32),
            pltpu.VMEM((vectors, 16, 128), f32),
            pltpu.VMEM((3,), f32),
            dma((count + 2,)),
        ],
        compiler_params=pltpu.CompilerParams(vmem_limit_bytes=16 * 1024 * 1024),
    )(tracer, surface, tail)
    return unpacked(tracer, columns), unpacked(surface, columns), growth


def solution(mesh):
    placed = (
        P("grp", None, "lon", None),
        P("grp", "lon", None),
        P(None, "lon", None),
        P(None, "lon", None),
        P("lon", None),
    )
    return jax.shard_map(
        functools.partial(on_device, mesh.shape["lon"], mesh.shape["grp"]),
        mesh=mesh,
        in_specs=placed,
        out_specs=(P("grp", None, "lon", None), P("grp", "lon", None), P("grp")),
        check_vma=False,
    )
```

```python
import functools

import jax
import jax.numpy as jnp
from jax import lax
from jax.experimental import pallas as pl
from jax.experimental.pallas import tpu as pltpu
from jax.sharding import PartitionSpec as P

DIFFUSIVITY = 0.5
TIME_STEP = 0.2
SURFACE_COUPLING = 0.5
STERIC_GAIN = 2.0
EPSILON = 1e-06
MESH = pl.DeviceIdType.MESH
CHUNKS = 5
UNROLL = 5
NEAR = (1, -1)
CENTRES = (0.0, 0.04, 0.16, 0.64)
FAR = 4
SLOT = {0: 0, **{s: s for s in range(1, FAR + 3)}, -1: FAR + 3}
OWN = (0, 1)
MOMENTS = (
    [("m", v, i, k) for v in range(2) for i in range(len(CENTRES)) for k in range(1 if i else 0, 6)]
    + [("h", v, w, j) for v in range(2) for w in range(2) for j in range(3)]
    + [("c", k) for k in range(5)]
)
TILE = (8, 128)


def chunk_bounds(levels):
    count = min(CHUNKS, levels)
    edges = [levels * i // count for i in range(count + 1)]
    return list(zip(edges[:-1], edges[1:]))


def spread_rounds(n):
    reach, rounds = 1, []
    while 2 * reach < n:
        rounds.append(reach)
        reach *= 2
    return rounds


def shares_zonal(groups, levels):
    return groups == 2 and levels % 2 == 0


def peers_loop(n, body):
    if n <= 16:
        for i in range(1, n):
            body(i)
    else:

        def step(i, carry):
            body(i)
            return carry

        lax.fori_loop(1, n, step, 0)


def kernel(
    n, share, trc_h, surf_h, zon_h, mer_h, bot_h, out, sout, gout,
    trc, surf, zon, mer, bot, s_t, r_t, s_z, r_z, s_b, r_b, coef, st, rx, red, flat, mo, pw,
    in_sem, t_send, t_recv, z_send, z_recv, b_send, b_recv,
    st_send, st_recv, rx_send, rx_recv, rd_send, rd_recv, met,
):
    me = lax.axis_index("lon")
    grp = lax.axis_index("grp")
    levels = zon.shape[0]
    chunks = chunk_bounds(levels)
    side_dev = (lax.rem(me + n - 1, n), lax.rem(me + 1, n))
    outer = lax.rem(me, 2)
    inner = 1 - outer
    lane = lax.broadcasted_iota(jnp.int32, TILE, 1)
    row = lax.broadcasted_iota(jnp.int32, TILE, 0)
    last_lane, first_lane = lane == 127, lane == 0

    def north(x):
        rolled = pltpu.roll(x, 127, 1)
        return jnp.where(last_lane, pltpu.roll(rolled, 7, 0), rolled)

    def south(x):
        rolled = pltpu.roll(x, 1, 1)
        return jnp.where(first_lane, pltpu.roll(rolled, 1, 0), rolled)

    def col(c):
        return pl.ds(c, 8, stride=2)

    def lon_peer(s):
        return {"lon": lax.rem(me + s + n, n)}

    barrier = pltpu.get_barrier_semaphore()
    for s in NEAR:
        pl.semaphore_signal(barrier, inc=1, device_id=lon_peer(s), device_id_type=MESH)
    if share:
        pl.semaphore_signal(barrier, inc=1, device_id={"grp": 1 - grp}, device_id_type=MESH)

    half = levels // 2
    mine = pl.ds(grp * half if share else 0, half)
    theirs = pl.ds((1 - grp) * half, half) if share else pl.ds(half, levels - half)

    def load(which, g):
        k0, k1 = chunks[g]
        ks = pl.ds(k0, k1 - k0)
        src, dst = ((trc_h.at[:, ks], trc.at[:, ks]), (mer_h.at[ks], mer.at[ks]))[which]
        return pltpu.make_async_copy(src, dst, in_sem.at[which, g])

    count = len(chunks)
    load_zon = [
        pltpu.make_async_copy(zon_h.at[ks], zon.at[ks], in_sem.at[2, i])
        for i, ks in enumerate((mine, theirs))
    ]
    load_bot = pltpu.make_async_copy(bot_h, bot, in_sem.at[3, 0])
    load_surf = pltpu.make_async_copy(surf_h, surf, in_sem.at[3, 1])
    load_zon[0].start()
    load_bot.start()
    load_surf.start()
    load(0, 0).start()
    load_zon[1].start()
    for g in range(1, count):
        load(0, g).start()
    for g in range(count):
        load(1, g).start()
    def gather_chunk(g):
        load(0, g).wait()

        def step(k, carry):
            for c in range(2):
                s_t[c, k, 0] = trc[0, k, col(c), :]
                s_t[c, k, 1] = trc[1, k, col(c), :]
            return carry

        lax.fori_loop(*chunks[g], step, 0, unroll=UNROLL)

    def side_copy(src, dst, send, recv, g, side):
        k0, k1 = chunks[g]
        return pltpu.make_async_remote_copy(
            src_ref=src.at[side, pl.ds(k0, k1 - k0)],
            dst_ref=dst.at[1 - side, pl.ds(k0, k1 - k0)],
            send_sem=send.at[side, g],
            recv_sem=recv.at[1 - side, g],
            device_id={"lon": side_dev[side]},
            device_id_type=MESH,
        )

    def t_copy(g, side):
        return side_copy(s_t, r_t, t_send, t_recv, g, side)

    def b_copy(g, side):
        return side_copy(s_b, r_b, b_send, b_recv, g, side)

    def gather_zonal(i):
        load_zon[i].wait()
        ks = (mine, theirs)[i]

        def step(k, carry):
            for c in range(2):
                s_z[c, ks.start + k] = zon[ks.start + k, col(c), :]
            return carry

        lax.fori_loop(0, ks.size, step, 0, unroll=UNROLL)

    def z_copy(which):
        if not share:
            return pltpu.make_async_remote_copy(
                src_ref=s_z.at[which],
                dst_ref=r_z.at[1 - which],
                send_sem=z_send.at[which],
                recv_sem=z_recv.at[which],
                device_id={"lon": side_dev[which]},
                device_id_type=MESH,
            )
        src, dst, dev = (
            (s_z.at[outer, mine], r_z.at[1 - outer, mine], lon_peer(2 * outer - 1)),
            (s_z.at[inner], r_z.at[1 - inner], lon_peer(2 * inner - 1)),
            (r_z.at[outer, mine], r_z.at[outer, mine], {"grp": 1 - grp}),
        )[which]
        return pltpu.make_async_remote_copy(
            src_ref=src,
            dst_ref=dst,
            send_sem=z_send.at[which],
            recv_sem=z_recv.at[which],
            device_id=dev,
            device_id_type=MESH,
        )

    def send_chunk(g):
        for side in range(2):
            t_copy(g, side).start()

    def shift_copy(buf, send, recv, s, part):
        return pltpu.make_async_remote_copy(
            src_ref=buf.at[0, part],
            dst_ref=buf.at[SLOT[s], part],
            send_sem=send.at[SLOT[s]],
            recv_sem=recv.at[SLOT[s]],
            device_id=lon_peer(s),
            device_id_type=MESH,
        )

    def shift_copies(buf, send, recv, cases, act):
        for s, usual, closing in cases:
            closes = me == (0 if act == "wait_recv" else n - s)
            if usual == closing:
                getattr(shift_copy(buf, send, recv, s, usual), act)()
                continue
            if usual is not None:

                @pl.when(jnp.logical_not(closes))
                def _():
                    getattr(shift_copy(buf, send, recv, s, usual), act)()

            @pl.when(closes)
            def _():
                getattr(shift_copy(buf, send, recv, s, closing), act)()

    every_tile = pl.ds(0, 6)
    st_near = ((1, pl.ds(0, 4), every_tile), (-1, pl.ds(2, 4), pl.ds(2, 4)))
    st_far = (
        (2, pl.ds(3, 1), every_tile),
        *((s, None, every_tile) for s in range(3, FAR + 1)),
        (FAR + 1, None, pl.ds(2, 2)),
        (FAR + 2, None, pl.ds(3, 1)),
    )
    rx_near = ((1, pl.ds(0, 4), pl.ds(0, 4)), (-1, pl.ds(0, 4), pl.ds(0, 4)))
    rx_second = ((2, pl.ds(2, 2), pl.ds(0, 4)),)
    rx_far = (
        *((s, None, pl.ds(0, 4)) for s in range(3, FAR + 2)),
        (FAR + 2, None, pl.ds(2, 2)),
    )

    def st_act(cases, act):
        shift_copies(st, st_send, st_recv, cases, act)

    def rx_act(cases, act):
        shift_copies(rx, rx_send, rx_recv, cases, act)

    near = me < n - FAR
    to_near = lax.rem(me + 2, n) < n - FAR

    gather_zonal(0)
    pl.semaphore_wait(barrier, len(NEAR) + (1 if share else 0))
    if share:
        z_copy(0).start()
    load_bot.wait()
    load_surf.wait()
    for c in range(2):
        d = bot[col(c), :].astype(jnp.float32)
        st[0, 2 + c] = d
        for v in range(2):
            st[0, (4, 0)[c] + v] = jnp.where(d > 0, surf[v, col(c), :], 0.0)
    st_act(st_near, "start")
    gather_chunk(0)
    send_chunk(0)
    gather_zonal(1)
    for which in range(1 if share else 0, 2):
        z_copy(which).start()
    rounds = spread_rounds(n)

    def spread(i):
        if i < len(rounds):
            for s in (rounds[i], -rounds[i]):
                pl.semaphore_signal(
                    met.at[i], inc=1, device_id=lon_peer(s), device_id_type=MESH
                )

    def spread_wait(i):
        if i < len(rounds):
            pl.semaphore_wait(met.at[i], 2)

    spread(0)
    for g in range(1, count):
        gather_chunk(g)
        send_chunk(g)

    spread_wait(0)
    spread(1)
    st_act(st_near, "wait_recv")

    depths = {-2: st[1, 2], -1: st[1, 3], 0: st[0, 2], 1: st[0, 3]}
    depths.update({2: st[SLOT[-1], 2], 3: st[SLOT[-1], 3]})

    def y_face(i):
        wall = jnp.logical_and(last_lane, row == 7)
        return jnp.where(wall, 0.0, jnp.minimum(depths[i], north(depths[i])))

    def x_face(i):
        return jnp.minimum(depths[i], depths[i + 1])

    for which in range(2):
        z_copy(which).wait_recv()
    if share:
        z_copy(2).start()
        z_copy(2).wait_recv()
    quarter = TIME_STEP * 0.25
    diff = TIME_STEP * DIFFUSIVITY
    faces_x = [x_face(f - 1) for f in range(3)]
    faces_y = [y_face(c) for c in range(2)]
    own_depth = [depths[c] for c in range(2)]

    for g, (k0, k1) in enumerate(chunks):
        load(1, g).wait()
        for side in range(2):
            t_copy(g, side).wait_recv()

        def first(k, carry):
            kf = k.astype(jnp.float32)
            z = (r_z[0, k], s_z[0, k], s_z[1, k], r_z[1, k])
            cx = []
            for f in range(3):
                open_f = kf < faces_x[f]
                u = quarter * (z[f] + z[f + 1])
                cx.append((jnp.where(open_f, u + diff, 0.0), jnp.where(open_f, u - diff, 0.0)))
            cy = []
            for c in range(2):
                open_f = kf < faces_y[c]
                m = mer[k, col(c), :]
                u = quarter * (m + north(m))
                cy.append((jnp.where(open_f, u + diff, 0.0), jnp.where(open_f, u - diff, 0.0)))
            for q, (lo, hi) in enumerate(cx + cy):
                coef[k, 2 * q] = lo
                coef[k, 2 * q + 1] = hi
            wet = [kf < own_depth[c] for c in range(2)]
            for v in range(2):
                t = (
                    r_t[0, k, v],
                    jnp.where(wet[0], s_t[0, k, v], 0.0),
                    jnp.where(wet[1], s_t[1, k, v], 0.0),
                    r_t[1, k, v],
                )
                fx = [cx[f][0] * t[f] + cx[f][1] * t[f + 1] for f in range(3)]
                for c in range(2):
                    fy = cy[c][0] * t[c + 1] + cy[c][1] * north(t[c + 1])
                    s_b[c, k, v] = t[c + 1] - ((fx[c + 1] - fx[c]) + (fy - south(fy)))
            return carry

        lax.fori_loop(k0, k1, first, 0, unroll=UNROLL)
        for side in range(2):
            b_copy(g, side).start()
    spread_wait(1)
    spread(2)

    face_x = {i: SURFACE_COUPLING * x_face(i) for i in range(-2, 3)}
    face_y = {i: SURFACE_COUPLING * y_face(i) for i in range(-2, 3)}
    face_s = {i: south(face_y[i]) for i in face_y}
    shared_faces = list(face_x)

    def lap(s, cols):
        gx = {i: face_x[i] * (s[i + 1] - s[i]) for i in range(cols[0] - 1, cols[-1] + 1)}
        res, rise = {}, {}
        for i in cols:
            rise[i] = north(s[i]) - s[i]
            fall = s[i] - south(s[i])
            res[i] = (gx[i - 1] - gx[i]) + (face_s[i] * fall - face_y[i] * rise[i])
        return res, rise

    height = [
        {-1: st[1, v], 0: st[0, 4 + v], 1: st[0, v], 2: st[SLOT[-1], 4 + v]}
        for v in range(2)
    ]
    lap_h = [lap(height[v], OWN)[0] for v in range(2)]

    zero = jnp.zeros(TILE, jnp.float32)
    totals = (zero,) * 7
    for g, (k0, k1) in enumerate(chunks):
        for side in range(2):
            b_copy(g, side).wait_recv()

        def second(k, carry):
            sums, grams = list(carry[:4]), list(carry[4:])
            cx = [(coef[k, 2 * f], coef[k, 2 * f + 1]) for f in range(3)]
            cy = [(coef[k, 6 + 2 * c], coef[k, 7 + 2 * c]) for c in range(2)]
            new = []
            for v in range(2):
                t = (r_b[0, k, v], s_b[0, k, v], s_b[1, k, v], r_b[1, k, v])
                fx = [cx[f][0] * t[f] + cx[f][1] * t[f + 1] for f in range(3)]
                for c in range(2):
                    fy = cy[c][0] * t[c + 1] + cy[c][1] * north(t[c + 1])
                    val = t[c + 1] - ((fx[c + 1] - fx[c]) + (fy - south(fy)))
                    out[v, k, col(c), :] = val
                    sums[2 * v + c] = sums[2 * v + c] + val
                    new.append(val)
            grams[0] = grams[0] + (new[0] * new[0] + new[1] * new[1])
            grams[1] = grams[1] + (new[0] * new[2] + new[1] * new[3])
            grams[2] = grams[2] + (new[2] * new[2] + new[3] * new[3])
            return tuple(sums + grams)

        totals = lax.fori_loop(k0, k1, second, totals, unroll=UNROLL)
        if g == (count - 1) // 2:
            for i in range(2, len(rounds)):
                spread_wait(i)
                spread(i + 1)
            st_act(st_far, "start")

    gain = STERIC_GAIN / levels
    for v in range(2):
        for c in range(2):
            rx[0, 2 * c + v] = gain * totals[2 * v + c] - lap_h[v][c]
    rx_act(rx_far, "start")

    @pl.when(to_near)
    def _():
        rx_act(rx_second, "start")

    rx_act(rx_near, "start")
    st_act(st_far, "wait_recv")

    def add_faces(first, last):
        for i in range(first, last):
            face_x.setdefault(i, SURFACE_COUPLING * x_face(i))
        for i in range(first + 1, last):
            if i not in face_y:
                face_y[i] = SURFACE_COUPLING * y_face(i)
                face_s[i] = south(face_y[i])

    span = 4.0 * levels

    def operator_powers(v, cols):
        l1, rise0 = lap(r_cols[v], range(cols[0] - 2, cols[-1] + 2))
        l2, rise1 = lap(l1, range(cols[0] - 1, cols[-1] + 1))
        return r_cols[v], l1, l2, rise0, rise1

    def moments(cols, tall):
        def gathered(term):
            return functools.reduce(lambda a, b: a + b, [term(c) for c in cols])

        def dot(a, b):
            return gathered(lambda i: a[i] * b[i])

        parts, powers = {}, []
        for v in range(2):
            r, l1, l2, rise0, rise1 = operator_powers(v, cols)
            powers.append((r, l1, l2))
            rise2 = {i: north(l2[i]) - l2[i] for i in cols}
            for i, centre in enumerate(CENTRES):
                shift = centre * span
                if i:
                    b1 = {c: l1[c] - shift * r[c] for c in cols}
                    b2 = {
                        c: (l2[c] - 2.0 * shift * l1[c]) + shift * shift * r[c]
                        for c in range(cols[0] - 1, cols[-1] + 1)
                    }
                    up = {
                        c: (rise2[c] - 2.0 * shift * rise1[c]) + shift * shift * rise0[c]
                        for c in cols
                    }
                else:
                    b1, b2, up = l1, l2, rise2
                    parts["m", v, i, 0] = dot(r, r)
                parts["m", v, i, 1] = dot(r, b1)
                parts["m", v, i, 2] = dot(b1, b1)
                parts["m", v, i, 3] = dot(b1, b2)
                parts["m", v, i, 4] = dot(b2, b2)

                def energy(c):
                    across = b2[c] - b2[c - 1]
                    return face_x[c - 1] * across * across + face_y[c] * up[c] * up[c]

                parts["m", v, i, 5] = gathered(energy)
        for v in range(2):
            for w in range(2):
                for j in range(3):
                    parts["h", v, w, j] = dot(tall[v], powers[w][j])
        for k in range(5):
            parts["c", k] = dot(powers[0][k // 2], powers[1][(k + 1) // 2])
        return parts, powers

    def keep_powers(powers):
        for v in range(2):
            for j in range(3):
                for c in OWN:
                    pw[v, j, c] = powers[v][j][c]

    def take_r(slot):
        for v in range(2):
            for c in range(2):
                r_cols[v][(2 if slot == SLOT[-1] else -2 * slot) + c] = rx[slot, 2 * c + v]

    r_cols = [{}, {}]

    @pl.when(near)
    def _():
        rx_act(rx_near + rx_second, "wait_recv")
        depths[-3] = st[2, 3]
        add_faces(-3, 3)
        for slot in (0, 1, SLOT[-1]):
            take_r(slot)
        for v in range(2):
            r_cols[v][-3] = rx[2, 2 + v]
        parts, powers = moments(OWN, height)
        for q, name in enumerate(MOMENTS):
            mo[q] = parts[name]
        keep_powers(powers)

    @pl.when(jnp.logical_not(near))
    def _():
        for q in range(len(MOMENTS)):
            mo[q] = zero

    for known in (face_x, face_y, face_s):
        for i in [i for i in known if i not in shared_faces]:
            del known[i]

    @pl.when(me == 0)
    def _():
        rx_act(rx_far, "wait_recv")
        tall = [{}, {}]
        for slot in range(1, FAR + 3):
            for c in range(2):
                depths[c - 2 * slot] = st[slot, 2 + c]
        for slot in range(FAR + 3):
            take_r(slot)
        for slot in range(1, FAR + 1):
            for v in range(2):
                tall[v].update({-2 * slot: st[slot, 4 + v], 1 - 2 * slot: st[slot, v]})
        add_faces(-2 * FAR - 3, 1)
        parts, _ = moments(range(-2 * FAR, 0), tall)
        for q, name in enumerate(MOMENTS):
            mo[q] = mo[q] + parts[name]

    for known in (face_x, face_y, face_s):
        for i in [i for i in known if i not in shared_faces]:
            del known[i]

    def dot(a, b):
        return a[0] * b[0] + a[1] * b[1]

    parts = {}
    for q in range(3):
        parts["gram", q] = totals[4 + q]
    parts["hh", 0] = dot(height[0], height[0])
    parts["hh", 1] = dot(height[1], height[1])
    parts["hh", 2] = dot(height[0], height[1])
    for q, name in enumerate(MOMENTS):
        parts[name] = mo[q]

    names = list(parts)
    place = lane - 16 * row
    local = zero
    for q in range(0, len(names), 8):
        level = [parts[name] for name in names[q : q + 8]]
        for shift in (1, 2, 4):
            even = jnp.bitwise_and(row, shift) == 0
            merged = []
            for i in range(0, len(level), 2):
                a, b = level[i], level[min(i + 1, len(level) - 1)]
                merged.append(jnp.where(even, a, b) + pltpu.roll(jnp.where(even, b, a), shift, 0))
            level = merged
        local = jnp.where(place == q // 8, jnp.sum(level[0], axis=1, keepdims=True), local)
    for shift in (4, 2, 1):
        local = local + pltpu.roll(local, shift, 0)
    red[me] = local[0:1]

    def red_copy(i):
        return pltpu.make_async_remote_copy(
            src_ref=red.at[me],
            dst_ref=red.at[me],
            send_sem=rd_send,
            recv_sem=rd_recv,
            device_id=lon_peer(i),
            device_id_type=MESH,
        )

    def every(sem):
        return pltpu.make_async_copy(red.at[pl.ds(0, n - 1)], red.at[pl.ds(0, n - 1)], sem)

    peers_loop(n, lambda i: red_copy(i).start())

    @pl.when(jnp.logical_not(near))
    def _():
        rx_act(rx_near, "wait_recv")
        for slot in (0, 1, SLOT[-1]):
            take_r(slot)
        powers = []
        for v in range(2):
            l1 = lap(r_cols[v], range(-1, 3))[0]
            powers.append((r_cols[v], l1, lap(l1, OWN)[0]))
        keep_powers(powers)

    every(rd_recv).wait()
    terms = [red[i] for i in range(n)]
    while len(terms) > 1:
        terms = [
            terms[i] + terms[i + 1] if i + 1 < len(terms) else terms[i]
            for i in range(0, len(terms), 2)
        ]
    every_row = jnp.broadcast_to(terms[0], TILE)
    for q in range(-(-len(names) // 8)):
        picked = jnp.where(place == q, every_row, 0.0)
        flat[q] = jnp.broadcast_to(jnp.sum(picked, axis=1, keepdims=True), TILE)
    total = {
        name: jnp.broadcast_to(flat[q // 8, q % 8 : q % 8 + 1], TILE)
        for q, name in enumerate(names)
    }

    coefs = []
    for v in range(2):
        m0 = total["m", v, 0, 0]
        m = [m0] + [total["m", v, 0, k] for k in range(1, 6)]
        first_moment = m[1]
        centre = zero
        for i in range(1, len(CENTRES)):
            limit = 0.5 * (CENTRES[i] + CENTRES[i - 1]) * span
            above = first_moment > limit * m0
            centre = jnp.where(above, CENTRES[i] * span, centre)
            m = [m0] + [jnp.where(above, total["m", v, i, k], m[k]) for k in range(1, 6)]
        unit = 1.0 + centre
        a = [unit * m[k] + m[k + 1] for k in range(4)] + [m[4] + m[5]]
        ratio = m[1] / m0
        step0 = m0 / a[0]
        rr1 = step0 * step0 * (m[2] - ratio * m[1])
        beta0 = rr1 / m0
        along = step0 * ratio + beta0
        p1ap1 = along * along * a[0] - 2.0 * along * step0 * a[1] + step0 * step0 * a[2]
        step1 = rr1 / p1ap1
        x0 = step0 * ratio - step1 * along * unit
        x1 = step1 * step0 * unit - (step0 + step1 * along)
        x2 = step1 * step0

        def form(y0, y1, y2, f):
            return (
                y0 * (y0 * f[0] + 2.0 * (y1 * f[1] + y2 * f[2]))
                + y1 * (y1 * f[2] + 2.0 * (y2 * f[3]))
                + y2 * (y2 * f[4])
            )

        rr2 = form(x0, x1, x2, m)
        beta1 = rr2 / rr1
        y0, y1, y2 = x0 + beta1 * along, x1 - beta1 * step0, x2
        step2 = rr2 / form(y0, y1, y2, a)
        e0 = step0 + step1 * along + step2 * y0
        e1 = step2 * y1 - step1 * step0
        e2 = step2 * y2
        coefs.append((e0 - centre * (e1 - centre * e2), e1 - 2.0 * centre * e2, e2))
        for c in OWN:
            w = coefs[v]
            s = pw[v, 0, c] * w[0] + (pw[v, 1, c] * w[1] + pw[v, 2, c] * w[2])
            sout[v, col(c), :] = height[v][c] + s

    def plain(v, k):
        return total["m", v, 0, k]

    gram = []
    for v in range(2):
        w = coefs[v]
        s = total["hh", v] + 2.0 * sum(w[j] * total["h", v, v, j] for j in range(3))
        for i in range(3):
            for j in range(3):
                s = s + w[i] * w[j] * plain(v, i + j)
        gram.append(total["gram", 2 * v] + s)
    mix = total["gram", 1] + total["hh", 2]
    for j in range(3):
        mix = mix + (coefs[1][j] * total["h", 0, 1, j] + coefs[0][j] * total["h", 1, 0, j])
    for i in range(3):
        for j in range(3):
            mix = mix + coefs[0][i] * coefs[1][j] * total["c", i + j]
    cells = float((levels + 1) * 2 * 8 * 128 * n)
    gram_one, gram_two, gram_mix = gram[0] / cells, gram[1] / cells, mix / cells
    scale_one = jnp.sqrt(gram_one + EPSILON)
    cross = gram_mix / scale_one
    rest = gram_two - 2.0 * cross * cross + cross * cross * gram_one / (gram_one + EPSILON)
    scale_two = jnp.sqrt(rest + EPSILON)
    gout[0] = 1.0 / scale_one
    gout[1] = cross
    gout[2] = 1.0 / scale_two
    gout[3] = jnp.where(lane == 0, scale_one, jnp.where(lane == 1, cross, scale_two))

    for g in range(count):
        for side in range(2):
            t_copy(g, side).wait_send()
            b_copy(g, side).wait_send()
    for which in range(3 if share else 2):
        z_copy(which).wait_send()
    st_act(st_near + st_far, "wait_send")
    rx_act(rx_near + rx_far, "wait_send")

    @pl.when(to_near)
    def _():
        rx_act(rx_second, "wait_send")

    every(rd_send).wait()


def scale_kernel(trc, surf, tail, out_h, sout_h, gout_h, out, sout, gvec, sem):
    levels = trc.shape[1]
    chunks = chunk_bounds(levels)
    one, cross, two = tail[0], tail[1], tail[2]
    gvec[...] = tail[3, 0, :3]
    grow = pltpu.make_async_copy(gvec, gout_h, sem.at[len(chunks) + 1])
    grow.start()

    def store(g):
        k0, k1 = chunks[g]
        return pltpu.make_async_copy(
            out.at[:, pl.ds(k0, k1 - k0)], out_h.at[:, pl.ds(k0, k1 - k0)], sem.at[g]
        )

    for g, (k0, k1) in enumerate(chunks):

        def step(k, carry):
            for h in range(2):
                rows = pl.ds(8 * h, 8)
                unit = trc[0, k, rows, :] * one
                out[0, k, rows, :] = unit
                out[1, k, rows, :] = (trc[1, k, rows, :] - cross * unit) * two
            return carry

        lax.fori_loop(k0, k1, step, 0, unroll=UNROLL)
        store(g).start()
    for h in range(2):
        rows = pl.ds(8 * h, 8)
        unit = surf[0, rows, :] * one
        sout[0, rows, :] = unit
        sout[1, rows, :] = (surf[1, rows, :] - cross * unit) * two
    last = pltpu.make_async_copy(sout, sout_h, sem.at[len(chunks)])
    last.start()
    for g in range(len(chunks)):
        store(g).wait()
    last.wait()
    grow.wait()


def packed(x):
    lead, (cols, rows) = x.shape[:-2], x.shape[-2:]
    x = x.reshape(lead + (cols, rows // 128, 128))
    x = jnp.swapaxes(x, -3, -2)
    return x.reshape(lead + (cols * (rows // 128), 128))


def unpacked(x, cols):
    lead, (rows, lanes) = x.shape[:-2], x.shape[-2:]
    x = x.reshape(lead + (rows // cols, cols, lanes))
    x = jnp.swapaxes(x, -3, -2)
    return x.reshape(lead + (cols, rows // cols * lanes))


def on_device(n, groups, tracer_pert, surface_pert, zonal_flow, merid_flow, bottom_level):
    vectors, levels, columns, rows = tracer_pert.shape
    count = len(chunk_bounds(levels))
    share = shares_zonal(groups, levels)
    f32 = jnp.float32
    vmem = pl.BlockSpec(memory_space=pltpu.VMEM)
    hbm = pl.BlockSpec(memory_space=pltpu.HBM)
    dma = pltpu.SemaphoreType.DMA
    zonal_sems = 3 if share else 2
    tracer, surface, tail = pl.pallas_call(
        functools.partial(kernel, n, share),
        out_shape=(
            jax.ShapeDtypeStruct((vectors, levels, 16, 128), f32),
            jax.ShapeDtypeStruct((vectors, 16, 128), f32),
            jax.ShapeDtypeStruct((4, 8, 128), f32),
        ),
        in_specs=[hbm] * 5,
        out_specs=(vmem,) * 3,
        scratch_shapes=[
            pltpu.VMEM((vectors, levels, 16, 128), f32),
            pltpu.VMEM((vectors, 16, 128), f32),
            pltpu.VMEM((levels, 16, 128), f32),
            pltpu.VMEM((levels, 16, 128), f32),
            pltpu.VMEM((16, 128), jnp.int32),
            pltpu.VMEM((2, levels, 2, 8, 128), f32),
            pltpu.VMEM((2, levels, 2, 8, 128), f32),
            pltpu.VMEM((2, levels, 8, 128), f32),
            pltpu.VMEM((2, levels, 8, 128), f32),
            pltpu.VMEM((2, levels, 2, 8, 128), f32),
            pltpu.VMEM((2, levels, 2, 8, 128), f32),
            pltpu.VMEM((levels, 10, 8, 128), f32),
            pltpu.VMEM((len(SLOT), 6, 8, 128), f32),
            pltpu.VMEM((len(SLOT), 4, 8, 128), f32),
            pltpu.VMEM((n, 1, 128), f32),
            pltpu.VMEM((16, 8, 128), f32),
            pltpu.VMEM((len(MOMENTS), 8, 128), f32),
            pltpu.VMEM((2, 3, 2, 8, 128), f32),
            dma((4, max(2, count))),
            dma((2, count)),
            dma((2, count)),
            dma((zonal_sems,)),
            dma((zonal_sems,)),
            dma((2, count)),
            dma((2, count)),
            dma((len(SLOT),)),
            dma((len(SLOT),)),
            dma((len(SLOT),)),
            dma((len(SLOT),)),
            dma(()),
            dma(()),
            pltpu.SemaphoreType.REGULAR((max(1, len(spread_rounds(n))),)),
        ],
        compiler_params=pltpu.CompilerParams(
            collective_id=0, has_side_effects=True, vmem_limit_bytes=40 * 1024 * 1024
        ),
    )(
        *(
            pltpu.with_memory_space_constraint(packed(x), pltpu.HBM)
            for x in (tracer_pert, surface_pert, zonal_flow, merid_flow, bottom_level)
        )
    )
    tracer, surface, growth = pl.pallas_call(
        scale_kernel,
        out_shape=(
            jax.ShapeDtypeStruct((vectors, levels, 16, 128), f32),
            jax.ShapeDtypeStruct((vectors, 16, 128), f32),
            jax.ShapeDtypeStruct((3,), f32),
        ),
        in_specs=[vmem] * 3,
        out_specs=(hbm,) * 3,
        scratch_shapes=[
            pltpu.VMEM((vectors, levels, 16, 128), f32),
            pltpu.VMEM((vectors, 16, 128), f32),
            pltpu.VMEM((3,), f32),
            dma((count + 2,)),
        ],
        compiler_params=pltpu.CompilerParams(vmem_limit_bytes=16 * 1024 * 1024),
    )(tracer, surface, tail)
    return unpacked(tracer, columns), unpacked(surface, columns), growth


def solution(mesh):
    placed = (
        P("grp", None, "lon", None),
        P("grp", "lon", None),
        P(None, "lon", None),
        P(None, "lon", None),
        P("lon", None),
    )
    return jax.shard_map(
        functools.partial(on_device, mesh.shape["lon"], mesh.shape["grp"]),
        mesh=mesh,
        in_specs=placed,
        out_specs=(P("grp", None, "lon", None), P("grp", "lon", None), P("grp")),
        check_vma=False,
    )
```

```python
import functools

import jax
import jax.numpy as jnp
from jax import lax
from jax.experimental import pallas as pl
from jax.experimental.pallas import tpu as pltpu
from jax.sharding import PartitionSpec as P

DIFFUSIVITY = 0.5
TIME_STEP = 0.2
SURFACE_COUPLING = 0.5
STERIC_GAIN = 2.0
EPSILON = 1e-06
MESH = pl.DeviceIdType.MESH
CHUNKS = 5
UNROLL = 10
NEAR = (1, -1)
CENTRES = (0.0, 0.04, 0.16, 0.64)
FAR = 4
SLOT = {0: 0, **{s: s for s in range(1, FAR + 3)}, -1: FAR + 3}
OWN = (0, 1)
MOMENTS = (
    [("m", v, i, k) for v in range(2) for i in range(len(CENTRES)) for k in range(1 if i else 0, 6)]
    + [("h", v, w, j) for v in range(2) for w in range(2) for j in range(3)]
    + [("c", k) for k in range(5)]
)
TILE = (8, 128)


def chunk_count(levels):
    return max(c for c in range(1, CHUNKS + 1) if levels % c == 0)


def spread_rounds(n):
    reach, rounds = 1, []
    while 2 * reach < n:
        rounds.append(reach)
        reach *= 2
    return rounds


def shares_zonal(groups, levels):
    return groups == 2 and levels % 2 == 0


def peers_loop(n, body):
    if n <= 16:
        for i in range(1, n):
            body(i)
    else:

        def step(i, carry):
            body(i)
            return carry

        lax.fori_loop(1, n, step, 0)


def kernel(
    n, share, trc_h, surf_h, zon_h, mer_h, bot_h, out, sout, gout,
    trc, surf, zon, mer, bot, s_t, r_t, s_z, r_z, s_b, r_b, coef, st, rx, red, flat, mo, pw,
    in_sem, t_send, t_recv, z_send, z_recv, b_send, b_recv,
    st_send, st_recv, rx_send, rx_recv, rd_send, rd_recv, met,
):
    me = lax.axis_index("lon")
    grp = lax.axis_index("grp")
    levels = zon.shape[0]
    count = chunk_count(levels)
    size = levels // count
    side_dev = (lax.rem(me + n - 1, n), lax.rem(me + 1, n))
    outer = lax.rem(me, 2)
    inner = 1 - outer
    lane = lax.broadcasted_iota(jnp.int32, TILE, 1)
    row = lax.broadcasted_iota(jnp.int32, TILE, 0)
    last_lane, first_lane = lane == 127, lane == 0

    def north(x):
        rolled = pltpu.roll(x, 127, 1)
        return jnp.where(last_lane, pltpu.roll(rolled, 7, 0), rolled)

    def south(x):
        rolled = pltpu.roll(x, 1, 1)
        return jnp.where(first_lane, pltpu.roll(rolled, 1, 0), rolled)

    def col(c):
        return pl.ds(c, 8, stride=2)

    def lon_peer(s):
        return {"lon": lax.rem(me + s + n, n)}

    barrier = pltpu.get_barrier_semaphore()
    for s in NEAR:
        pl.semaphore_signal(barrier, inc=1, device_id=lon_peer(s), device_id_type=MESH)
    if share:
        pl.semaphore_signal(barrier, inc=1, device_id={"grp": 1 - grp}, device_id_type=MESH)

    half = levels // 2
    mine = pl.ds(grp * half if share else 0, half)
    theirs = pl.ds((1 - grp) * half, half) if share else pl.ds(half, levels - half)

    def chunk(g):
        return pl.ds(g * size, size)

    def in_chunk(g, body, carry):
        return lax.fori_loop(
            0, size, lambda i, state: body(g * size + i, state), carry, unroll=min(UNROLL, size)
        )

    def load(which, g):
        ks = chunk(g)
        src, dst = ((trc_h.at[:, ks], trc.at[:, ks]), (mer_h.at[ks], mer.at[ks]))[which]
        return pltpu.make_async_copy(src, dst, in_sem.at[which, g])

    load_zon = [
        pltpu.make_async_copy(zon_h.at[ks], zon.at[ks], in_sem.at[2, i])
        for i, ks in enumerate((mine, theirs))
    ]
    load_bot = pltpu.make_async_copy(bot_h, bot, in_sem.at[3, 0])
    load_surf = pltpu.make_async_copy(surf_h, surf, in_sem.at[3, 1])
    load_zon[0].start()
    load_bot.start()
    load_surf.start()
    load(0, 0).start()
    load_zon[1].start()
    for g in range(1, count):
        load(0, g).start()
    for g in range(count):
        load(1, g).start()
    def gather_chunk(g):
        load(0, g).wait()

        def step(k, carry):
            for c in range(2):
                s_t[c, k, 0] = trc[0, k, col(c), :]
                s_t[c, k, 1] = trc[1, k, col(c), :]
            return carry

        in_chunk(g, step, 0)

    def side_copy(src, dst, send, recv, g, side):
        return pltpu.make_async_remote_copy(
            src_ref=src.at[side, chunk(g)],
            dst_ref=dst.at[1 - side, chunk(g)],
            send_sem=send.at[side, g],
            recv_sem=recv.at[1 - side, g],
            device_id={"lon": side_dev[side]},
            device_id_type=MESH,
        )

    def t_copy(g, side):
        return side_copy(s_t, r_t, t_send, t_recv, g, side)

    def b_copy(g, side):
        return side_copy(s_b, r_b, b_send, b_recv, g, side)

    def gather_zonal(i):
        load_zon[i].wait()
        ks = (mine, theirs)[i]

        def step(k, carry):
            for c in range(2):
                s_z[c, ks.start + k] = zon[ks.start + k, col(c), :]
            return carry

        lax.fori_loop(0, ks.size, step, 0, unroll=5)

    def z_copy(which):
        if not share:
            return pltpu.make_async_remote_copy(
                src_ref=s_z.at[which],
                dst_ref=r_z.at[1 - which],
                send_sem=z_send.at[which],
                recv_sem=z_recv.at[which],
                device_id={"lon": side_dev[which]},
                device_id_type=MESH,
            )
        src, dst, dev = (
            (s_z.at[outer, mine], r_z.at[1 - outer, mine], lon_peer(2 * outer - 1)),
            (s_z.at[inner], r_z.at[1 - inner], lon_peer(2 * inner - 1)),
            (r_z.at[outer, mine], r_z.at[outer, mine], {"grp": 1 - grp}),
        )[which]
        return pltpu.make_async_remote_copy(
            src_ref=src,
            dst_ref=dst,
            send_sem=z_send.at[which],
            recv_sem=z_recv.at[which],
            device_id=dev,
            device_id_type=MESH,
        )

    def send_chunk(g):
        for side in range(2):
            t_copy(g, side).start()

    def shift_copy(buf, send, recv, s, part):
        return pltpu.make_async_remote_copy(
            src_ref=buf.at[0, part],
            dst_ref=buf.at[SLOT[s], part],
            send_sem=send.at[SLOT[s]],
            recv_sem=recv.at[SLOT[s]],
            device_id=lon_peer(s),
            device_id_type=MESH,
        )

    def shift_copies(buf, send, recv, cases, act):
        for s, usual, closing in cases:
            closes = me == (0 if act == "wait_recv" else n - s)
            if usual == closing:
                getattr(shift_copy(buf, send, recv, s, usual), act)()
                continue
            if usual is not None:

                @pl.when(jnp.logical_not(closes))
                def _():
                    getattr(shift_copy(buf, send, recv, s, usual), act)()

            @pl.when(closes)
            def _():
                getattr(shift_copy(buf, send, recv, s, closing), act)()

    every_tile = pl.ds(0, 6)
    st_near = ((1, pl.ds(0, 4), every_tile), (-1, pl.ds(2, 4), pl.ds(2, 4)))
    st_far = (
        (2, pl.ds(3, 1), every_tile),
        *((s, None, every_tile) for s in range(3, FAR + 1)),
        (FAR + 1, None, pl.ds(2, 2)),
        (FAR + 2, None, pl.ds(3, 1)),
    )
    rx_near = ((1, pl.ds(0, 4), pl.ds(0, 4)), (-1, pl.ds(0, 4), pl.ds(0, 4)))
    rx_second = ((2, pl.ds(2, 2), pl.ds(0, 4)),)
    rx_far = (
        *((s, None, pl.ds(0, 4)) for s in range(3, FAR + 2)),
        (FAR + 2, None, pl.ds(2, 2)),
    )

    def st_act(cases, act):
        shift_copies(st, st_send, st_recv, cases, act)

    def rx_act(cases, act):
        shift_copies(rx, rx_send, rx_recv, cases, act)

    near = me < n - FAR
    to_near = lax.rem(me + 2, n) < n - FAR

    gather_zonal(0)
    pl.semaphore_wait(barrier, len(NEAR) + (1 if share else 0))
    if share:
        z_copy(0).start()
    load_bot.wait()
    load_surf.wait()
    for c in range(2):
        d = bot[col(c), :].astype(jnp.float32)
        st[0, 2 + c] = d
        for v in range(2):
            st[0, (4, 0)[c] + v] = jnp.where(d > 0, surf[v, col(c), :], 0.0)
    st_act(st_near, "start")
    gather_chunk(0)
    send_chunk(0)
    gather_zonal(1)
    for which in range(1 if share else 0, 2):
        z_copy(which).start()
    rounds = spread_rounds(n)

    def spread(i):
        if i < len(rounds):
            for s in (rounds[i], -rounds[i]):
                pl.semaphore_signal(
                    met.at[i], inc=1, device_id=lon_peer(s), device_id_type=MESH
                )

    def spread_wait(i):
        if i < len(rounds):
            pl.semaphore_wait(met.at[i], 2)

    spread(0)

    @pl.loop(1, count)
    def _(g):
        gather_chunk(g)
        send_chunk(g)


    spread_wait(0)
    spread(1)
    st_act(st_near, "wait_recv")

    depths = {-2: st[1, 2], -1: st[1, 3], 0: st[0, 2], 1: st[0, 3]}
    depths.update({2: st[SLOT[-1], 2], 3: st[SLOT[-1], 3]})

    def y_face(i):
        wall = jnp.logical_and(last_lane, row == 7)
        return jnp.where(wall, 0.0, jnp.minimum(depths[i], north(depths[i])))

    def x_face(i):
        return jnp.minimum(depths[i], depths[i + 1])

    for which in range(2):
        z_copy(which).wait_recv()
    if share:
        z_copy(2).start()
        z_copy(2).wait_recv()
    quarter = TIME_STEP * 0.25
    diff = TIME_STEP * DIFFUSIVITY
    faces_x = [x_face(f - 1) for f in range(3)]
    faces_y = [y_face(c) for c in range(2)]
    own_depth = [depths[c] for c in range(2)]

    @pl.loop(0, count)
    def _(g):
        load(1, g).wait()
        for side in range(2):
            t_copy(g, side).wait_recv()

        def first(k, carry):
            kf = k.astype(jnp.float32)
            z = (r_z[0, k], s_z[0, k], s_z[1, k], r_z[1, k])
            cx = []
            for f in range(3):
                open_f = kf < faces_x[f]
                u = quarter * (z[f] + z[f + 1])
                cx.append((jnp.where(open_f, u + diff, 0.0), jnp.where(open_f, u - diff, 0.0)))
            cy = []
            for c in range(2):
                open_f = kf < faces_y[c]
                m = mer[k, col(c), :]
                u = quarter * (m + north(m))
                cy.append((jnp.where(open_f, u + diff, 0.0), jnp.where(open_f, u - diff, 0.0)))
            for q, (lo, hi) in enumerate(cx + cy):
                coef[k, 2 * q] = lo
                coef[k, 2 * q + 1] = hi
            wet = [kf < own_depth[c] for c in range(2)]
            for v in range(2):
                t = (
                    r_t[0, k, v],
                    jnp.where(wet[0], s_t[0, k, v], 0.0),
                    jnp.where(wet[1], s_t[1, k, v], 0.0),
                    r_t[1, k, v],
                )
                fx = [cx[f][0] * t[f] + cx[f][1] * t[f + 1] for f in range(3)]
                for c in range(2):
                    fy = cy[c][0] * t[c + 1] + cy[c][1] * north(t[c + 1])
                    s_b[c, k, v] = t[c + 1] - ((fx[c + 1] - fx[c]) + (fy - south(fy)))
            return carry

        in_chunk(g, first, 0)
        for side in range(2):
            b_copy(g, side).start()
    spread_wait(1)
    spread(2)

    face_x = {i: SURFACE_COUPLING * x_face(i) for i in range(-2, 3)}
    face_y = {i: SURFACE_COUPLING * y_face(i) for i in range(-2, 3)}
    face_s = {i: south(face_y[i]) for i in face_y}
    shared_faces = list(face_x)

    def lap(s, cols):
        gx = {i: face_x[i] * (s[i + 1] - s[i]) for i in range(cols[0] - 1, cols[-1] + 1)}
        res, rise = {}, {}
        for i in cols:
            rise[i] = north(s[i]) - s[i]
            fall = s[i] - south(s[i])
            res[i] = (gx[i - 1] - gx[i]) + (face_s[i] * fall - face_y[i] * rise[i])
        return res, rise

    height = [
        {-1: st[1, v], 0: st[0, 4 + v], 1: st[0, v], 2: st[SLOT[-1], 4 + v]}
        for v in range(2)
    ]
    lap_h = [lap(height[v], OWN)[0] for v in range(2)]

    zero = jnp.zeros(TILE, jnp.float32)

    def second_chunk(g, totals):
        for side in range(2):
            b_copy(g, side).wait_recv()

        def second(k, carry):
            sums, grams = list(carry[:4]), list(carry[4:])
            cx = [(coef[k, 2 * f], coef[k, 2 * f + 1]) for f in range(3)]
            cy = [(coef[k, 6 + 2 * c], coef[k, 7 + 2 * c]) for c in range(2)]
            new = []
            for v in range(2):
                t = (r_b[0, k, v], s_b[0, k, v], s_b[1, k, v], r_b[1, k, v])
                fx = [cx[f][0] * t[f] + cx[f][1] * t[f + 1] for f in range(3)]
                for c in range(2):
                    fy = cy[c][0] * t[c + 1] + cy[c][1] * north(t[c + 1])
                    val = t[c + 1] - ((fx[c + 1] - fx[c]) + (fy - south(fy)))
                    out[v, k, col(c), :] = val
                    sums[2 * v + c] = sums[2 * v + c] + val
                    new.append(val)
            grams[0] = grams[0] + (new[0] * new[0] + new[1] * new[1])
            grams[1] = grams[1] + (new[0] * new[2] + new[1] * new[3])
            grams[2] = grams[2] + (new[2] * new[2] + new[3] * new[3])
            return tuple(sums + grams)

        return in_chunk(g, second, totals)

    totals = lax.fori_loop(0, count // 2 + 1, second_chunk, (zero,) * 7)
    for i in range(2, len(rounds)):
        spread_wait(i)
        spread(i + 1)
    st_act(st_far, "start")
    totals = lax.fori_loop(count // 2 + 1, count, second_chunk, totals)

    gain = STERIC_GAIN / levels
    for v in range(2):
        for c in range(2):
            rx[0, 2 * c + v] = gain * totals[2 * v + c] - lap_h[v][c]
    rx_act(rx_far, "start")

    @pl.when(to_near)
    def _():
        rx_act(rx_second, "start")

    rx_act(rx_near, "start")
    st_act(st_far, "wait_recv")

    def add_faces(first, last):
        for i in range(first, last):
            face_x.setdefault(i, SURFACE_COUPLING * x_face(i))
        for i in range(first + 1, last):
            if i not in face_y:
                face_y[i] = SURFACE_COUPLING * y_face(i)
                face_s[i] = south(face_y[i])

    span = 4.0 * levels

    def operator_powers(v, cols):
        l1, rise0 = lap(r_cols[v], range(cols[0] - 2, cols[-1] + 2))
        l2, rise1 = lap(l1, range(cols[0] - 1, cols[-1] + 1))
        return r_cols[v], l1, l2, rise0, rise1

    def moments(cols, tall):
        def gathered(term):
            return functools.reduce(lambda a, b: a + b, [term(c) for c in cols])

        def dot(a, b):
            return gathered(lambda i: a[i] * b[i])

        parts, powers = {}, []
        for v in range(2):
            r, l1, l2, rise0, rise1 = operator_powers(v, cols)
            powers.append((r, l1, l2))
            rise2 = {i: north(l2[i]) - l2[i] for i in cols}
            for i, centre in enumerate(CENTRES):
                shift = centre * span
                if i:
                    b1 = {c: l1[c] - shift * r[c] for c in cols}
                    b2 = {
                        c: (l2[c] - 2.0 * shift * l1[c]) + shift * shift * r[c]
                        for c in range(cols[0] - 1, cols[-1] + 1)
                    }
                    up = {
                        c: (rise2[c] - 2.0 * shift * rise1[c]) + shift * shift * rise0[c]
                        for c in cols
                    }
                else:
                    b1, b2, up = l1, l2, rise2
                    parts["m", v, i, 0] = dot(r, r)
                parts["m", v, i, 1] = dot(r, b1)
                parts["m", v, i, 2] = dot(b1, b1)
                parts["m", v, i, 3] = dot(b1, b2)
                parts["m", v, i, 4] = dot(b2, b2)

                def energy(c):
                    across = b2[c] - b2[c - 1]
                    return face_x[c - 1] * across * across + face_y[c] * up[c] * up[c]

                parts["m", v, i, 5] = gathered(energy)
        for v in range(2):
            for w in range(2):
                for j in range(3):
                    parts["h", v, w, j] = dot(tall[v], powers[w][j])
        for k in range(5):
            parts["c", k] = dot(powers[0][k // 2], powers[1][(k + 1) // 2])
        return parts, powers

    def keep_powers(powers):
        for v in range(2):
            for j in range(3):
                for c in OWN:
                    pw[v, j, c] = powers[v][j][c]

    def take_r(slot):
        for v in range(2):
            for c in range(2):
                r_cols[v][(2 if slot == SLOT[-1] else -2 * slot) + c] = rx[slot, 2 * c + v]

    r_cols = [{}, {}]

    @pl.when(near)
    def _():
        rx_act(rx_near + rx_second, "wait_recv")
        depths[-3] = st[2, 3]
        add_faces(-3, 3)
        for slot in (0, 1, SLOT[-1]):
            take_r(slot)
        for v in range(2):
            r_cols[v][-3] = rx[2, 2 + v]
        parts, powers = moments(OWN, height)
        for q, name in enumerate(MOMENTS):
            mo[q] = parts[name]
        keep_powers(powers)

    @pl.when(jnp.logical_not(near))
    def _():
        for q in range(len(MOMENTS)):
            mo[q] = zero

    for known in (face_x, face_y, face_s):
        for i in [i for i in known if i not in shared_faces]:
            del known[i]

    @pl.when(me == 0)
    def _():
        rx_act(rx_far, "wait_recv")
        tall = [{}, {}]
        for slot in range(1, FAR + 3):
            for c in range(2):
                depths[c - 2 * slot] = st[slot, 2 + c]
        for slot in range(FAR + 3):
            take_r(slot)
        for slot in range(1, FAR + 1):
            for v in range(2):
                tall[v].update({-2 * slot: st[slot, 4 + v], 1 - 2 * slot: st[slot, v]})
        add_faces(-2 * FAR - 3, 1)
        parts, _ = moments(range(-2 * FAR, 0), tall)
        for q, name in enumerate(MOMENTS):
            mo[q] = mo[q] + parts[name]

    for known in (face_x, face_y, face_s):
        for i in [i for i in known if i not in shared_faces]:
            del known[i]

    def dot(a, b):
        return a[0] * b[0] + a[1] * b[1]

    parts = {}
    for q in range(3):
        parts["gram", q] = totals[4 + q]
    parts["hh", 0] = dot(height[0], height[0])
    parts["hh", 1] = dot(height[1], height[1])
    parts["hh", 2] = dot(height[0], height[1])
    for q, name in enumerate(MOMENTS):
        parts[name] = mo[q]

    names = list(parts)
    place = lane - 16 * row
    local = zero
    for q in range(0, len(names), 8):
        level = [parts[name] for name in names[q : q + 8]]
        for shift in (1, 2, 4):
            even = jnp.bitwise_and(row, shift) == 0
            merged = []
            for i in range(0, len(level), 2):
                a, b = level[i], level[min(i + 1, len(level) - 1)]
                merged.append(jnp.where(even, a, b) + pltpu.roll(jnp.where(even, b, a), shift, 0))
            level = merged
        local = jnp.where(place == q // 8, jnp.sum(level[0], axis=1, keepdims=True), local)
    for shift in (4, 2, 1):
        local = local + pltpu.roll(local, shift, 0)
    red[me] = local[0:1]

    def red_copy(i):
        return pltpu.make_async_remote_copy(
            src_ref=red.at[me],
            dst_ref=red.at[me],
            send_sem=rd_send,
            recv_sem=rd_recv,
            device_id=lon_peer(i),
            device_id_type=MESH,
        )

    def every(sem):
        return pltpu.make_async_copy(red.at[pl.ds(0, n - 1)], red.at[pl.ds(0, n - 1)], sem)

    peers_loop(n, lambda i: red_copy(i).start())

    @pl.when(jnp.logical_not(near))
    def _():
        rx_act(rx_near, "wait_recv")
        for slot in (0, 1, SLOT[-1]):
            take_r(slot)
        powers = []
        for v in range(2):
            l1 = lap(r_cols[v], range(-1, 3))[0]
            powers.append((r_cols[v], l1, lap(l1, OWN)[0]))
        keep_powers(powers)

    every(rd_recv).wait()
    terms = [red[i] for i in range(n)]
    while len(terms) > 1:
        terms = [
            terms[i] + terms[i + 1] if i + 1 < len(terms) else terms[i]
            for i in range(0, len(terms), 2)
        ]
    every_row = jnp.broadcast_to(terms[0], TILE)
    for q in range(-(-len(names) // 8)):
        picked = jnp.where(place == q, every_row, 0.0)
        flat[q] = jnp.broadcast_to(jnp.sum(picked, axis=1, keepdims=True), TILE)
    total = {
        name: jnp.broadcast_to(flat[q // 8, q % 8 : q % 8 + 1], TILE)
        for q, name in enumerate(names)
    }

    coefs = []
    for v in range(2):
        m0 = total["m", v, 0, 0]
        m = [m0] + [total["m", v, 0, k] for k in range(1, 6)]
        first_moment = m[1]
        centre = zero
        for i in range(1, len(CENTRES)):
            limit = 0.5 * (CENTRES[i] + CENTRES[i - 1]) * span
            above = first_moment > limit * m0
            centre = jnp.where(above, CENTRES[i] * span, centre)
            m = [m0] + [jnp.where(above, total["m", v, i, k], m[k]) for k in range(1, 6)]
        unit = 1.0 + centre
        a = [unit * m[k] + m[k + 1] for k in range(4)] + [m[4] + m[5]]
        ratio = m[1] / m0
        step0 = m0 / a[0]
        rr1 = step0 * step0 * (m[2] - ratio * m[1])
        beta0 = rr1 / m0
        along = step0 * ratio + beta0
        p1ap1 = along * along * a[0] - 2.0 * along * step0 * a[1] + step0 * step0 * a[2]
        step1 = rr1 / p1ap1
        x0 = step0 * ratio - step1 * along * unit
        x1 = step1 * step0 * unit - (step0 + step1 * along)
        x2 = step1 * step0

        def form(y0, y1, y2, f):
            return (
                y0 * (y0 * f[0] + 2.0 * (y1 * f[1] + y2 * f[2]))
                + y1 * (y1 * f[2] + 2.0 * (y2 * f[3]))
                + y2 * (y2 * f[4])
            )

        rr2 = form(x0, x1, x2, m)
        beta1 = rr2 / rr1
        y0, y1, y2 = x0 + beta1 * along, x1 - beta1 * step0, x2
        step2 = rr2 / form(y0, y1, y2, a)
        e0 = step0 + step1 * along + step2 * y0
        e1 = step2 * y1 - step1 * step0
        e2 = step2 * y2
        coefs.append((e0 - centre * (e1 - centre * e2), e1 - 2.0 * centre * e2, e2))
        for c in OWN:
            w = coefs[v]
            s = pw[v, 0, c] * w[0] + (pw[v, 1, c] * w[1] + pw[v, 2, c] * w[2])
            sout[v, col(c), :] = height[v][c] + s

    def plain(v, k):
        return total["m", v, 0, k]

    gram = []
    for v in range(2):
        w = coefs[v]
        s = total["hh", v] + 2.0 * sum(w[j] * total["h", v, v, j] for j in range(3))
        for i in range(3):
            for j in range(3):
                s = s + w[i] * w[j] * plain(v, i + j)
        gram.append(total["gram", 2 * v] + s)
    mix = total["gram", 1] + total["hh", 2]
    for j in range(3):
        mix = mix + (coefs[1][j] * total["h", 0, 1, j] + coefs[0][j] * total["h", 1, 0, j])
    for i in range(3):
        for j in range(3):
            mix = mix + coefs[0][i] * coefs[1][j] * total["c", i + j]
    cells = float((levels + 1) * 2 * 8 * 128 * n)
    gram_one, gram_two, gram_mix = gram[0] / cells, gram[1] / cells, mix / cells
    scale_one = jnp.sqrt(gram_one + EPSILON)
    cross = gram_mix / scale_one
    rest = gram_two - 2.0 * cross * cross + cross * cross * gram_one / (gram_one + EPSILON)
    scale_two = jnp.sqrt(rest + EPSILON)
    gout[0] = 1.0 / scale_one
    gout[1] = cross
    gout[2] = 1.0 / scale_two
    gout[3] = jnp.where(lane == 0, scale_one, jnp.where(lane == 1, cross, scale_two))


    @pl.loop(0, count)
    def _(g):
        for side in range(2):
            t_copy(g, side).wait_send()
            b_copy(g, side).wait_send()

    for which in range(3 if share else 2):
        z_copy(which).wait_send()
    st_act(st_near + st_far, "wait_send")
    rx_act(rx_near + rx_far, "wait_send")

    @pl.when(to_near)
    def _():
        rx_act(rx_second, "wait_send")

    every(rd_send).wait()


def scale_kernel(trc, surf, tail, out_h, sout_h, gout_h, out, sout, gvec, sem):
    levels = trc.shape[1]
    count = chunk_count(levels)
    size = levels // count
    one, cross, two = tail[0], tail[1], tail[2]
    gvec[...] = tail[3, 0, :3]
    grow = pltpu.make_async_copy(gvec, gout_h, sem.at[count + 1])
    grow.start()

    def store(g):
        ks = pl.ds(g * size, size)
        return pltpu.make_async_copy(out.at[:, ks], out_h.at[:, ks], sem.at[g])

    @pl.loop(0, count)
    def _(g):
        def step(i, carry):
            k = g * size + i
            for h in range(2):
                rows = pl.ds(8 * h, 8)
                unit = trc[0, k, rows, :] * one
                out[0, k, rows, :] = unit
                out[1, k, rows, :] = (trc[1, k, rows, :] - cross * unit) * two
            return carry

        lax.fori_loop(0, size, step, 0, unroll=min(UNROLL, size))
        store(g).start()

    for h in range(2):
        rows = pl.ds(8 * h, 8)
        unit = surf[0, rows, :] * one
        sout[0, rows, :] = unit
        sout[1, rows, :] = (surf[1, rows, :] - cross * unit) * two
    last = pltpu.make_async_copy(sout, sout_h, sem.at[count])
    last.start()
    for g in range(count):
        store(g).wait()
    last.wait()
    grow.wait()


def packed(x):
    lead, (cols, rows) = x.shape[:-2], x.shape[-2:]
    x = x.reshape(lead + (cols, rows // 128, 128))
    x = jnp.swapaxes(x, -3, -2)
    return x.reshape(lead + (cols * (rows // 128), 128))


def unpacked(x, cols):
    lead, (rows, lanes) = x.shape[:-2], x.shape[-2:]
    x = x.reshape(lead + (rows // cols, cols, lanes))
    x = jnp.swapaxes(x, -3, -2)
    return x.reshape(lead + (cols, rows // cols * lanes))


def on_device(n, groups, tracer_pert, surface_pert, zonal_flow, merid_flow, bottom_level):
    vectors, levels, columns, rows = tracer_pert.shape
    count = chunk_count(levels)
    share = shares_zonal(groups, levels)
    f32 = jnp.float32
    vmem = pl.BlockSpec(memory_space=pltpu.VMEM)
    hbm = pl.BlockSpec(memory_space=pltpu.HBM)
    dma = pltpu.SemaphoreType.DMA
    zonal_sems = 3 if share else 2
    tracer, surface, tail = pl.pallas_call(
        functools.partial(kernel, n, share),
        out_shape=(
            jax.ShapeDtypeStruct((vectors, levels, 16, 128), f32),
            jax.ShapeDtypeStruct((vectors, 16, 128), f32),
            jax.ShapeDtypeStruct((4, 8, 128), f32),
        ),
        in_specs=[hbm] * 5,
        out_specs=(vmem,) * 3,
        scratch_shapes=[
            pltpu.VMEM((vectors, levels, 16, 128), f32),
            pltpu.VMEM((vectors, 16, 128), f32),
            pltpu.VMEM((levels, 16, 128), f32),
            pltpu.VMEM((levels, 16, 128), f32),
            pltpu.VMEM((16, 128), jnp.int32),
            pltpu.VMEM((2, levels, 2, 8, 128), f32),
            pltpu.VMEM((2, levels, 2, 8, 128), f32),
            pltpu.VMEM((2, levels, 8, 128), f32),
            pltpu.VMEM((2, levels, 8, 128), f32),
            pltpu.VMEM((2, levels, 2, 8, 128), f32),
            pltpu.VMEM((2, levels, 2, 8, 128), f32),
            pltpu.VMEM((levels, 10, 8, 128), f32),
            pltpu.VMEM((len(SLOT), 6, 8, 128), f32),
            pltpu.VMEM((len(SLOT), 4, 8, 128), f32),
            pltpu.VMEM((n, 1, 128), f32),
            pltpu.VMEM((16, 8, 128), f32),
            pltpu.VMEM((len(MOMENTS), 8, 128), f32),
            pltpu.VMEM((2, 3, 2, 8, 128), f32),
            dma((4, max(2, count))),
            dma((2, count)),
            dma((2, count)),
            dma((zonal_sems,)),
            dma((zonal_sems,)),
            dma((2, count)),
            dma((2, count)),
            dma((len(SLOT),)),
            dma((len(SLOT),)),
            dma((len(SLOT),)),
            dma((len(SLOT),)),
            dma(()),
            dma(()),
            pltpu.SemaphoreType.REGULAR((max(1, len(spread_rounds(n))),)),
        ],
        compiler_params=pltpu.CompilerParams(
            collective_id=0, has_side_effects=True, vmem_limit_bytes=40 * 1024 * 1024
        ),
    )(
        *(
            pltpu.with_memory_space_constraint(packed(x), pltpu.HBM)
            for x in (tracer_pert, surface_pert, zonal_flow, merid_flow, bottom_level)
        )
    )
    tracer, surface, growth = pl.pallas_call(
        scale_kernel,
        out_shape=(
            jax.ShapeDtypeStruct((vectors, levels, 16, 128), f32),
            jax.ShapeDtypeStruct((vectors, 16, 128), f32),
            jax.ShapeDtypeStruct((3,), f32),
        ),
        in_specs=[vmem] * 3,
        out_specs=(hbm,) * 3,
        scratch_shapes=[
            pltpu.VMEM((vectors, levels, 16, 128), f32),
            pltpu.VMEM((vectors, 16, 128), f32),
            pltpu.VMEM((3,), f32),
            dma((count + 2,)),
        ],
        compiler_params=pltpu.CompilerParams(vmem_limit_bytes=16 * 1024 * 1024),
    )(tracer, surface, tail)
    return unpacked(tracer, columns), unpacked(surface, columns), growth


def solution(mesh):
    placed = (
        P("grp", None, "lon", None),
        P("grp", "lon", None),
        P(None, "lon", None),
        P(None, "lon", None),
        P("lon", None),
    )
    return jax.shard_map(
        functools.partial(on_device, mesh.shape["lon"], mesh.shape["grp"]),
        mesh=mesh,
        in_specs=placed,
        out_specs=(P("grp", None, "lon", None), P("grp", "lon", None), P("grp")),
        check_vma=False,
    )
```

```python
import functools

import jax
import jax.numpy as jnp
from jax import lax
from jax.experimental import pallas as pl
from jax.experimental.pallas import tpu as pltpu
from jax.sharding import PartitionSpec as P

DIFFUSIVITY = 0.5
TIME_STEP = 0.2
SURFACE_COUPLING = 0.5
STERIC_GAIN = 2.0
EPSILON = 1e-06
MESH = pl.DeviceIdType.MESH
CHUNKS = 5
UNROLL = 10
NEAR = (1, -1)
CENTRES = (0.0, 0.04, 0.16, 0.64)
FAR = 4
SLOT = {0: 0, **{s: s for s in range(1, FAR + 3)}, -1: FAR + 3}
OWN = (0, 1)
MOMENTS = (
    [("m", v, i, k) for v in range(2) for i in range(len(CENTRES)) for k in range(1 if i else 0, 6)]
    + [("h", v, w, j) for v in range(2) for w in range(2) for j in range(3)]
    + [("c", k) for k in range(5)]
)
TILE = (8, 128)


def chunk_count(levels):
    return max(c for c in range(1, CHUNKS + 1) if levels % c == 0)


def spread_rounds(n):
    reach, rounds = 1, []
    while 2 * reach < n:
        rounds.append(reach)
        reach *= 2
    return rounds


def shares_zonal(groups, levels):
    return groups == 2 and levels % 2 == 0


def peers_loop(n, body):
    if n <= 16:
        for i in range(1, n):
            body(i)
    else:

        def step(i, carry):
            body(i)
            return carry

        lax.fori_loop(1, n, step, 0)


def kernel(
    n, share, trc_h, surf_h, zon_h, mer_h, bot_h, out, sout, gout,
    trc, surf, zon, mer, bot, s_t, r_t, s_z, r_z, s_b, r_b, coef, st, rx, red, flat, mo, pw,
    in_sem, t_send, t_recv, z_send, z_recv, b_send, b_recv,
    st_send, st_recv, rx_send, rx_recv, rd_send, rd_recv, met,
):
    me = lax.axis_index("lon")
    grp = lax.axis_index("grp")
    levels = zon.shape[0]
    count = chunk_count(levels)
    size = levels // count
    side_dev = (lax.rem(me + n - 1, n), lax.rem(me + 1, n))
    outer = lax.rem(me, 2)
    inner = 1 - outer
    lane = lax.broadcasted_iota(jnp.int32, TILE, 1)
    row = lax.broadcasted_iota(jnp.int32, TILE, 0)
    last_lane, first_lane = lane == 127, lane == 0

    def north(x):
        rolled = pltpu.roll(x, 127, 1)
        return jnp.where(last_lane, pltpu.roll(rolled, 7, 0), rolled)

    def south(x):
        rolled = pltpu.roll(x, 1, 1)
        return jnp.where(first_lane, pltpu.roll(rolled, 1, 0), rolled)

    def col(c):
        return pl.ds(c, 8, stride=2)

    def lon_peer(s):
        return {"lon": lax.rem(me + s + n, n)}

    barrier = pltpu.get_barrier_semaphore()
    for s in NEAR:
        pl.semaphore_signal(barrier, inc=1, device_id=lon_peer(s), device_id_type=MESH)
    if share:
        pl.semaphore_signal(barrier, inc=1, device_id={"grp": 1 - grp}, device_id_type=MESH)

    half = levels // 2
    mine = pl.ds(grp * half if share else 0, half)
    theirs = pl.ds((1 - grp) * half, half) if share else pl.ds(half, levels - half)

    def chunk(g):
        return pl.ds(g * size, size)

    def in_chunk(g, body, carry):
        return lax.fori_loop(
            0, size, lambda i, state: body(g * size + i, state), carry, unroll=min(UNROLL, size)
        )

    def load(which, g):
        ks = chunk(g)
        src, dst = ((trc_h.at[:, ks], trc.at[:, ks]), (mer_h.at[ks], mer.at[ks]))[which]
        return pltpu.make_async_copy(src, dst, in_sem.at[which, g])

    load_zon = [
        pltpu.make_async_copy(zon_h.at[ks], zon.at[ks], in_sem.at[2, i])
        for i, ks in enumerate((mine, theirs))
    ]
    load_bot = pltpu.make_async_copy(bot_h, bot, in_sem.at[3, 0])
    load_surf = pltpu.make_async_copy(surf_h, surf, in_sem.at[3, 1])
    load_zon[0].start()
    load_bot.start()
    load_surf.start()
    load(0, 0).start()
    load_zon[1].start()
    for g in range(1, count):
        load(0, g).start()
    for g in range(count):
        load(1, g).start()
    def gather_chunk(g):
        load(0, g).wait()

        def step(k, carry):
            for c in range(2):
                s_t[c, k, 0] = trc[0, k, col(c), :]
                s_t[c, k, 1] = trc[1, k, col(c), :]
            return carry

        in_chunk(g, step, 0)

    def side_copy(src, dst, send, recv, g, side):
        return pltpu.make_async_remote_copy(
            src_ref=src.at[side, chunk(g)],
            dst_ref=dst.at[1 - side, chunk(g)],
            send_sem=send.at[side, g],
            recv_sem=recv.at[1 - side, g],
            device_id={"lon": side_dev[side]},
            device_id_type=MESH,
        )

    def t_copy(g, side):
        return side_copy(s_t, r_t, t_send, t_recv, g, side)

    def b_copy(g, side):
        return side_copy(s_b, r_b, b_send, b_recv, g, side)

    def gather_zonal(i):
        load_zon[i].wait()
        ks = (mine, theirs)[i]

        def step(k, carry):
            for c in range(2):
                s_z[c, ks.start + k] = zon[ks.start + k, col(c), :]
            return carry

        lax.fori_loop(0, ks.size, step, 0, unroll=5)

    def z_copy(which):
        if not share:
            return pltpu.make_async_remote_copy(
                src_ref=s_z.at[which],
                dst_ref=r_z.at[1 - which],
                send_sem=z_send.at[which],
                recv_sem=z_recv.at[which],
                device_id={"lon": side_dev[which]},
                device_id_type=MESH,
            )
        src, dst, dev = (
            (s_z.at[outer, mine], r_z.at[1 - outer, mine], lon_peer(2 * outer - 1)),
            (s_z.at[inner], r_z.at[1 - inner], lon_peer(2 * inner - 1)),
            (r_z.at[outer, mine], r_z.at[outer, mine], {"grp": 1 - grp}),
        )[which]
        return pltpu.make_async_remote_copy(
            src_ref=src,
            dst_ref=dst,
            send_sem=z_send.at[which],
            recv_sem=z_recv.at[which],
            device_id=dev,
            device_id_type=MESH,
        )

    def send_chunk(g):
        for side in range(2):
            t_copy(g, side).start()

    def shift_copy(buf, send, recv, s, part):
        return pltpu.make_async_remote_copy(
            src_ref=buf.at[0, part],
            dst_ref=buf.at[SLOT[s], part],
            send_sem=send.at[SLOT[s]],
            recv_sem=recv.at[SLOT[s]],
            device_id=lon_peer(s),
            device_id_type=MESH,
        )

    def shift_copies(buf, send, recv, cases, act):
        for s, usual, closing in cases:
            closes = me == (0 if act == "wait_recv" else n - s)
            if usual == closing:
                getattr(shift_copy(buf, send, recv, s, usual), act)()
                continue
            if usual is not None:

                @pl.when(jnp.logical_not(closes))
                def _():
                    getattr(shift_copy(buf, send, recv, s, usual), act)()

            @pl.when(closes)
            def _():
                getattr(shift_copy(buf, send, recv, s, closing), act)()

    every_tile = pl.ds(0, 6)
    st_near = ((1, pl.ds(0, 4), every_tile), (-1, pl.ds(2, 4), pl.ds(2, 4)))
    st_far = (
        (2, pl.ds(3, 1), every_tile),
        *((s, None, every_tile) for s in range(3, FAR + 1)),
        (FAR + 1, None, pl.ds(2, 2)),
        (FAR + 2, None, pl.ds(3, 1)),
    )
    rx_near = ((1, pl.ds(0, 4), pl.ds(0, 4)), (-1, pl.ds(0, 4), pl.ds(0, 4)))
    rx_second = ((2, pl.ds(2, 2), pl.ds(0, 4)),)
    rx_far = (
        *((s, None, pl.ds(0, 4)) for s in range(3, FAR + 2)),
        (FAR + 2, None, pl.ds(2, 2)),
    )

    def st_act(cases, act):
        shift_copies(st, st_send, st_recv, cases, act)

    def rx_act(cases, act):
        shift_copies(rx, rx_send, rx_recv, cases, act)

    near = me < n - FAR
    to_near = lax.rem(me + 2, n) < n - FAR

    gather_zonal(0)
    pl.semaphore_wait(barrier, len(NEAR) + (1 if share else 0))
    if share:
        z_copy(0).start()
    load_bot.wait()
    load_surf.wait()
    for c in range(2):
        d = bot[col(c), :].astype(jnp.float32)
        st[0, 2 + c] = d
        for v in range(2):
            st[0, (4, 0)[c] + v] = jnp.where(d > 0, surf[v, col(c), :], 0.0)
    st_act(st_near, "start")
    gather_chunk(0)
    send_chunk(0)
    gather_zonal(1)
    for which in range(1 if share else 0, 2):
        z_copy(which).start()
    rounds = spread_rounds(n)

    def spread(i):
        if i < len(rounds):
            for s in (rounds[i], -rounds[i]):
                pl.semaphore_signal(
                    met.at[i], inc=1, device_id=lon_peer(s), device_id_type=MESH
                )

    def spread_wait(i):
        if i < len(rounds):
            pl.semaphore_wait(met.at[i], 2)

    spread(0)

    @pl.loop(1, count)
    def _(g):
        gather_chunk(g)
        send_chunk(g)


    spread_wait(0)
    spread(1)
    st_act(st_near, "wait_recv")

    depths = {-2: st[1, 2], -1: st[1, 3], 0: st[0, 2], 1: st[0, 3]}
    depths.update({2: st[SLOT[-1], 2], 3: st[SLOT[-1], 3]})

    def y_face(i):
        wall = jnp.logical_and(last_lane, row == 7)
        return jnp.where(wall, 0.0, jnp.minimum(depths[i], north(depths[i])))

    def x_face(i):
        return jnp.minimum(depths[i], depths[i + 1])

    for which in range(2):
        z_copy(which).wait_recv()
    if share:
        z_copy(2).start()
        z_copy(2).wait_recv()
    quarter = TIME_STEP * 0.25
    diff = TIME_STEP * DIFFUSIVITY
    faces_x = [x_face(f - 1) for f in range(3)]
    faces_y = [y_face(c) for c in range(2)]
    own_depth = [depths[c] for c in range(2)]

    def first_chunk(g):
        load(1, g).wait()
        for side in range(2):
            t_copy(g, side).wait_recv()

        def first(k, carry):
            kf = k.astype(jnp.float32)
            z = (r_z[0, k], s_z[0, k], s_z[1, k], r_z[1, k])
            cx = []
            for f in range(3):
                open_f = kf < faces_x[f]
                u = quarter * (z[f] + z[f + 1])
                cx.append((jnp.where(open_f, u + diff, 0.0), jnp.where(open_f, u - diff, 0.0)))
            cy = []
            for c in range(2):
                open_f = kf < faces_y[c]
                m = mer[k, col(c), :]
                u = quarter * (m + north(m))
                cy.append((jnp.where(open_f, u + diff, 0.0), jnp.where(open_f, u - diff, 0.0)))
            for q, (lo, hi) in enumerate(cx + cy):
                coef[k, 2 * q] = lo
                coef[k, 2 * q + 1] = hi
            wet = [kf < own_depth[c] for c in range(2)]
            for v in range(2):
                t = (
                    r_t[0, k, v],
                    jnp.where(wet[0], s_t[0, k, v], 0.0),
                    jnp.where(wet[1], s_t[1, k, v], 0.0),
                    r_t[1, k, v],
                )
                fx = [cx[f][0] * t[f] + cx[f][1] * t[f + 1] for f in range(3)]
                for c in range(2):
                    fy = cy[c][0] * t[c + 1] + cy[c][1] * north(t[c + 1])
                    s_b[c, k, v] = t[c + 1] - ((fx[c + 1] - fx[c]) + (fy - south(fy)))
            return carry

        in_chunk(g, first, 0)
        for side in range(2):
            b_copy(g, side).start()

    pl.loop(0, count - count // 3)(first_chunk)
    spread_wait(1)
    spread(2)
    pl.loop(count - count // 3, count)(first_chunk)
    for i in range(2, len(rounds)):
        spread_wait(i)
        spread(i + 1)
    st_act(st_far, "start")

    face_x = {i: SURFACE_COUPLING * x_face(i) for i in range(-2, 3)}
    face_y = {i: SURFACE_COUPLING * y_face(i) for i in range(-2, 3)}
    face_s = {i: south(face_y[i]) for i in face_y}
    shared_faces = list(face_x)

    def lap(s, cols):
        gx = {i: face_x[i] * (s[i + 1] - s[i]) for i in range(cols[0] - 1, cols[-1] + 1)}
        res, rise = {}, {}
        for i in cols:
            rise[i] = north(s[i]) - s[i]
            fall = s[i] - south(s[i])
            res[i] = (gx[i - 1] - gx[i]) + (face_s[i] * fall - face_y[i] * rise[i])
        return res, rise

    height = [
        {-1: st[1, v], 0: st[0, 4 + v], 1: st[0, v], 2: st[SLOT[-1], 4 + v]}
        for v in range(2)
    ]
    lap_h = [lap(height[v], OWN)[0] for v in range(2)]

    zero = jnp.zeros(TILE, jnp.float32)

    def second_chunk(g, totals):
        for side in range(2):
            b_copy(g, side).wait_recv()

        def second(k, carry):
            sums, grams = list(carry[:4]), list(carry[4:])
            cx = [(coef[k, 2 * f], coef[k, 2 * f + 1]) for f in range(3)]
            cy = [(coef[k, 6 + 2 * c], coef[k, 7 + 2 * c]) for c in range(2)]
            new = []
            for v in range(2):
                t = (r_b[0, k, v], s_b[0, k, v], s_b[1, k, v], r_b[1, k, v])
                fx = [cx[f][0] * t[f] + cx[f][1] * t[f + 1] for f in range(3)]
                for c in range(2):
                    fy = cy[c][0] * t[c + 1] + cy[c][1] * north(t[c + 1])
                    val = t[c + 1] - ((fx[c + 1] - fx[c]) + (fy - south(fy)))
                    out[v, k, col(c), :] = val
                    sums[2 * v + c] = sums[2 * v + c] + val
                    new.append(val)
            grams[0] = grams[0] + (new[0] * new[0] + new[1] * new[1])
            grams[1] = grams[1] + (new[0] * new[2] + new[1] * new[3])
            grams[2] = grams[2] + (new[2] * new[2] + new[3] * new[3])
            return tuple(sums + grams)

        return in_chunk(g, second, totals)

    totals = lax.fori_loop(0, count, second_chunk, (zero,) * 7)

    gain = STERIC_GAIN / levels
    for v in range(2):
        for c in range(2):
            rx[0, 2 * c + v] = gain * totals[2 * v + c] - lap_h[v][c]
    rx_act(rx_far, "start")

    @pl.when(to_near)
    def _():
        rx_act(rx_second, "start")

    rx_act(rx_near, "start")
    st_act(st_far, "wait_recv")

    def add_faces(first, last):
        for i in range(first, last):
            face_x.setdefault(i, SURFACE_COUPLING * x_face(i))
        for i in range(first + 1, last):
            if i not in face_y:
                face_y[i] = SURFACE_COUPLING * y_face(i)
                face_s[i] = south(face_y[i])

    span = 4.0 * levels

    def operator_powers(v, cols):
        l1, rise0 = lap(r_cols[v], range(cols[0] - 2, cols[-1] + 2))
        l2, rise1 = lap(l1, range(cols[0] - 1, cols[-1] + 1))
        return r_cols[v], l1, l2, rise0, rise1

    def moments(cols, tall):
        def gathered(term):
            return functools.reduce(lambda a, b: a + b, [term(c) for c in cols])

        def dot(a, b):
            return gathered(lambda i: a[i] * b[i])

        parts, powers = {}, []
        for v in range(2):
            r, l1, l2, rise0, rise1 = operator_powers(v, cols)
            powers.append((r, l1, l2))
            rise2 = {i: north(l2[i]) - l2[i] for i in cols}
            for i, centre in enumerate(CENTRES):
                shift = centre * span
                if i:
                    b1 = {c: l1[c] - shift * r[c] for c in cols}
                    b2 = {
                        c: (l2[c] - 2.0 * shift * l1[c]) + shift * shift * r[c]
                        for c in range(cols[0] - 1, cols[-1] + 1)
                    }
                    up = {
                        c: (rise2[c] - 2.0 * shift * rise1[c]) + shift * shift * rise0[c]
                        for c in cols
                    }
                else:
                    b1, b2, up = l1, l2, rise2
                    parts["m", v, i, 0] = dot(r, r)
                parts["m", v, i, 1] = dot(r, b1)
                parts["m", v, i, 2] = dot(b1, b1)
                parts["m", v, i, 3] = dot(b1, b2)
                parts["m", v, i, 4] = dot(b2, b2)

                def energy(c):
                    across = b2[c] - b2[c - 1]
                    return face_x[c - 1] * across * across + face_y[c] * up[c] * up[c]

                parts["m", v, i, 5] = gathered(energy)
        for v in range(2):
            for w in range(2):
                for j in range(3):
                    parts["h", v, w, j] = dot(tall[v], powers[w][j])
        for k in range(5):
            parts["c", k] = dot(powers[0][k // 2], powers[1][(k + 1) // 2])
        return parts, powers

    def keep_powers(powers):
        for v in range(2):
            for j in range(3):
                for c in OWN:
                    pw[v, j, c] = powers[v][j][c]

    def take_r(slot):
        for v in range(2):
            for c in range(2):
                r_cols[v][(2 if slot == SLOT[-1] else -2 * slot) + c] = rx[slot, 2 * c + v]

    r_cols = [{}, {}]

    def forget():
        for known in (face_x, face_y, face_s):
            for i in [i for i in known if i not in shared_faces]:
                del known[i]

    def closing_moments():
        tall = [{}, {}]
        for slot in range(FAR + 3):
            take_r(slot)
            for c in range(2):
                depths[c - 2 * slot] = st[slot, 2 + c]
        take_r(SLOT[-1])
        for slot in range(FAR + 1):
            for v in range(2):
                tall[v].update({-2 * slot: st[slot, 4 + v], 1 - 2 * slot: st[slot, v]})
        cols = range(-2 * FAR, 2)
        add_faces(cols[0] - 3, cols[-1] + 2)
        return moments(cols, tall)

    forget()

    @pl.when(jnp.logical_and(near, me != 0))
    def _():
        rx_act(rx_near + rx_second, "wait_recv")
        depths[-3] = st[2, 3]
        add_faces(-3, 3)
        for slot in (0, 1, SLOT[-1]):
            take_r(slot)
        for v in range(2):
            r_cols[v][-3] = rx[2, 2 + v]
        parts, powers = moments(OWN, height)
        for q, name in enumerate(MOMENTS):
            mo[q] = parts[name]
        keep_powers(powers)

    @pl.when(jnp.logical_not(near))
    def _():
        for q in range(len(MOMENTS)):
            mo[q] = zero

    forget()

    @pl.when(me == 0)
    def _():
        rx_act(rx_near + rx_second + rx_far, "wait_recv")
        parts, powers = closing_moments()
        for q, name in enumerate(MOMENTS):
            mo[q] = parts[name]
        keep_powers(powers)

    forget()

    def dot(a, b):
        return a[0] * b[0] + a[1] * b[1]

    parts = {}
    for q in range(3):
        parts["gram", q] = totals[4 + q]
    parts["hh", 0] = dot(height[0], height[0])
    parts["hh", 1] = dot(height[1], height[1])
    parts["hh", 2] = dot(height[0], height[1])
    for q, name in enumerate(MOMENTS):
        parts[name] = mo[q]

    names = list(parts)
    place = lane - 16 * row
    local = zero
    for q in range(0, len(names), 8):
        level = [parts[name] for name in names[q : q + 8]]
        for shift in (1, 2, 4):
            even = jnp.bitwise_and(row, shift) == 0
            merged = []
            for i in range(0, len(level), 2):
                a, b = level[i], level[min(i + 1, len(level) - 1)]
                merged.append(jnp.where(even, a, b) + pltpu.roll(jnp.where(even, b, a), shift, 0))
            level = merged
        local = jnp.where(place == q // 8, jnp.sum(level[0], axis=1, keepdims=True), local)
    for shift in (4, 2, 1):
        local = local + pltpu.roll(local, shift, 0)
    red[me] = local[0:1]

    def red_copy(i):
        return pltpu.make_async_remote_copy(
            src_ref=red.at[me],
            dst_ref=red.at[me],
            send_sem=rd_send,
            recv_sem=rd_recv,
            device_id=lon_peer(i),
            device_id_type=MESH,
        )

    def every(sem):
        return pltpu.make_async_copy(red.at[pl.ds(0, n - 1)], red.at[pl.ds(0, n - 1)], sem)

    peers_loop(n, lambda i: red_copy(i).start())

    @pl.when(jnp.logical_not(near))
    def _():
        rx_act(rx_near, "wait_recv")
        for slot in (0, 1, SLOT[-1]):
            take_r(slot)
        powers = []
        for v in range(2):
            l1 = lap(r_cols[v], range(-1, 3))[0]
            powers.append((r_cols[v], l1, lap(l1, OWN)[0]))
        keep_powers(powers)

    every(rd_recv).wait()
    terms = [red[i] for i in range(n)]
    while len(terms) > 1:
        terms = [
            terms[i] + terms[i + 1] if i + 1 < len(terms) else terms[i]
            for i in range(0, len(terms), 2)
        ]
    every_row = jnp.broadcast_to(terms[0], TILE)
    for q in range(-(-len(names) // 8)):
        picked = jnp.where(place == q, every_row, 0.0)
        flat[q] = jnp.broadcast_to(jnp.sum(picked, axis=1, keepdims=True), TILE)
    total = {
        name: jnp.broadcast_to(flat[q // 8, q % 8 : q % 8 + 1], TILE)
        for q, name in enumerate(names)
    }

    coefs = []
    for v in range(2):
        m0 = total["m", v, 0, 0]
        m = [m0] + [total["m", v, 0, k] for k in range(1, 6)]
        first_moment = m[1]
        centre = zero
        for i in range(1, len(CENTRES)):
            limit = 0.5 * (CENTRES[i] + CENTRES[i - 1]) * span
            above = first_moment > limit * m0
            centre = jnp.where(above, CENTRES[i] * span, centre)
            m = [m0] + [jnp.where(above, total["m", v, i, k], m[k]) for k in range(1, 6)]
        unit = 1.0 + centre
        a = [unit * m[k] + m[k + 1] for k in range(4)] + [m[4] + m[5]]
        ratio = m[1] / m0
        step0 = m0 / a[0]
        rr1 = step0 * step0 * (m[2] - ratio * m[1])
        beta0 = rr1 / m0
        along = step0 * ratio + beta0
        p1ap1 = along * along * a[0] - 2.0 * along * step0 * a[1] + step0 * step0 * a[2]
        step1 = rr1 / p1ap1
        x0 = step0 * ratio - step1 * along * unit
        x1 = step1 * step0 * unit - (step0 + step1 * along)
        x2 = step1 * step0

        def form(y0, y1, y2, f):
            return (
                y0 * (y0 * f[0] + 2.0 * (y1 * f[1] + y2 * f[2]))
                + y1 * (y1 * f[2] + 2.0 * (y2 * f[3]))
                + y2 * (y2 * f[4])
            )

        rr2 = form(x0, x1, x2, m)
        beta1 = rr2 / rr1
        y0, y1, y2 = x0 + beta1 * along, x1 - beta1 * step0, x2
        step2 = rr2 / form(y0, y1, y2, a)
        e0 = step0 + step1 * along + step2 * y0
        e1 = step2 * y1 - step1 * step0
        e2 = step2 * y2
        coefs.append((e0 - centre * (e1 - centre * e2), e1 - 2.0 * centre * e2, e2))
        for c in OWN:
            w = coefs[v]
            s = pw[v, 0, c] * w[0] + (pw[v, 1, c] * w[1] + pw[v, 2, c] * w[2])
            sout[v, col(c), :] = height[v][c] + s

    def plain(v, k):
        return total["m", v, 0, k]

    gram = []
    for v in range(2):
        w = coefs[v]
        s = total["hh", v] + 2.0 * sum(w[j] * total["h", v, v, j] for j in range(3))
        for i in range(3):
            for j in range(3):
                s = s + w[i] * w[j] * plain(v, i + j)
        gram.append(total["gram", 2 * v] + s)
    mix = total["gram", 1] + total["hh", 2]
    for j in range(3):
        mix = mix + (coefs[1][j] * total["h", 0, 1, j] + coefs[0][j] * total["h", 1, 0, j])
    for i in range(3):
        for j in range(3):
            mix = mix + coefs[0][i] * coefs[1][j] * total["c", i + j]
    cells = float((levels + 1) * 2 * 8 * 128 * n)
    gram_one, gram_two, gram_mix = gram[0] / cells, gram[1] / cells, mix / cells
    scale_one = jnp.sqrt(gram_one + EPSILON)
    cross = gram_mix / scale_one
    rest = gram_two - 2.0 * cross * cross + cross * cross * gram_one / (gram_one + EPSILON)
    scale_two = jnp.sqrt(jnp.maximum(rest, 0.0) + EPSILON)
    gout[0] = 1.0 / scale_one
    gout[1] = cross
    gout[2] = 1.0 / scale_two
    gout[3] = jnp.where(lane == 0, scale_one, jnp.where(lane == 1, cross, scale_two))


    @pl.loop(0, count)
    def _(g):
        for side in range(2):
            t_copy(g, side).wait_send()
            b_copy(g, side).wait_send()

    for which in range(3 if share else 2):
        z_copy(which).wait_send()
    st_act(st_near + st_far, "wait_send")
    rx_act(rx_near + rx_far, "wait_send")

    @pl.when(to_near)
    def _():
        rx_act(rx_second, "wait_send")

    every(rd_send).wait()


def scale_kernel(trc, surf, tail, out_h, sout_h, gout_h, out, sout, gvec, sem):
    levels = trc.shape[1]
    count = chunk_count(levels)
    size = levels // count
    one, cross, two = tail[0], tail[1], tail[2]
    gvec[...] = tail[3, 0, :3]
    grow = pltpu.make_async_copy(gvec, gout_h, sem.at[count + 1])
    grow.start()

    def store(g):
        ks = pl.ds(g * size, size)
        return pltpu.make_async_copy(out.at[:, ks], out_h.at[:, ks], sem.at[g])

    @pl.loop(0, count)
    def _(g):
        def step(i, carry):
            k = g * size + i
            for h in range(2):
                rows = pl.ds(8 * h, 8)
                unit = trc[0, k, rows, :] * one
                out[0, k, rows, :] = unit
                out[1, k, rows, :] = (trc[1, k, rows, :] - cross * unit) * two
            return carry

        lax.fori_loop(0, size, step, 0, unroll=min(UNROLL, size))
        store(g).start()

    for h in range(2):
        rows = pl.ds(8 * h, 8)
        unit = surf[0, rows, :] * one
        sout[0, rows, :] = unit
        sout[1, rows, :] = (surf[1, rows, :] - cross * unit) * two
    last = pltpu.make_async_copy(sout, sout_h, sem.at[count])
    last.start()
    for g in range(count):
        store(g).wait()
    last.wait()
    grow.wait()


def packed(x):
    lead, (cols, rows) = x.shape[:-2], x.shape[-2:]
    x = x.reshape(lead + (cols, rows // 128, 128))
    x = jnp.swapaxes(x, -3, -2)
    return x.reshape(lead + (cols * (rows // 128), 128))


def unpacked(x, cols):
    lead, (rows, lanes) = x.shape[:-2], x.shape[-2:]
    x = x.reshape(lead + (rows // cols, cols, lanes))
    x = jnp.swapaxes(x, -3, -2)
    return x.reshape(lead + (cols, rows // cols * lanes))


def on_device(n, groups, tracer_pert, surface_pert, zonal_flow, merid_flow, bottom_level):
    vectors, levels, columns, rows = tracer_pert.shape
    count = chunk_count(levels)
    share = shares_zonal(groups, levels)
    f32 = jnp.float32
    vmem = pl.BlockSpec(memory_space=pltpu.VMEM)
    hbm = pl.BlockSpec(memory_space=pltpu.HBM)
    dma = pltpu.SemaphoreType.DMA
    zonal_sems = 3 if share else 2
    tracer, surface, tail = pl.pallas_call(
        functools.partial(kernel, n, share),
        out_shape=(
            jax.ShapeDtypeStruct((vectors, levels, 16, 128), f32),
            jax.ShapeDtypeStruct((vectors, 16, 128), f32),
            jax.ShapeDtypeStruct((4, 8, 128), f32),
        ),
        in_specs=[hbm] * 5,
        out_specs=(vmem,) * 3,
        scratch_shapes=[
            pltpu.VMEM((vectors, levels, 16, 128), f32),
            pltpu.VMEM((vectors, 16, 128), f32),
            pltpu.VMEM((levels, 16, 128), f32),
            pltpu.VMEM((levels, 16, 128), f32),
            pltpu.VMEM((16, 128), jnp.int32),
            pltpu.VMEM((2, levels, 2, 8, 128), f32),
            pltpu.VMEM((2, levels, 2, 8, 128), f32),
            pltpu.VMEM((2, levels, 8, 128), f32),
            pltpu.VMEM((2, levels, 8, 128), f32),
            pltpu.VMEM((2, levels, 2, 8, 128), f32),
            pltpu.VMEM((2, levels, 2, 8, 128), f32),
            pltpu.VMEM((levels, 10, 8, 128), f32),
            pltpu.VMEM((len(SLOT), 6, 8, 128), f32),
            pltpu.VMEM((len(SLOT), 4, 8, 128), f32),
            pltpu.VMEM((n, 1, 128), f32),
            pltpu.VMEM((16, 8, 128), f32),
            pltpu.VMEM((len(MOMENTS), 8, 128), f32),
            pltpu.VMEM((2, 3, 2, 8, 128), f32),
            dma((4, max(2, count))),
            dma((2, count)),
            dma((2, count)),
            dma((zonal_sems,)),
            dma((zonal_sems,)),
            dma((2, count)),
            dma((2, count)),
            dma((len(SLOT),)),
            dma((len(SLOT),)),
            dma((len(SLOT),)),
            dma((len(SLOT),)),
            dma(()),
            dma(()),
            pltpu.SemaphoreType.REGULAR((max(1, len(spread_rounds(n))),)),
        ],
        compiler_params=pltpu.CompilerParams(
            collective_id=0, has_side_effects=True, vmem_limit_bytes=40 * 1024 * 1024
        ),
    )(
        *(
            pltpu.with_memory_space_constraint(packed(x), pltpu.HBM)
            for x in (tracer_pert, surface_pert, zonal_flow, merid_flow, bottom_level)
        )
    )
    tracer, surface, growth = pl.pallas_call(
        scale_kernel,
        out_shape=(
            jax.ShapeDtypeStruct((vectors, levels, 16, 128), f32),
            jax.ShapeDtypeStruct((vectors, 16, 128), f32),
            jax.ShapeDtypeStruct((3,), f32),
        ),
        in_specs=[vmem] * 3,
        out_specs=(hbm,) * 3,
        scratch_shapes=[
            pltpu.VMEM((vectors, levels, 16, 128), f32),
            pltpu.VMEM((vectors, 16, 128), f32),
            pltpu.VMEM((3,), f32),
            dma((count + 2,)),
        ],
        compiler_params=pltpu.CompilerParams(vmem_limit_bytes=16 * 1024 * 1024),
    )(tracer, surface, tail)
    return unpacked(tracer, columns), unpacked(surface, columns), growth


def solution(mesh):
    placed = (
        P("grp", None, "lon", None),
        P("grp", "lon", None),
        P(None, "lon", None),
        P(None, "lon", None),
        P("lon", None),
    )
    return jax.shard_map(
        functools.partial(on_device, mesh.shape["lon"], mesh.shape["grp"]),
        mesh=mesh,
        in_specs=placed,
        out_specs=(P("grp", None, "lon", None), P("grp", "lon", None), P("grp")),
        check_vma=False,
    )
```

```python
import functools

import jax
import jax.numpy as jnp
from jax import lax
from jax.experimental import pallas as pl
from jax.experimental.pallas import tpu as pltpu
from jax.sharding import PartitionSpec as P

DIFFUSIVITY = 0.5
TIME_STEP = 0.2
SURFACE_COUPLING = 0.5
STERIC_GAIN = 2.0
EPSILON = 1e-06
MESH = pl.DeviceIdType.MESH
CHUNKS = 5
UNROLL = 10
NEAR = (1, -1)
CENTRES = (0.0, 0.04, 0.16, 0.64)
FAR = 4
SLOT = {0: 0, **{s: s for s in range(1, FAR + 3)}, -1: FAR + 3}
OWN = (0, 1)
MOMENTS = (
    [("m", v, i, k) for v in range(2) for i in range(len(CENTRES)) for k in range(1 if i else 0, 6)]
    + [("h", v, w, j) for v in range(2) for w in range(2) for j in range(3)]
    + [("c", k) for k in range(5)]
)
TILE = (8, 128)


def chunk_count(levels):
    return max(c for c in range(1, CHUNKS + 1) if levels % c == 0)


def spread_rounds(n):
    reach, rounds = 1, []
    while 2 * reach < n:
        rounds.append(reach)
        reach *= 2
    return rounds


def shares_zonal(groups, levels):
    return groups == 2 and levels % 2 == 0


def peers_loop(n, body):
    if n <= 16:
        for i in range(1, n):
            body(i)
    else:

        def step(i, carry):
            body(i)
            return carry

        lax.fori_loop(1, n, step, 0)


def kernel(
    n, share, trc_h, surf_h, zon_h, mer_h, bot_h, out, sout, gout,
    trc, surf, zon, mer, bot, s_t, r_t, s_z, r_z, s_b, r_b, coef, st, rx, red, flat, mo, pw,
    in_sem, t_send, t_recv, z_send, z_recv, b_send, b_recv,
    st_send, st_recv, rx_send, rx_recv, rd_send, rd_recv, met,
):
    me = lax.axis_index("lon")
    grp = lax.axis_index("grp")
    levels = zon.shape[0]
    count = chunk_count(levels)
    size = levels // count
    side_dev = (lax.rem(me + n - 1, n), lax.rem(me + 1, n))
    outer = lax.rem(me, 2)
    inner = 1 - outer
    lane = lax.broadcasted_iota(jnp.int32, TILE, 1)
    row = lax.broadcasted_iota(jnp.int32, TILE, 0)
    last_lane, first_lane = lane == 127, lane == 0

    def north(x):
        rolled = pltpu.roll(x, 127, 1)
        return jnp.where(last_lane, pltpu.roll(rolled, 7, 0), rolled)

    def south(x):
        rolled = pltpu.roll(x, 1, 1)
        return jnp.where(first_lane, pltpu.roll(rolled, 1, 0), rolled)

    def col(c):
        return pl.ds(c, 8, stride=2)

    def lon_peer(s):
        return {"lon": lax.rem(me + s + n, n)}

    barrier = pltpu.get_barrier_semaphore()
    for s in NEAR:
        pl.semaphore_signal(barrier, inc=1, device_id=lon_peer(s), device_id_type=MESH)
    if share:
        pl.semaphore_signal(barrier, inc=1, device_id={"grp": 1 - grp}, device_id_type=MESH)

    half = levels // 2
    mine = pl.ds(grp * half if share else 0, half)
    theirs = pl.ds((1 - grp) * half, half) if share else pl.ds(half, levels - half)

    def chunk(g):
        return pl.ds(g * size, size)

    def in_chunk(g, body, carry):
        return lax.fori_loop(
            0, size, lambda i, state: body(g * size + i, state), carry, unroll=min(UNROLL, size)
        )

    def load(g):
        return pltpu.make_async_copy(trc_h.at[:, chunk(g)], trc.at[:, chunk(g)], in_sem.at[5 + g])

    load_zon = [
        pltpu.make_async_copy(zon_h.at[ks], zon.at[ks], in_sem.at[i])
        for i, ks in enumerate((mine, theirs))
    ]
    load_bot = pltpu.make_async_copy(bot_h, bot, in_sem.at[2])
    load_surf = pltpu.make_async_copy(surf_h, surf, in_sem.at[3])
    load_mer = pltpu.make_async_copy(mer_h, mer, in_sem.at[4])
    load_zon[0].start()
    load_bot.start()
    load_surf.start()
    load(0).start()
    load_zon[1].start()
    for g in range(1, count):
        load(g).start()
    load_mer.start()
    def gather_chunk(g):
        load(g).wait()

        def step(k, carry):
            for c in range(2):
                s_t[c, k, 0] = trc[0, k, col(c), :]
                s_t[c, k, 1] = trc[1, k, col(c), :]
            return carry

        in_chunk(g, step, 0)

    def side_copy(src, dst, send, recv, g, side):
        return pltpu.make_async_remote_copy(
            src_ref=src.at[side, chunk(g)],
            dst_ref=dst.at[1 - side, chunk(g)],
            send_sem=send,
            recv_sem=recv.at[1 - side, g],
            device_id={"lon": side_dev[side]},
            device_id_type=MESH,
        )

    def t_copy(g, side):
        return side_copy(s_t, r_t, t_send, t_recv, g, side)

    def b_copy(g, side):
        return side_copy(s_b, r_b, b_send, b_recv, g, side)

    def gather_zonal(i):
        load_zon[i].wait()
        ks = (mine, theirs)[i]

        def step(k, carry):
            for c in range(2):
                s_z[c, ks.start + k] = zon[ks.start + k, col(c), :]
            return carry

        lax.fori_loop(0, ks.size, step, 0, unroll=5)

    def z_copy(which):
        if not share:
            return pltpu.make_async_remote_copy(
                src_ref=s_z.at[which],
                dst_ref=r_z.at[1 - which],
                send_sem=z_send.at[which],
                recv_sem=z_recv.at[which],
                device_id={"lon": side_dev[which]},
                device_id_type=MESH,
            )
        src, dst, dev = (
            (s_z.at[outer, mine], r_z.at[1 - outer, mine], lon_peer(2 * outer - 1)),
            (s_z.at[inner], r_z.at[1 - inner], lon_peer(2 * inner - 1)),
            (r_z.at[outer, mine], r_z.at[outer, mine], {"grp": 1 - grp}),
        )[which]
        return pltpu.make_async_remote_copy(
            src_ref=src,
            dst_ref=dst,
            send_sem=z_send.at[which],
            recv_sem=z_recv.at[which],
            device_id=dev,
            device_id_type=MESH,
        )

    def send_chunk(g):
        for side in range(2):
            t_copy(g, side).start()

    def shift_copy(buf, send, recv, s, part):
        return pltpu.make_async_remote_copy(
            src_ref=buf.at[0, part],
            dst_ref=buf.at[SLOT[s], part],
            send_sem=send.at[SLOT[s]],
            recv_sem=recv.at[SLOT[s]],
            device_id=lon_peer(s),
            device_id_type=MESH,
        )

    def shift_copies(buf, send, recv, cases, act):
        for s, usual, closing in cases:
            closes = me == (0 if act == "wait_recv" else n - s)
            if usual == closing:
                getattr(shift_copy(buf, send, recv, s, usual), act)()
                continue
            if usual is not None:

                @pl.when(jnp.logical_not(closes))
                def _():
                    getattr(shift_copy(buf, send, recv, s, usual), act)()

            @pl.when(closes)
            def _():
                getattr(shift_copy(buf, send, recv, s, closing), act)()

    every_tile = pl.ds(0, 6)
    st_near = ((1, pl.ds(0, 4), every_tile), (-1, pl.ds(2, 4), pl.ds(2, 4)))
    st_far = (
        (2, pl.ds(3, 1), every_tile),
        *((s, None, every_tile) for s in range(3, FAR + 1)),
        (FAR + 1, None, pl.ds(2, 2)),
        (FAR + 2, None, pl.ds(3, 1)),
    )
    rx_near = ((1, pl.ds(0, 4), pl.ds(0, 4)), (-1, pl.ds(0, 4), pl.ds(0, 4)))
    rx_second = ((2, pl.ds(2, 2), pl.ds(0, 4)),)
    rx_far = (
        *((s, None, pl.ds(0, 4)) for s in range(3, FAR + 2)),
        (FAR + 2, None, pl.ds(2, 2)),
    )

    def st_act(cases, act):
        shift_copies(st, st_send, st_recv, cases, act)

    def rx_act(cases, act):
        shift_copies(rx, rx_send, rx_recv, cases, act)

    near = me < n - FAR
    to_near = lax.rem(me + 2, n) < n - FAR

    gather_zonal(0)
    pl.semaphore_wait(barrier, len(NEAR) + (1 if share else 0))
    if share:
        z_copy(0).start()
    load_bot.wait()
    load_surf.wait()
    for c in range(2):
        d = bot[col(c), :].astype(jnp.float32)
        st[0, 2 + c] = d
        for v in range(2):
            st[0, (4, 0)[c] + v] = jnp.where(d > 0, surf[v, col(c), :], 0.0)
    st_act(st_near, "start")
    gather_chunk(0)
    send_chunk(0)
    gather_zonal(1)
    for which in range(1 if share else 0, 2):
        z_copy(which).start()
    rounds = spread_rounds(n)

    def spread(i):
        if i < len(rounds):
            for s in (rounds[i], -rounds[i]):
                pl.semaphore_signal(
                    met.at[i], inc=1, device_id=lon_peer(s), device_id_type=MESH
                )

    def spread_wait(i):
        if i < len(rounds):
            pl.semaphore_wait(met.at[i], 2)

    spread(0)

    @pl.loop(1, count)
    def _(g):
        gather_chunk(g)
        send_chunk(g)


    spread_wait(0)
    spread(1)
    st_act(st_near, "wait_recv")

    depths = {-2: st[1, 2], -1: st[1, 3], 0: st[0, 2], 1: st[0, 3]}
    depths.update({2: st[SLOT[-1], 2], 3: st[SLOT[-1], 3]})

    def y_face(i):
        wall = jnp.logical_and(last_lane, row == 7)
        return jnp.where(wall, 0.0, jnp.minimum(depths[i], north(depths[i])))

    def x_face(i):
        return jnp.minimum(depths[i], depths[i + 1])

    for which in range(2):
        z_copy(which).wait_recv()
    if share:
        z_copy(2).start()
        z_copy(2).wait_recv()
    quarter = TIME_STEP * 0.25
    diff = TIME_STEP * DIFFUSIVITY
    faces_x = [x_face(f - 1) for f in range(3)]
    faces_y = [y_face(c) for c in range(2)]
    own_depth = [depths[c] for c in range(2)]

    load_mer.wait()

    def first_chunk(g):
        for side in range(2):
            t_copy(g, side).wait_recv()

        def first(k, carry):
            kf = k.astype(jnp.float32)
            z = (r_z[0, k], s_z[0, k], s_z[1, k], r_z[1, k])
            cx = []
            for f in range(3):
                open_f = kf < faces_x[f]
                u = quarter * (z[f] + z[f + 1])
                cx.append((jnp.where(open_f, u + diff, 0.0), jnp.where(open_f, u - diff, 0.0)))
            cy = []
            for c in range(2):
                open_f = kf < faces_y[c]
                m = mer[k, col(c), :]
                u = quarter * (m + north(m))
                cy.append((jnp.where(open_f, u + diff, 0.0), jnp.where(open_f, u - diff, 0.0)))
            for q, (lo, hi) in enumerate(cx + cy):
                coef[k, 2 * q] = lo
                coef[k, 2 * q + 1] = hi
            wet = [kf < own_depth[c] for c in range(2)]
            for v in range(2):
                t = (
                    r_t[0, k, v],
                    jnp.where(wet[0], s_t[0, k, v], 0.0),
                    jnp.where(wet[1], s_t[1, k, v], 0.0),
                    r_t[1, k, v],
                )
                fx = [cx[f][0] * t[f] + cx[f][1] * t[f + 1] for f in range(3)]
                for c in range(2):
                    fy = cy[c][0] * t[c + 1] + cy[c][1] * north(t[c + 1])
                    s_b[c, k, v] = t[c + 1] - ((fx[c + 1] - fx[c]) + (fy - south(fy)))
            return carry

        in_chunk(g, first, 0)
        for side in range(2):
            b_copy(g, side).start()

    pl.loop(0, count - count // 3)(first_chunk)
    spread_wait(1)
    spread(2)
    pl.loop(count - count // 3, count)(first_chunk)
    for i in range(2, len(rounds)):
        spread_wait(i)
        spread(i + 1)
    st_act(st_far, "start")

    face_x = {i: SURFACE_COUPLING * x_face(i) for i in range(-2, 3)}
    face_y = {i: SURFACE_COUPLING * y_face(i) for i in range(-2, 3)}
    face_s = {i: south(face_y[i]) for i in face_y}
    shared_faces = list(face_x)

    def lap(s, cols):
        gx = {i: face_x[i] * (s[i + 1] - s[i]) for i in range(cols[0] - 1, cols[-1] + 1)}
        res, rise = {}, {}
        for i in cols:
            rise[i] = north(s[i]) - s[i]
            fall = s[i] - south(s[i])
            res[i] = (gx[i - 1] - gx[i]) + (face_s[i] * fall - face_y[i] * rise[i])
        return res, rise

    height = [
        {-1: st[1, v], 0: st[0, 4 + v], 1: st[0, v], 2: st[SLOT[-1], 4 + v]}
        for v in range(2)
    ]
    lap_h = [lap(height[v], OWN)[0] for v in range(2)]

    zero = jnp.zeros(TILE, jnp.float32)

    def second_chunk(g, totals):
        for side in range(2):
            b_copy(g, side).wait_recv()

        def second(k, carry):
            sums, grams = list(carry[:4]), list(carry[4:])
            cx = [(coef[k, 2 * f], coef[k, 2 * f + 1]) for f in range(3)]
            cy = [(coef[k, 6 + 2 * c], coef[k, 7 + 2 * c]) for c in range(2)]
            new = []
            for v in range(2):
                t = (r_b[0, k, v], s_b[0, k, v], s_b[1, k, v], r_b[1, k, v])
                fx = [cx[f][0] * t[f] + cx[f][1] * t[f + 1] for f in range(3)]
                for c in range(2):
                    fy = cy[c][0] * t[c + 1] + cy[c][1] * north(t[c + 1])
                    val = t[c + 1] - ((fx[c + 1] - fx[c]) + (fy - south(fy)))
                    out[v, k, col(c), :] = val
                    sums[2 * v + c] = sums[2 * v + c] + val
                    new.append(val)
            grams[0] = grams[0] + (new[0] * new[0] + new[1] * new[1])
            grams[1] = grams[1] + (new[0] * new[2] + new[1] * new[3])
            grams[2] = grams[2] + (new[2] * new[2] + new[3] * new[3])
            return tuple(sums + grams)

        return in_chunk(g, second, totals)

    totals = lax.fori_loop(0, count, second_chunk, (zero,) * 7)

    gain = STERIC_GAIN / levels
    for v in range(2):
        for c in range(2):
            rx[0, 2 * c + v] = gain * totals[2 * v + c] - lap_h[v][c]
    rx_act(rx_far, "start")

    @pl.when(to_near)
    def _():
        rx_act(rx_second, "start")

    rx_act(rx_near, "start")
    st_act(st_far, "wait_recv")

    def add_faces(first, last):
        for i in range(first, last):
            face_x.setdefault(i, SURFACE_COUPLING * x_face(i))
        for i in range(first + 1, last):
            if i not in face_y:
                face_y[i] = SURFACE_COUPLING * y_face(i)
                face_s[i] = south(face_y[i])

    span = 4.0 * levels

    def operator_powers(v, cols):
        l1, rise0 = lap(r_cols[v], range(cols[0] - 2, cols[-1] + 2))
        l2, rise1 = lap(l1, range(cols[0] - 1, cols[-1] + 1))
        return r_cols[v], l1, l2, rise0, rise1

    def moments(cols, tall):
        def gathered(term):
            return functools.reduce(lambda a, b: a + b, [term(c) for c in cols])

        def dot(a, b):
            return gathered(lambda i: a[i] * b[i])

        parts, powers = {}, []
        for v in range(2):
            r, l1, l2, rise0, rise1 = operator_powers(v, cols)
            powers.append((r, l1, l2))
            rise2 = {i: north(l2[i]) - l2[i] for i in cols}
            for i, centre in enumerate(CENTRES):
                shift = centre * span
                if i:
                    b1 = {c: l1[c] - shift * r[c] for c in cols}
                    b2 = {
                        c: (l2[c] - 2.0 * shift * l1[c]) + shift * shift * r[c]
                        for c in range(cols[0] - 1, cols[-1] + 1)
                    }
                    up = {
                        c: (rise2[c] - 2.0 * shift * rise1[c]) + shift * shift * rise0[c]
                        for c in cols
                    }
                else:
                    b1, b2, up = l1, l2, rise2
                    parts["m", v, i, 0] = dot(r, r)
                parts["m", v, i, 1] = dot(r, b1)
                parts["m", v, i, 2] = dot(b1, b1)
                parts["m", v, i, 3] = dot(b1, b2)
                parts["m", v, i, 4] = dot(b2, b2)

                def energy(c):
                    across = b2[c] - b2[c - 1]
                    return face_x[c - 1] * across * across + face_y[c] * up[c] * up[c]

                parts["m", v, i, 5] = gathered(energy)
        for v in range(2):
            for w in range(2):
                for j in range(3):
                    parts["h", v, w, j] = dot(tall[v], powers[w][j])
        for k in range(5):
            parts["c", k] = dot(powers[0][k // 2], powers[1][(k + 1) // 2])
        return parts, powers

    def keep_powers(powers):
        for v in range(2):
            for j in range(3):
                for c in OWN:
                    pw[v, j, c] = powers[v][j][c]

    def take_r(slot):
        for v in range(2):
            for c in range(2):
                r_cols[v][(2 if slot == SLOT[-1] else -2 * slot) + c] = rx[slot, 2 * c + v]

    r_cols = [{}, {}]

    def forget():
        for known in (face_x, face_y, face_s):
            for i in [i for i in known if i not in shared_faces]:
                del known[i]

    def closing_moments():
        tall = [{}, {}]
        for slot in range(FAR + 3):
            take_r(slot)
            for c in range(2):
                depths[c - 2 * slot] = st[slot, 2 + c]
        take_r(SLOT[-1])
        for slot in range(FAR + 1):
            for v in range(2):
                tall[v].update({-2 * slot: st[slot, 4 + v], 1 - 2 * slot: st[slot, v]})
        cols = range(-2 * FAR, 2)
        add_faces(cols[0] - 3, cols[-1] + 2)
        return moments(cols, tall)

    forget()

    @pl.when(jnp.logical_and(near, me != 0))
    def _():
        rx_act(rx_near + rx_second, "wait_recv")
        depths[-3] = st[2, 3]
        add_faces(-3, 3)
        for slot in (0, 1, SLOT[-1]):
            take_r(slot)
        for v in range(2):
            r_cols[v][-3] = rx[2, 2 + v]
        parts, powers = moments(OWN, height)
        for q, name in enumerate(MOMENTS):
            mo[q] = parts[name]
        keep_powers(powers)

    @pl.when(jnp.logical_not(near))
    def _():
        for q in range(len(MOMENTS)):
            mo[q] = zero

    forget()

    @pl.when(me == 0)
    def _():
        rx_act(rx_near + rx_second + rx_far, "wait_recv")
        parts, powers = closing_moments()
        for q, name in enumerate(MOMENTS):
            mo[q] = parts[name]
        keep_powers(powers)

    forget()

    def dot(a, b):
        return a[0] * b[0] + a[1] * b[1]

    parts = {}
    for q in range(3):
        parts["gram", q] = totals[4 + q]
    parts["hh", 0] = dot(height[0], height[0])
    parts["hh", 1] = dot(height[1], height[1])
    parts["hh", 2] = dot(height[0], height[1])
    for q, name in enumerate(MOMENTS):
        parts[name] = mo[q]

    names = list(parts)
    place = lane - 16 * row
    local = zero
    for q in range(0, len(names), 8):
        level = [parts[name] for name in names[q : q + 8]]
        for shift in (1, 2, 4):
            even = jnp.bitwise_and(row, shift) == 0
            merged = []
            for i in range(0, len(level), 2):
                a, b = level[i], level[min(i + 1, len(level) - 1)]
                merged.append(jnp.where(even, a, b) + pltpu.roll(jnp.where(even, b, a), shift, 0))
            level = merged
        local = jnp.where(place == q // 8, jnp.sum(level[0], axis=1, keepdims=True), local)
    for shift in (4, 2, 1):
        local = local + pltpu.roll(local, shift, 0)
    red[me] = local[0:1]

    def red_copy(i):
        return pltpu.make_async_remote_copy(
            src_ref=red.at[me],
            dst_ref=red.at[me],
            send_sem=rd_send,
            recv_sem=rd_recv,
            device_id=lon_peer(i),
            device_id_type=MESH,
        )

    def every(sem):
        return pltpu.make_async_copy(red.at[pl.ds(0, n - 1)], red.at[pl.ds(0, n - 1)], sem)

    peers_loop(n, lambda i: red_copy(i).start())

    @pl.when(jnp.logical_not(near))
    def _():
        rx_act(rx_near, "wait_recv")
        for slot in (0, 1, SLOT[-1]):
            take_r(slot)
        powers = []
        for v in range(2):
            l1 = lap(r_cols[v], range(-1, 3))[0]
            powers.append((r_cols[v], l1, lap(l1, OWN)[0]))
        keep_powers(powers)

    every(rd_recv).wait()
    terms = [red[i] for i in range(n)]
    while len(terms) > 1:
        terms = [
            terms[i] + terms[i + 1] if i + 1 < len(terms) else terms[i]
            for i in range(0, len(terms), 2)
        ]
    every_row = jnp.broadcast_to(terms[0], TILE)
    for q in range(-(-len(names) // 8)):
        picked = jnp.where(place == q, every_row, 0.0)
        flat[q] = jnp.broadcast_to(jnp.sum(picked, axis=1, keepdims=True), TILE)
    total = {
        name: jnp.broadcast_to(flat[q // 8, q % 8 : q % 8 + 1], TILE)
        for q, name in enumerate(names)
    }

    coefs = []
    for v in range(2):
        m0 = total["m", v, 0, 0]
        m = [m0] + [total["m", v, 0, k] for k in range(1, 6)]
        first_moment = m[1]
        centre = zero
        for i in range(1, len(CENTRES)):
            limit = 0.5 * (CENTRES[i] + CENTRES[i - 1]) * span
            above = first_moment > limit * m0
            centre = jnp.where(above, CENTRES[i] * span, centre)
            m = [m0] + [jnp.where(above, total["m", v, i, k], m[k]) for k in range(1, 6)]
        unit = 1.0 + centre
        a = [unit * m[k] + m[k + 1] for k in range(4)] + [m[4] + m[5]]
        ratio = m[1] / m0
        step0 = m0 / a[0]
        rr1 = step0 * step0 * (m[2] - ratio * m[1])
        beta0 = rr1 / m0
        along = step0 * ratio + beta0
        p1ap1 = along * along * a[0] - 2.0 * along * step0 * a[1] + step0 * step0 * a[2]
        step1 = rr1 / p1ap1
        x0 = step0 * ratio - step1 * along * unit
        x1 = step1 * step0 * unit - (step0 + step1 * along)
        x2 = step1 * step0

        def form(y0, y1, y2, f):
            return (
                y0 * (y0 * f[0] + 2.0 * (y1 * f[1] + y2 * f[2]))
                + y1 * (y1 * f[2] + 2.0 * (y2 * f[3]))
                + y2 * (y2 * f[4])
            )

        rr2 = form(x0, x1, x2, m)
        beta1 = rr2 / rr1
        y0, y1, y2 = x0 + beta1 * along, x1 - beta1 * step0, x2
        step2 = rr2 / form(y0, y1, y2, a)
        e0 = step0 + step1 * along + step2 * y0
        e1 = step2 * y1 - step1 * step0
        e2 = step2 * y2
        coefs.append((e0 - centre * (e1 - centre * e2), e1 - 2.0 * centre * e2, e2))
        for c in OWN:
            w = coefs[v]
            s = pw[v, 0, c] * w[0] + (pw[v, 1, c] * w[1] + pw[v, 2, c] * w[2])
            sout[v, col(c), :] = height[v][c] + s

    def plain(v, k):
        return total["m", v, 0, k]

    gram = []
    for v in range(2):
        w = coefs[v]
        s = total["hh", v] + 2.0 * sum(w[j] * total["h", v, v, j] for j in range(3))
        for i in range(3):
            for j in range(3):
                s = s + w[i] * w[j] * plain(v, i + j)
        gram.append(total["gram", 2 * v] + s)
    mix = total["gram", 1] + total["hh", 2]
    for j in range(3):
        mix = mix + (coefs[1][j] * total["h", 0, 1, j] + coefs[0][j] * total["h", 1, 0, j])
    for i in range(3):
        for j in range(3):
            mix = mix + coefs[0][i] * coefs[1][j] * total["c", i + j]
    cells = float((levels + 1) * 2 * 8 * 128 * n)
    gram_one, gram_two, gram_mix = gram[0] / cells, gram[1] / cells, mix / cells
    scale_one = jnp.sqrt(gram_one + EPSILON)
    cross = gram_mix / scale_one
    rest = gram_two - 2.0 * cross * cross + cross * cross * gram_one / (gram_one + EPSILON)
    scale_two = jnp.sqrt(jnp.maximum(rest, 0.0) + EPSILON)
    gout[0] = 1.0 / scale_one
    gout[1] = cross
    gout[2] = 1.0 / scale_two
    gout[3] = jnp.where(lane == 0, scale_one, jnp.where(lane == 1, cross, scale_two))


    pltpu.make_async_copy(s_t, s_t, t_send).wait()
    pltpu.make_async_copy(s_b, s_b, b_send).wait()
    for which in range(3 if share else 2):
        z_copy(which).wait_send()
    st_act(st_near + st_far, "wait_send")
    rx_act(rx_near + rx_far, "wait_send")

    @pl.when(to_near)
    def _():
        rx_act(rx_second, "wait_send")

    every(rd_send).wait()


def scale_kernel(trc, surf, tail, out_h, sout_h, gout_h, out, sout, gvec, sem):
    levels = trc.shape[1]
    count = chunk_count(levels)
    size = levels // count
    one, cross, two = tail[0], tail[1], tail[2]
    gvec[...] = tail[3, 0, :3]
    grow = pltpu.make_async_copy(gvec, gout_h, sem.at[2])
    grow.start()

    def store(g):
        ks = pl.ds(g * size, size)
        return pltpu.make_async_copy(out.at[:, ks], out_h.at[:, ks], sem.at[0])

    @pl.loop(0, count)
    def _(g):
        def step(i, carry):
            k = g * size + i
            for h in range(2):
                rows = pl.ds(8 * h, 8)
                unit = trc[0, k, rows, :] * one
                out[0, k, rows, :] = unit
                out[1, k, rows, :] = (trc[1, k, rows, :] - cross * unit) * two
            return carry

        lax.fori_loop(0, size, step, 0, unroll=min(UNROLL, size))
        store(g).start()

    for h in range(2):
        rows = pl.ds(8 * h, 8)
        unit = surf[0, rows, :] * one
        sout[0, rows, :] = unit
        sout[1, rows, :] = (surf[1, rows, :] - cross * unit) * two
    last = pltpu.make_async_copy(sout, sout_h, sem.at[1])
    last.start()
    pltpu.make_async_copy(out, out_h, sem.at[0]).wait()
    last.wait()
    grow.wait()


def packed(x):
    lead, (cols, rows) = x.shape[:-2], x.shape[-2:]
    x = x.reshape(lead + (cols, rows // 128, 128))
    x = jnp.swapaxes(x, -3, -2)
    return x.reshape(lead + (cols * (rows // 128), 128))


def unpacked(x, cols):
    lead, (rows, lanes) = x.shape[:-2], x.shape[-2:]
    x = x.reshape(lead + (rows // cols, cols, lanes))
    x = jnp.swapaxes(x, -3, -2)
    return x.reshape(lead + (cols, rows // cols * lanes))


def on_device(n, groups, tracer_pert, surface_pert, zonal_flow, merid_flow, bottom_level):
    vectors, levels, columns, rows = tracer_pert.shape
    count = chunk_count(levels)
    share = shares_zonal(groups, levels)
    f32 = jnp.float32
    vmem = pl.BlockSpec(memory_space=pltpu.VMEM)
    hbm = pl.BlockSpec(memory_space=pltpu.HBM)
    dma = pltpu.SemaphoreType.DMA
    zonal_sems = 3 if share else 2
    tracer, surface, tail = pl.pallas_call(
        functools.partial(kernel, n, share),
        out_shape=(
            jax.ShapeDtypeStruct((vectors, levels, 16, 128), f32),
            jax.ShapeDtypeStruct((vectors, 16, 128), f32),
            jax.ShapeDtypeStruct((4, 8, 128), f32),
        ),
        in_specs=[hbm] * 5,
        out_specs=(vmem,) * 3,
        scratch_shapes=[
            pltpu.VMEM((vectors, levels, 16, 128), f32),
            pltpu.VMEM((vectors, 16, 128), f32),
            pltpu.VMEM((levels, 16, 128), f32),
            pltpu.VMEM((levels, 16, 128), f32),
            pltpu.VMEM((16, 128), jnp.int32),
            pltpu.VMEM((2, levels, 2, 8, 128), f32),
            pltpu.VMEM((2, levels, 2, 8, 128), f32),
            pltpu.VMEM((2, levels, 8, 128), f32),
            pltpu.VMEM((2, levels, 8, 128), f32),
            pltpu.VMEM((2, levels, 2, 8, 128), f32),
            pltpu.VMEM((2, levels, 2, 8, 128), f32),
            pltpu.VMEM((levels, 10, 8, 128), f32),
            pltpu.VMEM((len(SLOT), 6, 8, 128), f32),
            pltpu.VMEM((len(SLOT), 4, 8, 128), f32),
            pltpu.VMEM((n, 1, 128), f32),
            pltpu.VMEM((16, 8, 128), f32),
            pltpu.VMEM((len(MOMENTS), 8, 128), f32),
            pltpu.VMEM((2, 3, 2, 8, 128), f32),
            dma((5 + count,)),
            dma(()),
            dma((2, count)),
            dma((zonal_sems,)),
            dma((zonal_sems,)),
            dma(()),
            dma((2, count)),
            dma((len(SLOT),)),
            dma((len(SLOT),)),
            dma((len(SLOT),)),
            dma((len(SLOT),)),
            dma(()),
            dma(()),
            pltpu.SemaphoreType.REGULAR((max(1, len(spread_rounds(n))),)),
        ],
        compiler_params=pltpu.CompilerParams(
            collective_id=0, has_side_effects=True, vmem_limit_bytes=40 * 1024 * 1024
        ),
    )(
        *(
            pltpu.with_memory_space_constraint(packed(x), pltpu.HBM)
            for x in (tracer_pert, surface_pert, zonal_flow, merid_flow, bottom_level)
        )
    )
    tracer, surface, growth = pl.pallas_call(
        scale_kernel,
        out_shape=(
            jax.ShapeDtypeStruct((vectors, levels, 16, 128), f32),
            jax.ShapeDtypeStruct((vectors, 16, 128), f32),
            jax.ShapeDtypeStruct((3,), f32),
        ),
        in_specs=[vmem] * 3,
        out_specs=(hbm,) * 3,
        scratch_shapes=[
            pltpu.VMEM((vectors, levels, 16, 128), f32),
            pltpu.VMEM((vectors, 16, 128), f32),
            pltpu.VMEM((3,), f32),
            dma((3,)),
        ],
        compiler_params=pltpu.CompilerParams(vmem_limit_bytes=16 * 1024 * 1024),
    )(tracer, surface, tail)
    return unpacked(tracer, columns), unpacked(surface, columns), growth


def solution(mesh):
    placed = (
        P("grp", None, "lon", None),
        P("grp", "lon", None),
        P(None, "lon", None),
        P(None, "lon", None),
        P("lon", None),
    )
    return jax.shard_map(
        functools.partial(on_device, mesh.shape["lon"], mesh.shape["grp"]),
        mesh=mesh,
        in_specs=placed,
        out_specs=(P("grp", None, "lon", None), P("grp", "lon", None), P("grp")),
        check_vma=False,
    )
```

```python
import functools

import jax
import jax.numpy as jnp
from jax import lax
from jax.experimental import pallas as pl
from jax.experimental.pallas import tpu as pltpu
from jax.sharding import PartitionSpec as P

DIFFUSIVITY = 0.5
TIME_STEP = 0.2
SURFACE_COUPLING = 0.5
STERIC_GAIN = 2.0
EPSILON = 1e-06
MESH = pl.DeviceIdType.MESH
CHUNKS = 5
UNROLL = 10
NEAR = (1, -1)
CENTRES = (0.0, 0.04, 0.16, 0.64)
FAR = 4
SLOT = {0: 0, **{s: s for s in range(1, FAR + 3)}, -1: FAR + 3}
OWN = (0, 1)
MOMENTS = (
    [("m", v, i, k) for v in range(2) for i in range(len(CENTRES)) for k in range(1 if i else 0, 6)]
    + [("h", v, w, j) for v in range(2) for w in range(2) for j in range(3)]
    + [("c", k) for k in range(5)]
)
TILE = (8, 128)


def chunk_count(levels):
    return max(c for c in range(1, CHUNKS + 1) if levels % c == 0)


def spread_rounds(n):
    reach, rounds = 1, []
    while 2 * reach < n:
        rounds.append(reach)
        reach *= 2
    return rounds


def shares_zonal(groups, levels):
    return groups == 2 and levels % 2 == 0


def peers_loop(n, body):
    if n <= 16:
        for i in range(1, n):
            body(i)
    else:

        def step(i, carry):
            body(i)
            return carry

        lax.fori_loop(1, n, step, 0)


def kernel(
    n, share, trc_h, surf_h, zon_h, mer_h, bot_h, out, sout, gout,
    trc, surf, zon, mer, bot, s_t, r_t, s_z, r_z, s_b, r_b, coef, st, rx, red, flat, mo, pw,
    in_sem, t_send, t_recv, z_send, z_recv, b_send, b_recv,
    st_send, st_recv, rx_send, rx_recv, rd_send, rd_recv, met,
):
    me = lax.axis_index("lon")
    grp = lax.axis_index("grp")
    levels = zon.shape[0]
    count = chunk_count(levels)
    size = levels // count
    side_dev = (lax.rem(me + n - 1, n), lax.rem(me + 1, n))
    outer = lax.rem(me, 2)
    inner = 1 - outer
    lane = lax.broadcasted_iota(jnp.int32, TILE, 1)
    row = lax.broadcasted_iota(jnp.int32, TILE, 0)
    last_lane, first_lane = lane == 127, lane == 0

    def north(x):
        rolled = pltpu.roll(x, 127, 1)
        return jnp.where(last_lane, pltpu.roll(rolled, 7, 0), rolled)

    def south(x):
        rolled = pltpu.roll(x, 1, 1)
        return jnp.where(first_lane, pltpu.roll(rolled, 1, 0), rolled)

    def col(c):
        return pl.ds(c, 8, stride=2)

    def lon_peer(s):
        return {"lon": lax.rem(me + s + n, n)}

    barrier = pltpu.get_barrier_semaphore()
    for s in NEAR:
        pl.semaphore_signal(barrier, inc=1, device_id=lon_peer(s), device_id_type=MESH)
    if share:
        pl.semaphore_signal(barrier, inc=1, device_id={"grp": 1 - grp}, device_id_type=MESH)

    half = levels // 2
    mine = pl.ds(grp * half if share else 0, half)
    theirs = pl.ds((1 - grp) * half, half) if share else pl.ds(half, levels - half)

    def chunk(g):
        return pl.ds(g * size, size)

    def in_chunk(g, body, carry):
        return lax.fori_loop(
            0, size, lambda i, state: body(g * size + i, state), carry, unroll=min(UNROLL, size)
        )

    def load(g):
        return pltpu.make_async_copy(trc_h.at[:, chunk(g)], trc.at[:, chunk(g)], in_sem.at[5 + g])

    load_zon = [
        pltpu.make_async_copy(zon_h.at[ks], zon.at[ks], in_sem.at[i])
        for i, ks in enumerate((mine, theirs))
    ]
    load_bot = pltpu.make_async_copy(bot_h, bot, in_sem.at[2])
    load_surf = pltpu.make_async_copy(surf_h, surf, in_sem.at[3])
    load_mer = pltpu.make_async_copy(mer_h, mer, in_sem.at[4])
    load_zon[0].start()
    load_bot.start()
    load_surf.start()
    load(0).start()
    load_zon[1].start()
    for g in range(1, count):
        load(g).start()
    load_mer.start()
    def gather_chunk(g):
        load(g).wait()

        def step(k, carry):
            for c in range(2):
                s_t[c, k, 0] = trc[0, k, col(c), :]
                s_t[c, k, 1] = trc[1, k, col(c), :]
            return carry

        in_chunk(g, step, 0)

    def side_copy(src, dst, send, recv, g, side):
        return pltpu.make_async_remote_copy(
            src_ref=src.at[side, chunk(g)],
            dst_ref=dst.at[1 - side, chunk(g)],
            send_sem=send,
            recv_sem=recv.at[1 - side, g],
            device_id={"lon": side_dev[side]},
            device_id_type=MESH,
        )

    def t_copy(g, side):
        return side_copy(s_t, r_t, t_send, t_recv, g, side)

    def b_copy(g, side):
        return side_copy(s_b, r_b, b_send, b_recv, g, side)

    def gather_zonal(i):
        load_zon[i].wait()
        ks = (mine, theirs)[i]

        def step(k, carry):
            for c in range(2):
                s_z[c, ks.start + k] = zon[ks.start + k, col(c), :]
            return carry

        lax.fori_loop(0, ks.size, step, 0, unroll=5)

    def z_copy(which):
        if not share:
            return pltpu.make_async_remote_copy(
                src_ref=s_z.at[which],
                dst_ref=r_z.at[1 - which],
                send_sem=z_send.at[which],
                recv_sem=z_recv.at[which],
                device_id={"lon": side_dev[which]},
                device_id_type=MESH,
            )
        src, dst, dev = (
            (s_z.at[outer, mine], r_z.at[1 - outer, mine], lon_peer(2 * outer - 1)),
            (s_z.at[inner], r_z.at[1 - inner], lon_peer(2 * inner - 1)),
            (r_z.at[outer, mine], r_z.at[outer, mine], {"grp": 1 - grp}),
        )[which]
        return pltpu.make_async_remote_copy(
            src_ref=src,
            dst_ref=dst,
            send_sem=z_send.at[which],
            recv_sem=z_recv.at[which],
            device_id=dev,
            device_id_type=MESH,
        )

    def send_chunk(g):
        for side in range(2):
            t_copy(g, side).start()

    def shift_copy(buf, send, recv, s, part):
        return pltpu.make_async_remote_copy(
            src_ref=buf.at[0, part],
            dst_ref=buf.at[SLOT[s], part],
            send_sem=send.at[s % 4 if s < 3 else 0],
            recv_sem=recv.at[SLOT[s] - 1],
            device_id=lon_peer(s),
            device_id_type=MESH,
        )

    def shift_copies(buf, send, recv, cases, act):
        for s, usual, closing in cases:
            closes = me == (0 if act == "wait_recv" else n - s)
            if usual == closing:
                getattr(shift_copy(buf, send, recv, s, usual), act)()
                continue
            if usual is not None:

                @pl.when(jnp.logical_not(closes))
                def _():
                    getattr(shift_copy(buf, send, recv, s, usual), act)()

            @pl.when(closes)
            def _():
                getattr(shift_copy(buf, send, recv, s, closing), act)()

    every_tile = pl.ds(0, 6)
    st_near = ((1, pl.ds(0, 4), every_tile), (-1, pl.ds(2, 4), pl.ds(2, 4)))
    st_far = (
        (2, pl.ds(3, 1), every_tile),
        *((s, None, every_tile) for s in range(3, FAR + 1)),
        (FAR + 1, None, pl.ds(2, 2)),
        (FAR + 2, None, pl.ds(3, 1)),
    )
    rx_near = ((1, pl.ds(0, 4), pl.ds(0, 4)), (-1, pl.ds(0, 4), pl.ds(0, 4)))
    rx_second = ((2, pl.ds(2, 2), pl.ds(0, 4)),)
    rx_far = (
        *((s, None, pl.ds(0, 4)) for s in range(3, FAR + 2)),
        (FAR + 2, None, pl.ds(2, 2)),
    )

    def st_act(cases, act):
        shift_copies(st, st_send, st_recv, cases, act)

    def rx_act(cases, act):
        shift_copies(rx, rx_send, rx_recv, cases, act)

    near = me < n - FAR
    to_near = lax.rem(me + 2, n) < n - FAR

    gather_zonal(0)
    pl.semaphore_wait(barrier, len(NEAR) + (1 if share else 0))
    if share:
        z_copy(0).start()
    load_bot.wait()
    load_surf.wait()
    for c in range(2):
        d = bot[col(c), :].astype(jnp.float32)
        st[0, 2 + c] = d
        for v in range(2):
            st[0, (4, 0)[c] + v] = jnp.where(d > 0, surf[v, col(c), :], 0.0)
    st_act(st_near, "start")
    gather_chunk(0)
    send_chunk(0)
    gather_zonal(1)
    for which in range(1 if share else 0, 2):
        z_copy(which).start()
    rounds = spread_rounds(n)

    def spread(i):
        if i < len(rounds):
            for s in (rounds[i], -rounds[i]):
                pl.semaphore_signal(
                    met.at[i], inc=1, device_id=lon_peer(s), device_id_type=MESH
                )

    def spread_wait(i):
        if i < len(rounds):
            pl.semaphore_wait(met.at[i], 2)

    spread(0)

    @pl.loop(1, count)
    def _(g):
        gather_chunk(g)
        send_chunk(g)


    spread_wait(0)
    spread(1)
    st_act(st_near, "wait_recv")

    depths = {-2: st[1, 2], -1: st[1, 3], 0: st[0, 2], 1: st[0, 3]}
    depths.update({2: st[SLOT[-1], 2], 3: st[SLOT[-1], 3]})

    def y_face(i):
        wall = jnp.logical_and(last_lane, row == 7)
        return jnp.where(wall, 0.0, jnp.minimum(depths[i], north(depths[i])))

    def x_face(i):
        return jnp.minimum(depths[i], depths[i + 1])

    for which in range(2):
        z_copy(which).wait_recv()
    if share:
        z_copy(2).start()
        z_copy(2).wait_recv()
    quarter = TIME_STEP * 0.25
    diff = TIME_STEP * DIFFUSIVITY
    faces_x = [x_face(f - 1) for f in range(3)]
    faces_y = [y_face(c) for c in range(2)]
    own_depth = [depths[c] for c in range(2)]

    load_mer.wait()

    def first_chunk(g):
        for side in range(2):
            t_copy(g, side).wait_recv()

        def first(k, carry):
            kf = k.astype(jnp.float32)
            z = (r_z[0, k], s_z[0, k], s_z[1, k], r_z[1, k])
            cx = []
            for f in range(3):
                open_f = kf < faces_x[f]
                u = quarter * (z[f] + z[f + 1])
                cx.append((jnp.where(open_f, u + diff, 0.0), jnp.where(open_f, u - diff, 0.0)))
            cy = []
            for c in range(2):
                open_f = kf < faces_y[c]
                m = mer[k, col(c), :]
                u = quarter * (m + north(m))
                cy.append((jnp.where(open_f, u + diff, 0.0), jnp.where(open_f, u - diff, 0.0)))
            for q, (lo, hi) in enumerate(cx + cy):
                coef[k, 2 * q] = lo
                coef[k, 2 * q + 1] = hi
            wet = [kf < own_depth[c] for c in range(2)]
            for v in range(2):
                t = (
                    r_t[0, k, v],
                    jnp.where(wet[0], s_t[0, k, v], 0.0),
                    jnp.where(wet[1], s_t[1, k, v], 0.0),
                    r_t[1, k, v],
                )
                fx = [cx[f][0] * t[f] + cx[f][1] * t[f + 1] for f in range(3)]
                for c in range(2):
                    fy = cy[c][0] * t[c + 1] + cy[c][1] * north(t[c + 1])
                    s_b[c, k, v] = t[c + 1] - ((fx[c + 1] - fx[c]) + (fy - south(fy)))
            return carry

        in_chunk(g, first, 0)
        for side in range(2):
            b_copy(g, side).start()

    pl.loop(0, count - count // 3)(first_chunk)
    spread_wait(1)
    spread(2)
    pl.loop(count - count // 3, count)(first_chunk)
    for i in range(2, len(rounds)):
        spread_wait(i)
        spread(i + 1)
    st_act(st_far, "start")

    face_x = {i: SURFACE_COUPLING * x_face(i) for i in range(-2, 3)}
    face_y = {i: SURFACE_COUPLING * y_face(i) for i in range(-2, 3)}
    face_s = {i: south(face_y[i]) for i in face_y}
    shared_faces = list(face_x)

    def lap(s, cols):
        gx = {i: face_x[i] * (s[i + 1] - s[i]) for i in range(cols[0] - 1, cols[-1] + 1)}
        res, rise = {}, {}
        for i in cols:
            rise[i] = north(s[i]) - s[i]
            fall = s[i] - south(s[i])
            res[i] = (gx[i - 1] - gx[i]) + (face_s[i] * fall - face_y[i] * rise[i])
        return res, rise

    height = [
        {-1: st[1, v], 0: st[0, 4 + v], 1: st[0, v], 2: st[SLOT[-1], 4 + v]}
        for v in range(2)
    ]
    lap_h = [lap(height[v], OWN)[0] for v in range(2)]

    zero = jnp.zeros(TILE, jnp.float32)

    def second_chunk(g, totals):
        for side in range(2):
            b_copy(g, side).wait_recv()

        def second(k, carry):
            sums, grams = list(carry[:4]), list(carry[4:])
            cx = [(coef[k, 2 * f], coef[k, 2 * f + 1]) for f in range(3)]
            cy = [(coef[k, 6 + 2 * c], coef[k, 7 + 2 * c]) for c in range(2)]
            new = []
            for v in range(2):
                t = (r_b[0, k, v], s_b[0, k, v], s_b[1, k, v], r_b[1, k, v])
                fx = [cx[f][0] * t[f] + cx[f][1] * t[f + 1] for f in range(3)]
                for c in range(2):
                    fy = cy[c][0] * t[c + 1] + cy[c][1] * north(t[c + 1])
                    val = t[c + 1] - ((fx[c + 1] - fx[c]) + (fy - south(fy)))
                    out[v, k, col(c), :] = val
                    sums[2 * v + c] = sums[2 * v + c] + val
                    new.append(val)
            grams[0] = grams[0] + (new[0] * new[0] + new[1] * new[1])
            grams[1] = grams[1] + (new[0] * new[2] + new[1] * new[3])
            grams[2] = grams[2] + (new[2] * new[2] + new[3] * new[3])
            return tuple(sums + grams)

        return in_chunk(g, second, totals)

    totals = lax.fori_loop(0, count, second_chunk, (zero,) * 7)

    gain = STERIC_GAIN / levels
    for v in range(2):
        for c in range(2):
            rx[0, 2 * c + v] = gain * totals[2 * v + c] - lap_h[v][c]
    rx_act(rx_far, "start")

    @pl.when(to_near)
    def _():
        rx_act(rx_second, "start")

    rx_act(rx_near, "start")
    st_act(st_far, "wait_recv")

    def add_faces(first, last):
        for i in range(first, last):
            face_x.setdefault(i, SURFACE_COUPLING * x_face(i))
        for i in range(first + 1, last):
            if i not in face_y:
                face_y[i] = SURFACE_COUPLING * y_face(i)
                face_s[i] = south(face_y[i])

    span = 4.0 * levels

    def operator_powers(v, cols):
        l1, rise0 = lap(r_cols[v], range(cols[0] - 2, cols[-1] + 2))
        l2, rise1 = lap(l1, range(cols[0] - 1, cols[-1] + 1))
        return r_cols[v], l1, l2, rise0, rise1

    def moments(cols, tall):
        def gathered(term):
            return functools.reduce(lambda a, b: a + b, [term(c) for c in cols])

        def dot(a, b):
            return gathered(lambda i: a[i] * b[i])

        parts, powers = {}, []
        for v in range(2):
            r, l1, l2, rise0, rise1 = operator_powers(v, cols)
            powers.append((r, l1, l2))
            rise2 = {i: north(l2[i]) - l2[i] for i in cols}
            for i, centre in enumerate(CENTRES):
                shift = centre * span
                if i:
                    b1 = {c: l1[c] - shift * r[c] for c in cols}
                    b2 = {
                        c: (l2[c] - 2.0 * shift * l1[c]) + shift * shift * r[c]
                        for c in range(cols[0] - 1, cols[-1] + 1)
                    }
                    up = {
                        c: (rise2[c] - 2.0 * shift * rise1[c]) + shift * shift * rise0[c]
                        for c in cols
                    }
                else:
                    b1, b2, up = l1, l2, rise2
                    parts["m", v, i, 0] = dot(r, r)
                parts["m", v, i, 1] = dot(r, b1)
                parts["m", v, i, 2] = dot(b1, b1)
                parts["m", v, i, 3] = dot(b1, b2)
                parts["m", v, i, 4] = dot(b2, b2)

                def energy(c):
                    across = b2[c] - b2[c - 1]
                    return face_x[c - 1] * across * across + face_y[c] * up[c] * up[c]

                parts["m", v, i, 5] = gathered(energy)
        for v in range(2):
            for w in range(2):
                for j in range(3):
                    parts["h", v, w, j] = dot(tall[v], powers[w][j])
        for k in range(5):
            parts["c", k] = dot(powers[0][k // 2], powers[1][(k + 1) // 2])
        return parts, powers

    def keep_powers(powers):
        for v in range(2):
            for j in range(3):
                for c in OWN:
                    pw[v, j, c] = powers[v][j][c]

    def take_r(slot):
        for v in range(2):
            for c in range(2):
                r_cols[v][(2 if slot == SLOT[-1] else -2 * slot) + c] = rx[slot, 2 * c + v]

    r_cols = [{}, {}]

    def forget():
        for known in (face_x, face_y, face_s):
            for i in [i for i in known if i not in shared_faces]:
                del known[i]

    def closing_moments():
        tall = [{}, {}]
        for slot in range(FAR + 3):
            take_r(slot)
            for c in range(2):
                depths[c - 2 * slot] = st[slot, 2 + c]
        take_r(SLOT[-1])
        for slot in range(FAR + 1):
            for v in range(2):
                tall[v].update({-2 * slot: st[slot, 4 + v], 1 - 2 * slot: st[slot, v]})
        cols = range(-2 * FAR, 2)
        add_faces(cols[0] - 3, cols[-1] + 2)
        return moments(cols, tall)

    forget()

    @pl.when(jnp.logical_and(near, me != 0))
    def _():
        rx_act(rx_near + rx_second, "wait_recv")
        depths[-3] = st[2, 3]
        add_faces(-3, 3)
        for slot in (0, 1, SLOT[-1]):
            take_r(slot)
        for v in range(2):
            r_cols[v][-3] = rx[2, 2 + v]
        parts, powers = moments(OWN, height)
        for q, name in enumerate(MOMENTS):
            mo[q] = parts[name]
        keep_powers(powers)

    @pl.when(jnp.logical_not(near))
    def _():
        for q in range(len(MOMENTS)):
            mo[q] = zero

    forget()

    @pl.when(me == 0)
    def _():
        rx_act(rx_near + rx_second + rx_far, "wait_recv")
        parts, powers = closing_moments()
        for q, name in enumerate(MOMENTS):
            mo[q] = parts[name]
        keep_powers(powers)

    forget()

    def dot(a, b):
        return a[0] * b[0] + a[1] * b[1]

    parts = {}
    for q in range(3):
        parts["gram", q] = totals[4 + q]
    parts["hh", 0] = dot(height[0], height[0])
    parts["hh", 1] = dot(height[1], height[1])
    parts["hh", 2] = dot(height[0], height[1])
    for q, name in enumerate(MOMENTS):
        parts[name] = mo[q]

    names = list(parts)
    place = lane - 16 * row
    local = zero
    for q in range(0, len(names), 8):
        level = [parts[name] for name in names[q : q + 8]]
        for shift in (1, 2, 4):
            even = jnp.bitwise_and(row, shift) == 0
            merged = []
            for i in range(0, len(level), 2):
                a, b = level[i], level[min(i + 1, len(level) - 1)]
                merged.append(jnp.where(even, a, b) + pltpu.roll(jnp.where(even, b, a), shift, 0))
            level = merged
        local = jnp.where(place == q // 8, jnp.sum(level[0], axis=1, keepdims=True), local)
    for shift in (4, 2, 1):
        local = local + pltpu.roll(local, shift, 0)
    red[me] = local[0:1]

    def red_copy(i):
        return pltpu.make_async_remote_copy(
            src_ref=red.at[me],
            dst_ref=red.at[me],
            send_sem=rd_send,
            recv_sem=rd_recv,
            device_id=lon_peer(i),
            device_id_type=MESH,
        )

    def every(sem):
        return pltpu.make_async_copy(red.at[pl.ds(0, n - 1)], red.at[pl.ds(0, n - 1)], sem)

    peers_loop(n, lambda i: red_copy(i).start())

    @pl.when(jnp.logical_not(near))
    def _():
        rx_act(rx_near, "wait_recv")
        for slot in (0, 1, SLOT[-1]):
            take_r(slot)
        powers = []
        for v in range(2):
            l1 = lap(r_cols[v], range(-1, 3))[0]
            powers.append((r_cols[v], l1, lap(l1, OWN)[0]))
        keep_powers(powers)

    every(rd_recv).wait()
    terms = [red[i] for i in range(n)]
    while len(terms) > 1:
        terms = [
            terms[i] + terms[i + 1] if i + 1 < len(terms) else terms[i]
            for i in range(0, len(terms), 2)
        ]
    every_row = jnp.broadcast_to(terms[0], TILE)
    for q in range(-(-len(names) // 8)):
        picked = jnp.where(place == q, every_row, 0.0)
        flat[q] = jnp.broadcast_to(jnp.sum(picked, axis=1, keepdims=True), TILE)
    total = {
        name: jnp.broadcast_to(flat[q // 8, q % 8 : q % 8 + 1], TILE)
        for q, name in enumerate(names)
    }

    coefs = []
    for v in range(2):
        m0 = total["m", v, 0, 0]
        m = [m0] + [total["m", v, 0, k] for k in range(1, 6)]
        first_moment = m[1]
        centre = zero
        for i in range(1, len(CENTRES)):
            limit = 0.5 * (CENTRES[i] + CENTRES[i - 1]) * span
            above = first_moment > limit * m0
            centre = jnp.where(above, CENTRES[i] * span, centre)
            m = [m0] + [jnp.where(above, total["m", v, i, k], m[k]) for k in range(1, 6)]
        unit = 1.0 + centre
        a = [unit * m[k] + m[k + 1] for k in range(4)] + [m[4] + m[5]]
        ratio = m[1] / m0
        step0 = m0 / a[0]
        rr1 = step0 * step0 * (m[2] - ratio * m[1])
        beta0 = rr1 / m0
        along = step0 * ratio + beta0
        p1ap1 = along * along * a[0] - 2.0 * along * step0 * a[1] + step0 * step0 * a[2]
        step1 = rr1 / p1ap1
        x0 = step0 * ratio - step1 * along * unit
        x1 = step1 * step0 * unit - (step0 + step1 * along)
        x2 = step1 * step0

        def form(y0, y1, y2, f):
            return (
                y0 * (y0 * f[0] + 2.0 * (y1 * f[1] + y2 * f[2]))
                + y1 * (y1 * f[2] + 2.0 * (y2 * f[3]))
                + y2 * (y2 * f[4])
            )

        rr2 = form(x0, x1, x2, m)
        beta1 = rr2 / rr1
        y0, y1, y2 = x0 + beta1 * along, x1 - beta1 * step0, x2
        step2 = rr2 / form(y0, y1, y2, a)
        e0 = step0 + step1 * along + step2 * y0
        e1 = step2 * y1 - step1 * step0
        e2 = step2 * y2
        coefs.append((e0 - centre * (e1 - centre * e2), e1 - 2.0 * centre * e2, e2))
        for c in OWN:
            w = coefs[v]
            s = pw[v, 0, c] * w[0] + (pw[v, 1, c] * w[1] + pw[v, 2, c] * w[2])
            sout[v, col(c), :] = height[v][c] + s

    def plain(v, k):
        return total["m", v, 0, k]

    gram = []
    for v in range(2):
        w = coefs[v]
        s = total["hh", v] + 2.0 * sum(w[j] * total["h", v, v, j] for j in range(3))
        for i in range(3):
            for j in range(3):
                s = s + w[i] * w[j] * plain(v, i + j)
        gram.append(total["gram", 2 * v] + s)
    mix = total["gram", 1] + total["hh", 2]
    for j in range(3):
        mix = mix + (coefs[1][j] * total["h", 0, 1, j] + coefs[0][j] * total["h", 1, 0, j])
    for i in range(3):
        for j in range(3):
            mix = mix + coefs[0][i] * coefs[1][j] * total["c", i + j]
    cells = float((levels + 1) * 2 * 8 * 128 * n)
    gram_one, gram_two, gram_mix = gram[0] / cells, gram[1] / cells, mix / cells
    scale_one = jnp.sqrt(gram_one + EPSILON)
    cross = gram_mix / scale_one
    rest = gram_two - 2.0 * cross * cross + cross * cross * gram_one / (gram_one + EPSILON)
    scale_two = jnp.sqrt(jnp.maximum(rest, 0.0) + EPSILON)
    gout[0] = 1.0 / scale_one
    gout[1] = cross
    gout[2] = 1.0 / scale_two
    gout[3] = jnp.where(lane == 0, scale_one, jnp.where(lane == 1, cross, scale_two))


    pltpu.make_async_copy(s_t, s_t, t_send).wait()
    pltpu.make_async_copy(s_b, s_b, b_send).wait()
    for which in range(3 if share else 2):
        z_copy(which).wait_send()
    st_act(st_near + st_far, "wait_send")
    rx_act(rx_near + rx_far, "wait_send")

    @pl.when(to_near)
    def _():
        rx_act(rx_second, "wait_send")

    every(rd_send).wait()


def scale_kernel(trc, surf, tail, out_h, sout_h, gout_h, out, sout, gvec, sem):
    levels = trc.shape[1]
    count = chunk_count(levels)
    size = levels // count
    one, cross, two = tail[0], tail[1], tail[2]
    gvec[...] = tail[3, 0, :3]
    grow = pltpu.make_async_copy(gvec, gout_h, sem.at[2])
    grow.start()

    def store(g):
        ks = pl.ds(g * size, size)
        return pltpu.make_async_copy(out.at[:, ks], out_h.at[:, ks], sem.at[0])

    @pl.loop(0, count)
    def _(g):
        def step(i, carry):
            k = g * size + i
            for h in range(2):
                rows = pl.ds(8 * h, 8)
                unit = trc[0, k, rows, :] * one
                out[0, k, rows, :] = unit
                out[1, k, rows, :] = (trc[1, k, rows, :] - cross * unit) * two
            return carry

        lax.fori_loop(0, size, step, 0, unroll=min(UNROLL, size))
        store(g).start()

    for h in range(2):
        rows = pl.ds(8 * h, 8)
        unit = surf[0, rows, :] * one
        sout[0, rows, :] = unit
        sout[1, rows, :] = (surf[1, rows, :] - cross * unit) * two
    last = pltpu.make_async_copy(sout, sout_h, sem.at[1])
    last.start()
    pltpu.make_async_copy(out, out_h, sem.at[0]).wait()
    last.wait()
    grow.wait()


def packed(x):
    lead, (cols, rows) = x.shape[:-2], x.shape[-2:]
    x = x.reshape(lead + (cols, rows // 128, 128))
    x = jnp.swapaxes(x, -3, -2)
    return x.reshape(lead + (cols * (rows // 128), 128))


def unpacked(x, cols):
    lead, (rows, lanes) = x.shape[:-2], x.shape[-2:]
    x = x.reshape(lead + (rows // cols, cols, lanes))
    x = jnp.swapaxes(x, -3, -2)
    return x.reshape(lead + (cols, rows // cols * lanes))


def on_device(n, groups, tracer_pert, surface_pert, zonal_flow, merid_flow, bottom_level):
    vectors, levels, columns, rows = tracer_pert.shape
    count = chunk_count(levels)
    share = shares_zonal(groups, levels)
    f32 = jnp.float32
    vmem = pl.BlockSpec(memory_space=pltpu.VMEM)
    hbm = pl.BlockSpec(memory_space=pltpu.HBM)
    dma = pltpu.SemaphoreType.DMA
    zonal_sems = 3 if share else 2
    tracer, surface, tail = pl.pallas_call(
        functools.partial(kernel, n, share),
        out_shape=(
            jax.ShapeDtypeStruct((vectors, levels, 16, 128), f32),
            jax.ShapeDtypeStruct((vectors, 16, 128), f32),
            jax.ShapeDtypeStruct((4, 8, 128), f32),
        ),
        in_specs=[hbm] * 5,
        out_specs=(vmem,) * 3,
        scratch_shapes=[
            pltpu.VMEM((vectors, levels, 16, 128), f32),
            pltpu.VMEM((vectors, 16, 128), f32),
            pltpu.VMEM((levels, 16, 128), f32),
            pltpu.VMEM((levels, 16, 128), f32),
            pltpu.VMEM((16, 128), jnp.int32),
            pltpu.VMEM((2, levels, 2, 8, 128), f32),
            pltpu.VMEM((2, levels, 2, 8, 128), f32),
            pltpu.VMEM((2, levels, 8, 128), f32),
            pltpu.VMEM((2, levels, 8, 128), f32),
            pltpu.VMEM((2, levels, 2, 8, 128), f32),
            pltpu.VMEM((2, levels, 2, 8, 128), f32),
            pltpu.VMEM((levels, 10, 8, 128), f32),
            pltpu.VMEM((len(SLOT), 6, 8, 128), f32),
            pltpu.VMEM((len(SLOT), 4, 8, 128), f32),
            pltpu.VMEM((n, 1, 128), f32),
            pltpu.VMEM((16, 8, 128), f32),
            pltpu.VMEM((len(MOMENTS), 8, 128), f32),
            pltpu.VMEM((2, 3, 2, 8, 128), f32),
            dma((5 + count,)),
            dma(()),
            dma((2, count)),
            dma((zonal_sems,)),
            dma((zonal_sems,)),
            dma(()),
            dma((2, count)),
            dma((4,)),
            dma((len(SLOT) - 1,)),
            dma((4,)),
            dma((len(SLOT) - 1,)),
            dma(()),
            dma(()),
            pltpu.SemaphoreType.REGULAR((max(1, len(spread_rounds(n))),)),
        ],
        compiler_params=pltpu.CompilerParams(
            collective_id=0, has_side_effects=True, vmem_limit_bytes=40 * 1024 * 1024
        ),
    )(
        *(
            pltpu.with_memory_space_constraint(packed(x), pltpu.HBM)
            for x in (tracer_pert, surface_pert, zonal_flow, merid_flow, bottom_level)
        )
    )
    tracer, surface, growth = pl.pallas_call(
        scale_kernel,
        out_shape=(
            jax.ShapeDtypeStruct((vectors, levels, 16, 128), f32),
            jax.ShapeDtypeStruct((vectors, 16, 128), f32),
            jax.ShapeDtypeStruct((3,), f32),
        ),
        in_specs=[vmem] * 3,
        out_specs=(hbm,) * 3,
        scratch_shapes=[
            pltpu.VMEM((vectors, levels, 16, 128), f32),
            pltpu.VMEM((vectors, 16, 128), f32),
            pltpu.VMEM((3,), f32),
            dma((3,)),
        ],
        compiler_params=pltpu.CompilerParams(vmem_limit_bytes=16 * 1024 * 1024),
    )(tracer, surface, tail)
    return unpacked(tracer, columns), unpacked(surface, columns), growth


def solution(mesh):
    placed = (
        P("grp", None, "lon", None),
        P("grp", "lon", None),
        P(None, "lon", None),
        P(None, "lon", None),
        P("lon", None),
    )
    return jax.shard_map(
        functools.partial(on_device, mesh.shape["lon"], mesh.shape["grp"]),
        mesh=mesh,
        in_specs=placed,
        out_specs=(P("grp", None, "lon", None), P("grp", "lon", None), P("grp")),
        check_vma=False,
    )
```
